32 devices in a mesh: ctx: 16 (over z, x, core), tp: 2 (over y).
Axes of the slice: x: 2, y: 2, z: 4, core: 2. Of those that a mesh axis runs over, the one named last changes fastest.
Arguments:
- doc_lengths: int32 [32], replicated, may hold values from 1 to 512, 2048 in all
- ssm_x: bfloat16 [2048, 8192], P('ctx', 'tp'), may hold values from -6 to 6
- ssm_gate: bfloat16 [2048, 8192], P('ctx', 'tp'), may hold values from -6 to 6
- ssm_b: bfloat16 [2048, 2048], P('ctx', 'tp'), may hold values from -6 to 6
- ssm_c: bfloat16 [2048, 2048], P('ctx', 'tp'), may hold values from -0.375 to 0.375
- step_size: float32 [2048, 128], P('ctx', 'tp'), as said below
- decay_rate: float32 [128], P('tp'), as said below
- norm_weight: float32 [8192], P('tp'), may hold values from 0.1 to 1.9
- queries: bfloat16 [2048, 8192], P('ctx', 'tp'), may hold values from -96 to 96
- keys: bfloat16 [2048, 1024], P('ctx', 'tp'), may hold values from -4 to 4
- values: bfloat16 [2048, 1024], P('ctx', 'tp'), may hold values from -6 to 6
Outputs:
- mixed: bfloat16 [2048, 8192], P(('ctx', 'tp'))
- attended: bfloat16 [2048, 8192], P(('ctx', 'tp'))
The draws below stay inside these ranges and needn't reach their ends.
Inputs may be any that keep to these rules, and one draw needn't show every extreme that they name: `doc_lengths`: every document has at least one token; the longest has exactly 512. `step_size`: Positive. `decay_rate`: Positive, at most 0.04.
All inputs are finite; a program needn't handle non-finite values.
Results may differ from the reference program's by a relative error of at most 0.0049.
Values may be sent and summed in bfloat16 or wider, within the bound.
A program may use at most 192 MiB of HBM per device.

```python
import math
import jax
import jax.numpy as jnp
import numpy as np
from jax import lax

HEADS = 128
HEAD_DIM = 64
STATE = 256
GROUPS = 8
QHEADS = 64
KVHEADS = 8
ATT_DIM = 128
TOK_DEV = 128
NDOC = 32
SEQ = 2048
MAXDOC = 512


def log_uniform(key, out_shape, low_end, high_end):
    unit_draw = jax.random.uniform(key, out_shape, jnp.float32)
    return jnp.exp(math.log(low_end) + unit_draw * math.log(high_end / low_end))


def draw_decay_rate(key, part):
    head_order = jax.random.permutation(jax.random.fold_in(key, 11), HEADS)
    slow_rate = log_uniform(jax.random.fold_in(key, 12), (HEADS,), 0.3, 1.0) / MAXDOC
    fast_rate = log_uniform(jax.random.fold_in(key, 13), (HEADS,), 0.02, 0.04)
    fast_count = HEADS // 2
    return jnp.where(head_order < fast_count, fast_rate, slow_rate).astype(jnp.float32)


def draw_step_size(key, part):
    block_count = SEQ // TOK_DEV
    coarse = log_uniform(jax.random.fold_in(key, 21), (block_count, HEADS), 0.5, 2.0)
    fine_part = log_uniform(jax.random.fold_in(key, 22), (SEQ, HEADS), 0.5, 2.0)
    return (jnp.repeat(coarse, TOK_DEV, axis=0) * fine_part).astype(jnp.float32)


def attention_pair(key):
    base_key = jax.random.fold_in(key, 31)
    q_groups = QHEADS // KVHEADS
    keys_f = jnp.clip(jax.random.normal(jax.random.fold_in(base_key, 1), (SEQ, KVHEADS, ATT_DIM), jnp.float32), -4.0, 4.0)
    queries_f = jnp.clip(jax.random.normal(jax.random.fold_in(base_key, 2), (SEQ, KVHEADS, q_groups, ATT_DIM), jnp.float32), -4.0, 4.0)
    return (queries_f.reshape(SEQ, QHEADS * ATT_DIM), keys_f.reshape(SEQ, KVHEADS * ATT_DIM))


def draw_queries(key, part):
    return attention_pair(key)[0].astype(jnp.bfloat16)


def draw_keys(key, part):
    return attention_pair(key)[1].astype(jnp.bfloat16)


def shard_levels(own_key, extent, cuts, smallest, largest):
    def one(position, blocks):
        steps = jax.random.uniform(jax.random.fold_in(jax.random.fold_in(own_key, 6), position), (blocks,), jnp.float32, smallest / len(cuts), largest / len(cuts))
        return jnp.repeat(jnp.exp(steps), extent[position] // blocks).reshape((-1,) + (1,) * (len(extent) - position - 1))

    factor_of = one(*cuts[0])
    for cut in cuts[1:]:
        factor_of = factor_of * one(*cut)
    return factor_of


def profile(number_of, total, reach, lean):
    loads = [(1 << 20) // math.isqrt(rank ** lean) + 1 for rank in range(2, number_of + 1)]
    spare, holding = total - reach - (number_of - 1), [1] * (number_of - 1)
    while spare > 0:
        candidates = [i for i in range(number_of - 1) if holding[i] < reach]
        whole, remaining = sum([loads[i] for i in candidates]), spare
        for i in candidates:
            addition = min(reach - holding[i], max(1, remaining * loads[i] // whole), spare)
            holding[i] = holding[i] + addition
            spare = spare - addition
    return np.array([reach] + holding)


def ragged(stream_key, count, total, bound, lean):
    if count == 2:
        one = jax.random.randint(stream_key, (), max(1, total - bound), min(bound, total - 1) + 1)
        return jnp.stack([one, total - one])
    sizes = jnp.asarray(profile(count, total, bound, lean), jnp.int32)
    pairs = (count - 1) // 2
    donor, taker = sizes[1:1 + 2 * pairs:2], sizes[2:2 + 2 * pairs:2]
    slack = jnp.minimum(donor - 1, bound - taker)
    passed = jax.random.randint(jax.random.fold_in(stream_key, 1), (pairs,), 0, 1 << 20) % (slack + 1)
    sizes = sizes.at[1:1 + 2 * pairs:2].set(donor - passed).at[2:2 + 2 * pairs:2].set(taker + passed)
    return sizes[jax.random.permutation(jax.random.fold_in(stream_key, 2), count)]


def normal_values(stream_key, extent, scale, most, pieces=(), held_as=jnp.bfloat16):
    drawn = scale * jax.random.normal(stream_key, extent, jnp.float32)
    if pieces:
        drawn = drawn * shard_levels(stream_key, extent, pieces, -0.22, 0.18)
    return jnp.clip(drawn, -most, most).astype(held_as)


def setup_inputs(seed: int = 0) -> dict:
    streams_of = jax.random.split(jax.random.key(seed), 12)
    return {
        "doc_lengths": ragged(streams_of[0], NDOC, SEQ, MAXDOC, 2).astype(jnp.int32),
        "ssm_x": normal_values(streams_of[1], (SEQ, HEADS * HEAD_DIM), 1.0, 6.0, ((0, 16), (1, 2))),
        "ssm_gate": normal_values(streams_of[2], (SEQ, HEADS * HEAD_DIM), 1.0, 6.0, ((0, 16), (1, 2))),
        "ssm_b": normal_values(streams_of[3], (SEQ, GROUPS * STATE), 1.0, 6.0, ((0, 16), (1, 2))),
        "ssm_c": normal_values(streams_of[4], (SEQ, GROUPS * STATE), STATE ** -0.5, 0.375, ((0, 16), (1, 2))),
        "step_size": draw_step_size(jax.random.fold_in(streams_of[11], 71), 0),
        "decay_rate": draw_decay_rate(jax.random.fold_in(streams_of[11], 71), 0),
        "norm_weight": jnp.clip(1.0 + 0.18 * jax.random.normal(streams_of[7], (HEADS * HEAD_DIM,), jnp.float32), 0.1, 1.9),
        "queries": draw_queries(jax.random.fold_in(streams_of[11], 71), 0),
        "keys": draw_keys(jax.random.fold_in(streams_of[11], 71), 0),
        "values": normal_values(streams_of[10], (SEQ, KVHEADS * ATT_DIM), 1.0, 6.0, ((0, 16), (1, 2))),
    }


def doc_starts(doc_lengths):
    return (jnp.cumsum(doc_lengths) - doc_lengths).astype(jnp.int32)

def doc_index(positions, starts):
    return (lax.optimization_barrier(jnp.sum((starts[None, :] <= positions[:, None]).astype(jnp.int32), axis=1)) - 1).astype(jnp.int32)

def block_terms(ssm_x, ssm_b, ssm_c, step_size, decay_rate, doc_ids, prev_id, group_heads):
    tok_rows = ssm_x.shape[0]
    head_count = step_size.shape[1]
    group_count = head_count // group_heads
    head_size = ssm_x.shape[1] // head_count
    state_size = ssm_b.shape[1] // group_count
    inputs = ssm_x.reshape(tok_rows, group_count, group_heads, head_size)
    in_proj = ssm_b.reshape(tok_rows, group_count, state_size)
    out_proj = ssm_c.reshape(tok_rows, group_count, state_size)
    log_decay = -(step_size * decay_rate[None, :])
    cumulative = jnp.cumsum(log_decay, axis=0)
    same_doc = doc_ids[:, None] == doc_ids[None, :]
    causal = jnp.arange(tok_rows)[:, None] >= jnp.arange(tok_rows)[None, :]
    allowed = (same_doc & causal)[None]
    spread = cumulative.T[:, :, None] - cumulative.T[:, None, :]
    weights = jnp.where(allowed, jnp.exp(jnp.where(allowed, spread, 0.0)), 0.0) * step_size.T[:, None, :]
    intersection = jnp.einsum('tgn,sgn->gts', out_proj.astype(jnp.float32), in_proj.astype(jnp.float32))
    mixing = (weights.reshape(group_count, group_heads, tok_rows, tok_rows) * intersection[:, None]).astype(jnp.bfloat16)
    y_intra = jnp.einsum('ghts,sghp->tghp', mixing.astype(jnp.float32), inputs.astype(jnp.float32))
    final_sum = cumulative[-1]
    tail = jnp.exp(final_sum[None, :] - cumulative) * step_size * (doc_ids == doc_ids[-1]).astype(jnp.float32)[:, None]
    scaled = (inputs.astype(jnp.float32) * tail.reshape(tok_rows, group_count, group_heads)[..., None]).astype(jnp.bfloat16)
    state_local = jnp.einsum('sghp,sgn->ghpn', scaled.astype(jnp.float32), in_proj.astype(jnp.float32))
    entry = jnp.exp(cumulative) * (doc_ids == prev_id).astype(jnp.float32)[:, None]
    transmit = jnp.exp(final_sum) * (doc_ids[-1] == prev_id).astype(jnp.float32)
    return (y_intra, state_local, entry, transmit.reshape(group_count, group_heads))

def finish_rows(y_intra, entry, carried, ssm_c, ssm_gate, norm_weight):
    tok_rows, group_count, group_heads, head_size = y_intra.shape
    out_proj = ssm_c.reshape(tok_rows, group_count, -1).astype(jnp.float32)
    incoming = jnp.einsum('tgn,ghpn->tghp', out_proj, carried, precision=lax.Precision.HIGHEST)
    mixer_out = y_intra + incoming * entry.reshape(tok_rows, group_count, group_heads)[..., None]
    gate_vals = ssm_gate.reshape(tok_rows, group_count, group_heads, head_size).astype(jnp.float32)
    gated = (mixer_out * jax.nn.silu(gate_vals)).reshape(tok_rows, group_count, group_heads * head_size)
    factor = lax.rsqrt(lax.optimization_barrier(jnp.mean(gated * gated, axis=2, keepdims=True)) + 1e-05)
    return ((gated * factor).reshape(tok_rows, -1) * norm_weight[None, :]).astype(jnp.bfloat16)

def take_rows(array, begin, count):
    return lax.dynamic_slice_in_dim(array, begin, count, 0)

def reference(doc_lengths, ssm_x, ssm_gate, ssm_b, ssm_c, step_size, decay_rate, norm_weight, queries, keys, values):
    starts = doc_starts(doc_lengths)
    block_count = SEQ // TOK_DEV
    group_heads = HEADS // GROUPS

    def mixer_block(carried, block_index):
        begin = (block_index * TOK_DEV).astype(jnp.int32)
        positions = begin + jnp.arange(TOK_DEV, dtype=jnp.int32)
        doc_ids = doc_index(positions, starts)
        prev_id = doc_index(jnp.reshape(begin - 1, (1,)).astype(jnp.int32), starts)[0]
        y_intra, state_local, entry, transmit = block_terms(take_rows(ssm_x, begin, TOK_DEV), take_rows(ssm_b, begin, TOK_DEV), take_rows(ssm_c, begin, TOK_DEV), take_rows(step_size, begin, TOK_DEV), decay_rate, doc_ids, prev_id, group_heads)
        rows_out = finish_rows(y_intra, entry, carried, take_rows(ssm_c, begin, TOK_DEV), take_rows(ssm_gate, begin, TOK_DEV), norm_weight)
        return (transmit[:, :, None, None] * carried + state_local, rows_out)
    start_state = jnp.zeros((GROUPS, group_heads, HEAD_DIM, STATE), jnp.float32)
    unused_state, mixed_blocks = lax.scan(mixer_block, start_state, jnp.arange(block_count, dtype=jnp.int32))
    mixed = mixed_blocks.reshape(SEQ, HEADS * HEAD_DIM)
    q_groups = QHEADS // KVHEADS
    window = MAXDOC + TOK_DEV
    scale = ATT_DIM ** (-0.5)

    def attention_block(block_index):
        begin = (block_index * TOK_DEV).astype(jnp.int32)
        window_begin = jnp.maximum(begin - MAXDOC, 0).astype(jnp.int32)
        query_rows = take_rows(queries, begin, TOK_DEV).reshape(TOK_DEV, KVHEADS, q_groups, ATT_DIM).astype(jnp.float32)
        key_rows = take_rows(keys, window_begin, window).reshape(window, KVHEADS, ATT_DIM).astype(jnp.float32)
        value_rows = take_rows(values, window_begin, window).reshape(window, KVHEADS, ATT_DIM).astype(jnp.float32)
        query_pos = begin + jnp.arange(TOK_DEV, dtype=jnp.int32)
        key_pos = window_begin + jnp.arange(window, dtype=jnp.int32)
        allowed = (doc_index(query_pos, starts)[:, None] == doc_index(key_pos, starts)[None, :]) & (key_pos[None, :] <= query_pos[:, None])
        scores = jnp.einsum('tngd,knd->ngtk', query_rows, key_rows) * scale
        scores = jnp.where(allowed[None, None], scores, -jnp.inf)
        top_score = lax.optimization_barrier(jnp.max(scores, axis=3, keepdims=True))
        probs = jnp.exp(scores - top_score)
        total = lax.optimization_barrier(jnp.sum(probs, axis=3))
        rounded = lax.optimization_barrier(probs.astype(jnp.bfloat16))
        summed = jnp.einsum('ngtk,knd->ngtd', rounded.astype(jnp.float32), value_rows)
        result = summed / total[..., None]
        return jnp.transpose(result, (2, 0, 1, 3)).reshape(TOK_DEV, -1).astype(jnp.bfloat16)
    attended = lax.map(attention_block, jnp.arange(block_count, dtype=jnp.int32)).reshape(SEQ, QHEADS * ATT_DIM)
    return (mixed, attended)
```

```python
import functools

import jax
import jax.numpy as jnp
from jax import lax
from jax.experimental import pallas as pl
from jax.experimental.pallas import tpu as pltpu
from jax.sharding import PartitionSpec as P

HEADS = 128
GROUPS = 8
ATT_DIM = 128
DOC_DEVS = 4


NEG_LARGE = -1e30


def for_sending(x):
    return jax.tree.map(lambda a: a.astype(jnp.bfloat16) if a.dtype == jnp.float32 else a, x)


def passed_along(block, axis, distance):
    devices = range(lax.axis_size(axis))
    route = [(i - distance, i) for i in devices if i - distance in devices]
    return lax.ppermute(block, axis, route)


def doc_starts(doc_lengths):
    return jnp.cumsum(doc_lengths) - doc_lengths


def doc_index(positions, starts):
    return jnp.sum((starts[None, :] <= positions[:, None]).astype(jnp.int32), axis=1) - 1


def block_terms(ssm_x, ssm_b, ssm_c, step_size, decay_rate, doc_ids, prev_id, group_heads):
    tok_rows = ssm_x.shape[0]
    head_count = step_size.shape[1]
    group_count = head_count // group_heads
    head_size = ssm_x.shape[1] // head_count
    state_size = ssm_b.shape[1] // group_count
    inputs = ssm_x.reshape(tok_rows, group_count, group_heads, head_size)
    in_proj = ssm_b.reshape(tok_rows, group_count, state_size)
    out_proj = ssm_c.reshape(tok_rows, group_count, state_size)
    log_decay = -(step_size * decay_rate[None, :])
    cumulative = jnp.cumsum(log_decay, axis=0)
    same_doc = doc_ids[:, None] == doc_ids[None, :]
    causal = jnp.arange(tok_rows)[:, None] >= jnp.arange(tok_rows)[None, :]
    allowed = (same_doc & causal)[None]
    spread = cumulative.T[:, :, None] - cumulative.T[:, None, :]
    weights = (
        jnp.where(allowed, jnp.exp(jnp.where(allowed, spread, 0.0)), 0.0) * step_size.T[:, None, :]
    )
    intersection = jnp.einsum("tgn,sgn->gts", out_proj, in_proj, preferred_element_type=jnp.float32)
    mixing = (
        weights.reshape(group_count, group_heads, tok_rows, tok_rows) * intersection[:, None]
    ).astype(jnp.bfloat16)
    y_intra = jnp.einsum("ghts,sghp->tghp", mixing, inputs, preferred_element_type=jnp.float32)
    final_sum = cumulative[-1]
    tail = (
        jnp.exp(final_sum[None, :] - cumulative)
        * step_size
        * (doc_ids == doc_ids[-1]).astype(jnp.float32)[:, None]
    )
    scaled = (
        inputs.astype(jnp.float32) * tail.reshape(tok_rows, group_count, group_heads)[..., None]
    ).astype(jnp.bfloat16)
    state_local = jnp.einsum("sghp,sgn->ghpn", scaled, in_proj, preferred_element_type=jnp.float32)
    entry = jnp.exp(cumulative) * (doc_ids == prev_id).astype(jnp.float32)[:, None]
    transmit = jnp.exp(final_sum) * (doc_ids[-1] == prev_id).astype(jnp.float32)
    return (y_intra, state_local, entry, transmit.reshape(group_count, group_heads))


def finish_rows(y_intra, entry, carried, ssm_c, ssm_gate, norm_weight):
    tok_rows, group_count, group_heads, head_size = y_intra.shape
    out_proj = ssm_c.reshape(tok_rows, group_count, -1).astype(jnp.float32)
    incoming = jnp.einsum("tgn,ghpn->tghp", out_proj, carried, precision=lax.Precision.HIGHEST)
    mixer_out = y_intra + incoming * entry.reshape(tok_rows, group_count, group_heads)[..., None]
    gate_vals = ssm_gate.reshape(tok_rows, group_count, group_heads, head_size).astype(jnp.float32)
    gated = (mixer_out * jax.nn.silu(gate_vals)).reshape(
        tok_rows, group_count, group_heads * head_size
    )
    factor = lax.rsqrt(jnp.mean(gated * gated, axis=2, keepdims=True) + 1e-05)
    return ((gated * factor).reshape(tok_rows, -1) * norm_weight[None, :]).astype(jnp.bfloat16)


def chain_states(earlier, later):
    return (earlier[0] * later[0], later[0][:, :, None, None] * earlier[1] + later[1])


def attention_update(
    carry, query_rows, key_block, value_block, key_pos, query_pos, query_doc, starts
):
    running_max, running_sum, running_acc = carry
    block_rows = key_block.shape[0]
    kv_local = key_block.shape[1] // ATT_DIM
    key_heads = key_block.reshape(block_rows, kv_local, ATT_DIM)
    value_heads = value_block.reshape(block_rows, kv_local, ATT_DIM)
    key_doc = doc_index(key_pos, starts)
    allowed = (query_doc[:, None] == key_doc[None, :]) & (key_pos[None, :] <= query_pos[:, None])
    scores = jnp.einsum(
        "tngd,knd->ngtk", query_rows, key_heads, preferred_element_type=jnp.float32
    ) * ATT_DIM ** (-0.5)
    scores = jnp.where(allowed[None, None], scores, -jnp.inf)
    new_max = jnp.maximum(running_max, jnp.max(scores, axis=3))
    probs = jnp.exp(scores - new_max[..., None])
    factor = jnp.exp(running_max - new_max)
    new_sum = running_sum * factor + jnp.sum(probs, axis=3)
    weighted = jnp.einsum(
        "ngtk,knd->ngtd",
        probs.astype(jnp.bfloat16),
        value_heads,
        preferred_element_type=jnp.float32,
    )
    return (new_max, new_sum, running_acc * factor[..., None] + weighted)


def local_any(
    doc_lengths,
    ssm_x,
    ssm_gate,
    ssm_b,
    ssm_c,
    step_size,
    decay_rate,
    norm_weight,
    queries,
    keys,
    values,
):
    tok_rows = ssm_x.shape[0]
    ctx_index = lax.axis_index("ctx")
    begin = ctx_index * tok_rows
    positions = begin + jnp.arange(tok_rows, dtype=jnp.int32)
    starts = doc_starts(doc_lengths)
    doc_ids = doc_index(positions, starts)
    prev_id = doc_index(jnp.reshape(begin - 1, (1,)), starts)[0]
    group_heads = HEADS // GROUPS
    y_intra, state_local, entry, transmit = block_terms(
        ssm_x, ssm_b, ssm_c, step_size, decay_rate, doc_ids, prev_id, group_heads
    )
    merged = (transmit, state_local)
    for level_bit in range(DOC_DEVS.bit_length() - 1):
        earlier = passed_along(
            (for_sending(merged[0]), for_sending(merged[1])), "ctx", 1 << level_bit
        )
        merged = chain_states(earlier, merged)
    carried = passed_along(merged[1], "ctx", 1)
    mixed_rows = finish_rows(y_intra, entry, carried, ssm_c, ssm_gate, norm_weight)
    kv_local = keys.shape[1] // ATT_DIM
    q_groups = queries.shape[1] // (kv_local * ATT_DIM)
    query_rows = queries.reshape(tok_rows, kv_local, q_groups, ATT_DIM)
    floor_start = jnp.max(jnp.where(starts <= begin, starts, 0))
    query_last = begin + tok_rows - 1
    carry_shape = (kv_local, q_groups, tok_rows)
    initial = (
        jnp.full(carry_shape, NEG_LARGE, jnp.float32),
        jnp.zeros(carry_shape, jnp.float32),
        jnp.zeros(carry_shape + (ATT_DIM,), jnp.float32),
    )

    def visit(carry, key_block, value_block, key_begin):
        block_rows = key_block.shape[0]
        needed = (key_begin <= query_last) & (key_begin + block_rows - 1 >= floor_start)

        def update(inner):
            key_pos = key_begin + jnp.arange(block_rows, dtype=jnp.int32)
            return attention_update(
                inner, query_rows, key_block, value_block, key_pos, positions, doc_ids, starts
            )

        def unchanged(inner):
            return inner

        return lax.cond(needed, update, unchanged, carry)

    totals = visit(initial, keys, values, begin)
    for hop_count in range(1, DOC_DEVS + 1):
        near_keys, near_values = passed_along((keys, values), "ctx", hop_count)
        totals = visit(totals, near_keys, near_values, begin - hop_count * tok_rows)
    final_out = totals[2] / totals[1][..., None]
    attended_rows = (
        jnp.transpose(final_out, (2, 0, 1, 3)).reshape(tok_rows, -1).astype(jnp.bfloat16)
    )
    mixed_local, attended_local = (
        lax.all_to_all(mixed_rows, "tp", split_axis=0, concat_axis=1, tiled=True),
        lax.all_to_all(attended_rows, "tp", split_axis=0, concat_axis=1, tiled=True),
    )
    return (mixed_local, attended_local)


LOG2E = 1.4426950408889634
F32 = jnp.float32
BF16 = jnp.bfloat16
MESH_ID = pl.DeviceIdType.MESH
COLS_LAST = (((1,), (1,)), ((), ()))
ROWS_FIRST = (((0,), (0,)), ((), ()))
PIECE = 128
HEADS_AT_ONCE = 2
MERGE_AFTER = (0, 1, 3, 4, 6, 7)
PASS_AFTER = (5, 6, 7)


def dot(a, b, dims=(((1,), (0,)), ((), ())), precision=None):
    return lax.dot_general(a, b, dims, precision=precision, preferred_element_type=F32)


def spread_heads(columns, head, head_size):
    lane = lax.broadcasted_iota(jnp.int32, (columns.shape[0], 128), 1)
    wide = jnp.broadcast_to(columns[:, head : head + 1], lane.shape)
    for k in range(1, 128 // head_size):
        wide = jnp.where(lane >= k * head_size, columns[:, head + k : head + k + 1], wide)
    return wide


def pair_kernel(
    n,
    lengths,
    x_in,
    gate_in,
    b_in,
    c_in,
    step_in,
    q_in,
    k_in,
    v_in,
    rate_ref,
    weight_ref,
    raw_out,
    sums_out,
    attended_out,
    x_s,
    gate_s,
    b_s,
    c_s,
    step_s,
    q_s,
    kv_s,
    own_s,
    beside_s,
    merged_s,
    behind_s,
    passed_s,
    second_s,
    t_own,
    t_beside,
    coef_s,
    y_s,
    raw_s,
    sums_s,
    attended_s,
    bias_s,
    l_s,
    lt_s,
    dtt_s,
    tail_s,
    entry_s,
    send_sem,
    recv_sem,
    own_sem,
):
    index = lax.axis_index("ctx")
    tp = lax.axis_index("tp")
    parity, pair = lax.rem(index, 2), lax.div(index, 2)
    odd = lax.rem(pair, 2)
    base = index - parity
    other = 1 - parity
    tok = x_in.shape[0]
    rows = 2 * tok
    width = x_s.shape[1]
    group_heads = HEADS // GROUPS
    heads = step_in.shape[0] // 2
    groups = heads // group_heads
    group_width = width // groups
    state = b_s.shape[1] // groups
    head_size = width // heads
    kv_width = kv_s.shape[2]
    kv_heads = kv_width // ATT_DIM
    q_width = q_s.shape[1] // kv_heads
    pieces = group_width // PIECE
    group_of = (odd, 1 - odd)

    core_peer = (base + other, tp)
    tp_peer = (index, 1 - tp)
    cross_peer = (base + other, 1 - tp)
    beside = (index + 2 - 4 * odd, tp)
    barrier = pltpu.get_barrier_semaphore()
    greeted = jnp.int32(3)
    reach = {}
    for step in (2, 4, -2, -4):
        reach[step] = (base + step >= 0) & (base + step < n)
        greeted += 2 * reach[step].astype(jnp.int32)

        @pl.when(reach[step])
        def _():
            for core in range(2):
                peer = (base + step + core, tp)
                pl.semaphore_signal(barrier, inc=1, device_id=peer, device_id_type=MESH_ID)

    for peer in (core_peer, tp_peer, cross_peer):
        pl.semaphore_signal(barrier, inc=1, device_id=peer, device_id_type=MESH_ID)
    pl.semaphore_wait(barrier, greeted)
    ahead, behind = reach[4], reach[-4]

    used = [0, 0, 0]

    def slots(kind, count=1):
        used[kind] += count
        return used[kind] - count

    def remote(src, dst, peer, send, recv):
        return pltpu.make_async_remote_copy(
            src_ref=src,
            dst_ref=dst,
            send_sem=send_sem.at[send],
            recv_sem=recv_sem.at[recv],
            device_id=peer,
            device_id_type=MESH_ID,
        )

    at_mine = pl.multiple_of(parity * tok, tok)
    mine = pl.ds(at_mine, tok)
    closing = []

    def trade(moves, whole):
        send, recv, own = slots(0), slots(1), slots(2)
        for give, keep, place in moves:
            remote(give, place, core_peer, send, recv).start()
            pltpu.make_async_copy(keep, place, own_sem.at[own]).start()
        closing.append(remote(whole, whole, core_peer, send, recv).wait_send)

        def ready():
            pltpu.make_async_copy(whole, whole, own_sem.at[own]).wait()
            remote(whole, whole, core_peer, send, recv).wait_recv()

        return ready

    def by_group(src, dst, local_groups):
        size = dst.shape[1] // groups

        def part(core, local):
            at = core * groups * size + group_of[local] * size
            return src.at[:, pl.ds(pl.multiple_of(at, 128), size)]

        moves, first = [], local_groups[0]
        for local in local_groups:
            place = dst.at[mine, local * size : (local + 1) * size]
            moves.append((part(other, local), part(parity, local), place))
        return trade(moves, dst.at[:tok, first * size : (first + len(local_groups)) * size])

    def part_of(src, core, begin, size, total):
        return src.at[:, pl.ds(pl.multiple_of(core * total + begin, 128), size)]

    @pl.when(pair < 2)
    def _():
        kv_s[:, :rows, :] = jnp.zeros((2, rows, kv_width), BF16)

    @pl.when(pair < 1)
    def _():
        kv_s[:, rows : 2 * rows, :] = jnp.zeros((2, rows, kv_width), BF16)

    past_send = (slots(0), slots(0))
    past_recv = [(slots(1), slots(1)) for head in range(kv_heads)]

    def send_past(head):
        cols = slice(head * ATT_DIM, (head + 1) * ATT_DIM)
        for which, step, skip in ((0, 2, rows), (1, 4, 0)):

            @pl.when(reach[step])
            def _():
                for k, src in enumerate((k_in, v_in)):
                    for core in range(2):
                        remote(
                            part_of(src, core, cols.start, ATT_DIM, kv_width),
                            kv_s.at[k, pl.ds(at_mine + skip, tok), cols],
                            (base + step + core, tp),
                            past_send[which],
                            past_recv[head][which],
                        ).start()

    def wait_past(head):
        cols = slice(head * ATT_DIM, (head + 1) * ATT_DIM)
        for which, step, skip in ((0, -2, rows), (1, -4, 0)):

            @pl.when(reach[step])
            def _():
                place = kv_s.at[:, skip : skip + rows, cols]
                remote(place, place, core_peer, past_send[which], past_recv[head][which]).wait_recv()

    send_past(0)
    moves = []
    for local in range(groups):
        place = step_s.at[local * group_heads : (local + 1) * group_heads, mine]

        def step_part(core):
            at = (core * groups + group_of[local]) * group_heads
            return step_in.at[pl.ds(pl.multiple_of(at, 8), group_heads)]

        moves.append((step_part(other), step_part(parity), place))
    ready_step = trade(moves, step_s.at[:, :tok])
    ready_b = by_group(b_in, b_s, tuple(range(groups)))
    ready_x = {local: by_group(x_in, x_s, (local,)) for local in (1, 0)}
    for head in range(1, kv_heads):
        send_past(head)
    ready_c = by_group(c_in, c_s, tuple(range(groups)))
    moves = []
    for k, src in enumerate((k_in, v_in)):
        give = part_of(src, other, 0, kv_width, kv_width)
        keep = part_of(src, parity, 0, kv_width, kv_width)
        moves.append((give, keep, kv_s.at[k, pl.ds(at_mine + 2 * rows, tok), :]))
    ready_kv = trade(moves, kv_s.at[:, 2 * rows : 2 * rows + tok, :])
    q_all = q_s.shape[1]
    give, keep = part_of(q_in, other, 0, q_all, q_all), part_of(q_in, parity, 0, q_all, q_all)
    ready_q = trade([(give, keep, q_s.at[mine, :])], q_s.at[:tok, :])
    ready_gate = by_group(gate_in, gate_s, tuple(range(groups)))

    @pl.when(pair < 2)
    def _():
        behind_s[...] = jnp.zeros_like(behind_s)

    begin = pair * rows
    row_at = begin - 2 * rows + lax.broadcasted_iota(jnp.int32, (1, 3 * rows), 1)
    col_at = begin + lax.broadcasted_iota(jnp.int32, (rows, 1), 0)
    row_doc = jnp.zeros_like(row_at) - 1
    col_doc = jnp.zeros_like(col_at) - 1
    begun, prev_id, last_id = jnp.int32(0), jnp.int32(-1), jnp.int32(-1)
    for j in range(lengths.shape[0]):
        row_doc += (row_at >= begun).astype(jnp.int32)
        col_doc += (col_at >= begun).astype(jnp.int32)
        prev_id += (begin - 1 >= begun).astype(jnp.int32)
        last_id += (begin + rows - 1 >= begun).astype(jnp.int32)
        begun = begun + lengths[j]
    bias_s[...] = jnp.where((row_doc == col_doc) & (row_at <= col_at), 0.0, NEG_LARGE)

    ready_step()
    step_t = jnp.concatenate([step_s[...], jnp.zeros((128 - heads, rows), F32)], axis=0)
    step = step_t.T
    rates = []
    for local in range(groups):
        rate = jnp.zeros((1, group_heads), F32)
        for k in range(2 * groups):
            here = parity * groups + group_of[local] == k
            rate = jnp.where(here, rate_ref[:, k * group_heads : (k + 1) * group_heads], rate)
        rates.append(rate)
    rate = jnp.concatenate(rates + [jnp.zeros((1, 128 - heads), F32)], axis=1)
    at = lax.broadcasted_iota(jnp.int32, (rows, rows), 0)
    to = lax.broadcasted_iota(jnp.int32, (rows, rows), 1)
    lower = (to <= at).astype(F32)
    total_decay = dot(lower, -(step * rate), precision=lax.Precision.HIGHEST)
    final_sum = total_decay[rows - 1 :, :]
    l_s[...] = total_decay
    lt_s[...] = total_decay.T
    dtt_s[...] = step_t
    tail_s[...] = jnp.where(col_doc == last_id, jnp.exp(final_sum - total_decay) * step, 0.0)
    entry_s[...] = jnp.where(col_doc == prev_id, jnp.exp(total_decay), 0.0)
    passing = (last_id == prev_id).astype(F32)
    t_own[...] = jnp.broadcast_to(jnp.exp(final_sum) * passing, t_own.shape)
    t_trip = remote(t_own, t_beside, beside, slots(0), slots(1))
    t_trip.start()
    closing.append(t_trip.wait_send)

    first_send, first_recv = slots(0), slots(1, pieces)
    merge_send, merge_recv = slots(0), slots(1, pieces)
    pass_send, pass_recv = slots(0), slots(1, pieces)

    def first_trip(k):
        return remote(
            own_s.at[pieces + k], beside_s.at[k], beside, first_send, first_recv + k
        )

    def merge_trip(k):
        return remote(
            merged_s.at[k], behind_s.at[k], (index + 4, tp), merge_send, merge_recv + k
        )

    def pass_trip(k):
        return remote(passed_s.at[k], second_s.at[k], beside, pass_send, pass_recv + k)

    per = 128 // head_size
    ready_b()
    for local in (1, 0):
        ready_x[local]()
        b_t = b_s[:, local * state : (local + 1) * state].T
        for k in range(local * pieces, (local + 1) * pieces, 2):
            parts = []
            for tile in range(2):
                lead = (k + tile) * PIECE
                wide = spread_heads(tail_s[...], lead // head_size, head_size)
                parts.append((x_s[:, lead : lead + PIECE].astype(F32) * wide).astype(BF16))
            made = dot(b_t, jnp.concatenate(parts, axis=1)).astype(BF16)
            for tile in range(2):
                own_s[k + tile] = made[:, tile * PIECE : (tile + 1) * PIECE]
                if local == 1:
                    first_trip(k + tile - pieces).start()

    lane = lax.broadcasted_iota(jnp.int32, (rows, 128), 1)
    ready_c()
    for g in range(groups):
        proj = slice(g * state, (g + 1) * state)
        inter = dot(c_s[:, proj], b_s[:, proj], COLS_LAST)
        for tile in range(group_width // 128):
            lead = g * group_width + tile * 128
            halves = []
            for r in range(0, rows, tok):
                seen = slice(0, r + tok)
                bias = bias_s[r : r + tok, 2 * rows : 2 * rows + r + tok]
                mixing = []
                for h in range(lead // head_size, lead // head_size + per):
                    spread = l_s[r : r + tok, h : h + 1] - lt_s[h : h + 1, seen]
                    w = jnp.exp(spread + bias) * dtt_s[h : h + 1, seen] * inter[r : r + tok, seen]
                    mixing.append(w.astype(BF16))
                both = dot(jnp.concatenate(mixing, axis=0), x_s[seen, lead : lead + 128])
                whole = both[:tok]
                for k in range(1, per):
                    part = both[k * tok : (k + 1) * tok]
                    whole = jnp.where(lane[:tok] >= k * head_size, part, whole)
                y_s[r : r + tok, lead : lead + 128] = whole

    part_rows = rows // 4
    exits = ((tp_peer, 0, 1), (cross_peer, 1, 1), (core_peer, 1, 0))

    def exit_slots():
        return slots(0, 3), slots(1, 3), slots(2)

    def leave(sems, piece_for, home):
        send, recv, own = sems
        for k, (peer, far_core, far_tp) in enumerate(exits):
            src = piece_for(other if far_core else parity, 1 - tp if far_tp else tp)
            remote(src, home, peer, send + k, recv + k).start()
        pltpu.make_async_copy(piece_for(parity, tp), home, own_sem.at[own]).start()

    def settle(sems, whole):
        send, recv, own = sems
        for k, (peer, far_core, far_tp) in enumerate(exits):
            remote(whole, whole, peer, send + k, recv + k).wait()
        pltpu.make_async_copy(whole, whole, own_sem.at[own]).wait()

    def row_part(src, cols):
        def piece_for(core, side):
            at = (core * 2 + side) * part_rows
            return src.at[pl.ds(pl.multiple_of(at, part_rows), part_rows), cols]

        return piece_for

    raw_exit, attended_exit, sums_exit = exit_slots(), exit_slots(), exit_slots()

    def coefficients():
        t_trip.wait_recv()
        even = jnp.broadcast_to(odd == 0, (8, 128))
        row = lax.broadcasted_iota(jnp.int32, (8, 128), 0)
        for k in range(pieces):
            h = k * PIECE // head_size
            ours = spread_heads(t_own[...], h, head_size)
            theirs = spread_heads(t_beside[...], group_heads + h, head_size)
            values = (
                (1.0, ours),
                (theirs, 1.0),
                (1.0, 0.0),
                (ours, 1.0),
                (0.0, 1.0),
                (1.0, theirs),
            )
            table = jnp.zeros((8, 128), F32)
            for j, (if_even, if_odd) in enumerate(values):
                table = jnp.where(row == j, jnp.where(even, if_even, if_odd), table)
            coef_s[:, k * PIECE : (k + 1) * PIECE] = table

    def blend(left, right, k, row):
        cols = slice(k * PIECE, (k + 1) * PIECE)
        total = left[k].astype(F32) * coef_s[row : row + 1, cols]
        total += right[k].astype(F32) * coef_s[row + 1 : row + 2, cols]
        return total.astype(BF16)

    def merge(k):
        first_trip(k).wait_recv()
        merged_s[k] = blend(beside_s, own_s, k, 0)

        @pl.when(ahead)
        def _():
            merge_trip(k).start()

    def pass_on(k):
        @pl.when(behind)
        def _():
            merge_trip(k).wait_recv()

        passed_s[k] = blend(own_s, behind_s, k, 2)
        pass_trip(k).start()

    scale = LOG2E * ATT_DIM ** (-0.5)
    ready_kv()
    ready_q()
    coefficients()
    step_no = 0
    for kv_head in range(kv_heads):
        kv_cols = slice(kv_head * ATT_DIM, (kv_head + 1) * ATT_DIM)
        wait_past(kv_head)
        for lead in range(kv_head * q_width, (kv_head + 1) * q_width, HEADS_AT_ONCE * ATT_DIM):
            for r in range(0, rows, tok):
                seen = slice(r, r + 2 * rows + tok)
                asked = jnp.concatenate(
                    [
                        q_s[r : r + tok, lead + h * ATT_DIM : lead + (h + 1) * ATT_DIM]
                        for h in range(HEADS_AT_ONCE)
                    ],
                    axis=0,
                )
                scores = dot(asked, kv_s[0, seen, kv_cols], COLS_LAST)
                bias = bias_s[r : r + tok, seen]
                scores = scores + jnp.concatenate([bias] * HEADS_AT_ONCE, axis=0)
                top = jnp.max(scores, axis=1, keepdims=True)
                probs = jnp.exp2((scores - top) * scale)
                total = jnp.sum(probs, axis=1, keepdims=True)
                summed = dot(probs.astype(BF16), kv_s[1, seen, kv_cols]) / total
                for h in range(HEADS_AT_ONCE):
                    cols = slice(lead + h * ATT_DIM, lead + (h + 1) * ATT_DIM)
                    attended_s[r : r + tok, cols] = summed[h * tok : (h + 1) * tok].astype(BF16)
            size = HEADS_AT_ONCE * ATT_DIM
            at = pl.multiple_of((tp * 2 + parity) * q_all + lead, 128)
            home = attended_out.at[:, pl.ds(at, size)]
            leave(attended_exit, row_part(attended_s, slice(lead, lead + size)), home)
            for k in range(len(MERGE_AFTER)):
                if MERGE_AFTER[k] == step_no:
                    merge(k)
            for k in range(len(PASS_AFTER)):
                if PASS_AFTER[k] == step_no:
                    pass_on(k)
            step_no += 1

    ones = jnp.ones((8, 128), F32)
    squares = [jnp.zeros((rows, 128), F32)] * groups

    def finish(local, first):
        carried = []
        for k in range(first, first + 2):
            if local == 0:
                carried.append(blend(beside_s, behind_s, k, 4))
            else:
                pass_trip(k).wait_recv()
                carried.append(second_s[k])
        proj = slice(local * state, (local + 1) * state)
        incoming = dot(c_s[:, proj], jnp.concatenate(carried, axis=1))
        lead = local * group_width + first * PIECE
        square = squares[local]
        for tile in range(0, 2 * PIECE, 128):
            cols = slice(lead + tile, lead + tile + 128)
            wide = spread_heads(entry_s[...], cols.start // head_size, head_size)
            z = gate_s[:, cols].astype(F32)
            total = y_s[:, cols] + incoming[:, tile : tile + 128] * wide
            total = total * (z / (1.0 + jnp.exp(-z)))
            square += total * total
            at = parity * width + group_of[local] * group_width + first * PIECE + tile
            gain = weight_ref[:, pl.ds(pl.multiple_of(at, 128), 128)]
            raw_s[:, cols] = (total * gain).astype(BF16)
        squares[local] = square
        at = (tp * 2 + parity) * width + group_of[local] * group_width + first * PIECE
        home = raw_out.at[:, pl.ds(pl.multiple_of(at, 128), 2 * PIECE)]
        leave(raw_exit, row_part(raw_s, slice(lead, lead + 2 * PIECE)), home)
        if first + 2 == pieces:
            here = slice(local * 8, local * 8 + 8)
            sums_s[here, :] = dot(ones, square, COLS_LAST, lax.Precision.HIGHEST)
            at = ((tp * 2 + parity) * groups + group_of[local]) * 8
            home = sums_out.at[pl.ds(pl.multiple_of(at, 8), 8), :]

            def half(core, side):
                return sums_s.at[here, pl.ds(pl.multiple_of(core * tok, tok), tok)]

            leave(sums_exit, half, home)

    ready_gate()
    for k in range(len(MERGE_AFTER), pieces):
        merge(k)
    passed = len(PASS_AFTER)
    for k in range(0, pieces, 2):
        while passed < min(pieces, k + 4):
            pass_on(passed)
            passed += 1
        finish(0, k)
    for k in range(0, pieces, 2):
        finish(1, k)

    assert used == [send_sem.shape[0], recv_sem.shape[0], own_sem.shape[0]], used
    for close in closing:
        close()
    for which, step in ((0, 2), (1, 4)):

        @pl.when(reach[step])
        def _():
            place = kv_s.at[:, :rows, :]
            remote(place, place, core_peer, past_send[which], past_recv[0][which]).wait_send()

    half = own_s.at[:pieces]
    remote(half, half, beside, first_send, first_recv).wait_send()
    remote(half, half, beside, pass_send, pass_recv).wait_send()

    @pl.when(ahead)
    def _():
        remote(half, half, beside, merge_send, merge_recv).wait_send()

    settle(attended_exit, attended_s.at[:part_rows, :])
    settle(raw_exit, raw_s.at[:part_rows, :])
    settle(sums_exit, sums_s.at[:, :tok])


def scale_kernel(raw, sums, attended, mixed_out, attended_out, mixed_s, sem):
    tp = lax.axis_index("tp")
    rows, width = raw.shape
    group_width = width // GROUPS
    whole = pltpu.make_async_copy(attended, attended_out, sem.at[GROUPS])
    whole.start()
    squares = sums[...]
    squares = jnp.concatenate([squares, jnp.zeros((128 - squares.shape[0], 128), F32)], axis=0).T
    squares = jnp.where(tp == 0, squares[:rows], squares[rows:])
    factor = lax.rsqrt(squares * (1.0 / group_width) + 1e-05)
    copies = [whole]
    for g in range(GROUPS):
        cols = slice(g * group_width, (g + 1) * group_width)
        mixed_s[:, cols] = (raw[:, cols].astype(F32) * factor[:, 8 * g : 8 * g + 1]).astype(BF16)
        copy = pltpu.make_async_copy(mixed_s.at[:, cols], mixed_out.at[:, cols], sem.at[g])
        copy.start()
        copies.append(copy)
    for copy in copies:
        copy.wait()


def local_pair(
    doc_lengths,
    ssm_x,
    ssm_gate,
    ssm_b,
    ssm_c,
    step_size,
    decay_rate,
    norm_weight,
    queries,
    keys,
    values,
):
    tok, width = ssm_x.shape
    rows, half = 2 * tok, width // 2
    groups = step_size.shape[1] * GROUPS // HEADS // 2
    state = ssm_b.shape[1] // (2 * groups)
    kv_half = keys.shape[1] // 2
    q_half = queries.shape[1] // 2
    pieces = half // PIECE
    any_spec = pl.BlockSpec(memory_space=pl.ANY)
    vmem_spec = pl.BlockSpec(memory_space=pltpu.VMEM)
    part = rows // 4
    group_pieces = pieces // groups
    state_piece = pltpu.VMEM((group_pieces, state, PIECE), BF16)
    scratch = [
        pltpu.VMEM((rows, half), BF16),
        pltpu.VMEM((rows, half), BF16),
        pltpu.VMEM((rows, groups * state), BF16),
        pltpu.VMEM((rows, groups * state), BF16),
        pltpu.VMEM((step_size.shape[1] // 2, rows), F32),
        pltpu.VMEM((rows, q_half), BF16),
        pltpu.VMEM((2, 3 * rows, kv_half), BF16),
        pltpu.VMEM((pieces, state, PIECE), BF16),
        state_piece,
        state_piece,
        state_piece,
        state_piece,
        state_piece,
        pltpu.VMEM((8, 128), F32),
        pltpu.VMEM((8, 128), F32),
        pltpu.VMEM((8, half // groups), F32),
        pltpu.VMEM((rows, half), F32),
        pltpu.VMEM((rows, half), BF16),
        pltpu.VMEM((8 * groups, rows), F32),
        pltpu.VMEM((rows, q_half), BF16),
        pltpu.VMEM((rows, 3 * rows), F32),
        pltpu.VMEM((rows, 128), F32),
        pltpu.VMEM((128, rows), F32),
        pltpu.VMEM((128, rows), F32),
        pltpu.VMEM((rows, 128), F32),
        pltpu.VMEM((rows, 128), F32),
        pltpu.SemaphoreType.DMA((23,)),
        pltpu.SemaphoreType.DMA((18 + kv_half // ATT_DIM * 2 + 3 * group_pieces,)),
        pltpu.SemaphoreType.DMA((11,)),
    ]
    raw, sums, attended = pl.pallas_call(
        functools.partial(pair_kernel, lax.axis_size("ctx")),
        out_shape=(
            pltpu.VMEM((part, 4 * half), BF16),
            pltpu.VMEM((8 * GROUPS, tok), F32),
            pltpu.VMEM((part, 4 * q_half), BF16),
        ),
        in_specs=[pl.BlockSpec(memory_space=pltpu.SMEM)] + [any_spec] * 8 + [vmem_spec] * 2,
        out_specs=(vmem_spec, vmem_spec, vmem_spec),
        scratch_shapes=scratch,
        compiler_params=pltpu.CompilerParams(collective_id=0, has_side_effects=True),
    )(
        doc_lengths,
        ssm_x,
        ssm_gate,
        ssm_b,
        ssm_c,
        step_size.T,
        queries,
        keys,
        values,
        decay_rate[None, :],
        norm_weight[None, :],
    )
    return pl.pallas_call(
        scale_kernel,
        out_shape=(
            jax.ShapeDtypeStruct(raw.shape, BF16),
            jax.ShapeDtypeStruct(attended.shape, BF16),
        ),
        in_specs=[vmem_spec] * 3,
        out_specs=(any_spec, any_spec),
        scratch_shapes=[pltpu.VMEM(raw.shape, BF16), pltpu.SemaphoreType.DMA((GROUPS + 1,))],
    )(*[pltpu.with_memory_space_constraint(a, pltpu.VMEM) for a in (raw, sums, attended)])


def solution(mesh):
    tp = mesh.shape["tp"]
    paired = tp == 2 and mesh.shape["ctx"] % 4 == 0 and mesh.shape["ctx"] > 4 and GROUPS // tp % 2 == 0
    return jax.shard_map(
        local_pair if paired else local_any,
        mesh=mesh,
        in_specs=(
            P(),
            P("ctx", "tp"),
            P("ctx", "tp"),
            P("ctx", "tp"),
            P("ctx", "tp"),
            P("ctx", "tp"),
            P("tp"),
            P("tp"),
            P("ctx", "tp"),
            P("ctx", "tp"),
            P("ctx", "tp"),
        ),
        out_specs=(P(("ctx", "tp"), None), P(("ctx", "tp"), None)),
        check_vma=False,
    )
```

```python
import functools

import jax
import jax.numpy as jnp
from jax import lax
from jax.experimental import pallas as pl
from jax.experimental.pallas import tpu as pltpu
from jax.sharding import PartitionSpec as P

HEADS = 128
GROUPS = 8
ATT_DIM = 128
DOC_DEVS = 4


NEG_LARGE = -1e30


def for_sending(x):
    return jax.tree.map(lambda a: a.astype(jnp.bfloat16) if a.dtype == jnp.float32 else a, x)


def passed_along(block, axis, distance):
    devices = range(lax.axis_size(axis))
    route = [(i - distance, i) for i in devices if i - distance in devices]
    return lax.ppermute(block, axis, route)


def doc_starts(doc_lengths):
    return jnp.cumsum(doc_lengths) - doc_lengths


def doc_index(positions, starts):
    return jnp.sum((starts[None, :] <= positions[:, None]).astype(jnp.int32), axis=1) - 1


def block_terms(ssm_x, ssm_b, ssm_c, step_size, decay_rate, doc_ids, prev_id, group_heads):
    tok_rows = ssm_x.shape[0]
    head_count = step_size.shape[1]
    group_count = head_count // group_heads
    head_size = ssm_x.shape[1] // head_count
    state_size = ssm_b.shape[1] // group_count
    inputs = ssm_x.reshape(tok_rows, group_count, group_heads, head_size)
    in_proj = ssm_b.reshape(tok_rows, group_count, state_size)
    out_proj = ssm_c.reshape(tok_rows, group_count, state_size)
    log_decay = -(step_size * decay_rate[None, :])
    cumulative = jnp.cumsum(log_decay, axis=0)
    same_doc = doc_ids[:, None] == doc_ids[None, :]
    causal = jnp.arange(tok_rows)[:, None] >= jnp.arange(tok_rows)[None, :]
    allowed = (same_doc & causal)[None]
    spread = cumulative.T[:, :, None] - cumulative.T[:, None, :]
    weights = (
        jnp.where(allowed, jnp.exp(jnp.where(allowed, spread, 0.0)), 0.0) * step_size.T[:, None, :]
    )
    intersection = jnp.einsum("tgn,sgn->gts", out_proj, in_proj, preferred_element_type=jnp.float32)
    mixing = (
        weights.reshape(group_count, group_heads, tok_rows, tok_rows) * intersection[:, None]
    ).astype(jnp.bfloat16)
    y_intra = jnp.einsum("ghts,sghp->tghp", mixing, inputs, preferred_element_type=jnp.float32)
    final_sum = cumulative[-1]
    tail = (
        jnp.exp(final_sum[None, :] - cumulative)
        * step_size
        * (doc_ids == doc_ids[-1]).astype(jnp.float32)[:, None]
    )
    scaled = (
        inputs.astype(jnp.float32) * tail.reshape(tok_rows, group_count, group_heads)[..., None]
    ).astype(jnp.bfloat16)
    state_local = jnp.einsum("sghp,sgn->ghpn", scaled, in_proj, preferred_element_type=jnp.float32)
    entry = jnp.exp(cumulative) * (doc_ids == prev_id).astype(jnp.float32)[:, None]
    transmit = jnp.exp(final_sum) * (doc_ids[-1] == prev_id).astype(jnp.float32)
    return (y_intra, state_local, entry, transmit.reshape(group_count, group_heads))


def finish_rows(y_intra, entry, carried, ssm_c, ssm_gate, norm_weight):
    tok_rows, group_count, group_heads, head_size = y_intra.shape
    out_proj = ssm_c.reshape(tok_rows, group_count, -1).astype(jnp.float32)
    incoming = jnp.einsum("tgn,ghpn->tghp", out_proj, carried, precision=lax.Precision.HIGHEST)
    mixer_out = y_intra + incoming * entry.reshape(tok_rows, group_count, group_heads)[..., None]
    gate_vals = ssm_gate.reshape(tok_rows, group_count, group_heads, head_size).astype(jnp.float32)
    gated = (mixer_out * jax.nn.silu(gate_vals)).reshape(
        tok_rows, group_count, group_heads * head_size
    )
    factor = lax.rsqrt(jnp.mean(gated * gated, axis=2, keepdims=True) + 1e-05)
    return ((gated * factor).reshape(tok_rows, -1) * norm_weight[None, :]).astype(jnp.bfloat16)


def chain_states(earlier, later):
    return (earlier[0] * later[0], later[0][:, :, None, None] * earlier[1] + later[1])


def attention_update(
    carry, query_rows, key_block, value_block, key_pos, query_pos, query_doc, starts
):
    running_max, running_sum, running_acc = carry
    block_rows = key_block.shape[0]
    kv_local = key_block.shape[1] // ATT_DIM
    key_heads = key_block.reshape(block_rows, kv_local, ATT_DIM)
    value_heads = value_block.reshape(block_rows, kv_local, ATT_DIM)
    key_doc = doc_index(key_pos, starts)
    allowed = (query_doc[:, None] == key_doc[None, :]) & (key_pos[None, :] <= query_pos[:, None])
    scores = jnp.einsum(
        "tngd,knd->ngtk", query_rows, key_heads, preferred_element_type=jnp.float32
    ) * ATT_DIM ** (-0.5)
    scores = jnp.where(allowed[None, None], scores, -jnp.inf)
    new_max = jnp.maximum(running_max, jnp.max(scores, axis=3))
    probs = jnp.exp(scores - new_max[..., None])
    factor = jnp.exp(running_max - new_max)
    new_sum = running_sum * factor + jnp.sum(probs, axis=3)
    weighted = jnp.einsum(
        "ngtk,knd->ngtd",
        probs.astype(jnp.bfloat16),
        value_heads,
        preferred_element_type=jnp.float32,
    )
    return (new_max, new_sum, running_acc * factor[..., None] + weighted)


def local_any(
    doc_lengths,
    ssm_x,
    ssm_gate,
    ssm_b,
    ssm_c,
    step_size,
    decay_rate,
    norm_weight,
    queries,
    keys,
    values,
):
    tok_rows = ssm_x.shape[0]
    ctx_index = lax.axis_index("ctx")
    begin = ctx_index * tok_rows
    positions = begin + jnp.arange(tok_rows, dtype=jnp.int32)
    starts = doc_starts(doc_lengths)
    doc_ids = doc_index(positions, starts)
    prev_id = doc_index(jnp.reshape(begin - 1, (1,)), starts)[0]
    group_heads = HEADS // GROUPS
    y_intra, state_local, entry, transmit = block_terms(
        ssm_x, ssm_b, ssm_c, step_size, decay_rate, doc_ids, prev_id, group_heads
    )
    merged = (transmit, state_local)
    for level_bit in range(DOC_DEVS.bit_length() - 1):
        earlier = passed_along(
            (for_sending(merged[0]), for_sending(merged[1])), "ctx", 1 << level_bit
        )
        merged = chain_states(earlier, merged)
    carried = passed_along(merged[1], "ctx", 1)
    mixed_rows = finish_rows(y_intra, entry, carried, ssm_c, ssm_gate, norm_weight)
    kv_local = keys.shape[1] // ATT_DIM
    q_groups = queries.shape[1] // (kv_local * ATT_DIM)
    query_rows = queries.reshape(tok_rows, kv_local, q_groups, ATT_DIM)
    floor_start = jnp.max(jnp.where(starts <= begin, starts, 0))
    query_last = begin + tok_rows - 1
    carry_shape = (kv_local, q_groups, tok_rows)
    initial = (
        jnp.full(carry_shape, NEG_LARGE, jnp.float32),
        jnp.zeros(carry_shape, jnp.float32),
        jnp.zeros(carry_shape + (ATT_DIM,), jnp.float32),
    )

    def visit(carry, key_block, value_block, key_begin):
        block_rows = key_block.shape[0]
        needed = (key_begin <= query_last) & (key_begin + block_rows - 1 >= floor_start)

        def update(inner):
            key_pos = key_begin + jnp.arange(block_rows, dtype=jnp.int32)
            return attention_update(
                inner, query_rows, key_block, value_block, key_pos, positions, doc_ids, starts
            )

        def unchanged(inner):
            return inner

        return lax.cond(needed, update, unchanged, carry)

    totals = visit(initial, keys, values, begin)
    for hop_count in range(1, DOC_DEVS + 1):
        near_keys, near_values = passed_along((keys, values), "ctx", hop_count)
        totals = visit(totals, near_keys, near_values, begin - hop_count * tok_rows)
    final_out = totals[2] / totals[1][..., None]
    attended_rows = (
        jnp.transpose(final_out, (2, 0, 1, 3)).reshape(tok_rows, -1).astype(jnp.bfloat16)
    )
    mixed_local, attended_local = (
        lax.all_to_all(mixed_rows, "tp", split_axis=0, concat_axis=1, tiled=True),
        lax.all_to_all(attended_rows, "tp", split_axis=0, concat_axis=1, tiled=True),
    )
    return (mixed_local, attended_local)


LOG2E = 1.4426950408889634
F32 = jnp.float32
BF16 = jnp.bfloat16
MESH_ID = pl.DeviceIdType.MESH
COLS_LAST = (((1,), (1,)), ((), ()))
ROWS_FIRST = (((0,), (0,)), ((), ()))
PIECE = 128
HEADS_AT_ONCE = 2
MERGE_AFTER = (1, 2, 3, 5, 6, 7)
PASS_AFTER = (4, 5, 7)


def dot(a, b, dims=(((1,), (0,)), ((), ())), precision=None):
    return lax.dot_general(a, b, dims, precision=precision, preferred_element_type=F32)


def spread_heads(columns, head, head_size):
    lane = lax.broadcasted_iota(jnp.int32, (columns.shape[0], 128), 1)
    wide = jnp.broadcast_to(columns[:, head : head + 1], lane.shape)
    for k in range(1, 128 // head_size):
        wide = jnp.where(lane >= k * head_size, columns[:, head + k : head + k + 1], wide)
    return wide


def pair_kernel(
    n,
    lengths,
    x_in,
    gate_in,
    b_in,
    c_in,
    step_in,
    q_in,
    k_in,
    v_in,
    rate_ref,
    weight_ref,
    raw_out,
    sums_out,
    attended_out,
    x_s,
    gate_s,
    b_s,
    c_s,
    step_s,
    q_s,
    kv_s,
    own_s,
    beside_s,
    merged_s,
    behind_s,
    passed_s,
    second_s,
    t_own,
    t_beside,
    coef_s,
    loan_s,
    y_s,
    raw_s,
    sums_s,
    attended_s,
    bias_s,
    l_s,
    lt_s,
    dtt_s,
    tail_s,
    entry_s,
    send_sem,
    recv_sem,
    own_sem,
):
    index = lax.axis_index("ctx")
    tp = lax.axis_index("tp")
    parity, pair = lax.rem(index, 2), lax.div(index, 2)
    odd = lax.rem(pair, 2)
    base = index - parity
    other = 1 - parity
    tok = x_in.shape[0]
    rows = 2 * tok
    width = x_s.shape[1]
    group_heads = HEADS // GROUPS
    heads = step_in.shape[0] // 2
    groups = heads // group_heads
    group_width = width // groups
    state = b_s.shape[1] // groups
    head_size = width // heads
    kv_width = kv_s.shape[2]
    kv_heads = kv_width // ATT_DIM
    q_width = q_s.shape[1] // kv_heads
    pieces = group_width // PIECE
    group_of = (odd, 1 - odd)

    core_peer = (base + other, tp)
    tp_peer = (index, 1 - tp)
    cross_peer = (base + other, 1 - tp)
    beside = (index + 2 - 4 * odd, tp)
    barrier = pltpu.get_barrier_semaphore()
    greeted = jnp.int32(3)
    reach = {}
    for step in (2, 4, -2, -4):
        reach[step] = (base + step >= 0) & (base + step < n)
        greeted += 2 * reach[step].astype(jnp.int32)

        @pl.when(reach[step])
        def _():
            for core in range(2):
                peer = (base + step + core, tp)
                pl.semaphore_signal(barrier, inc=1, device_id=peer, device_id_type=MESH_ID)

    for peer in (core_peer, tp_peer, cross_peer):
        pl.semaphore_signal(barrier, inc=1, device_id=peer, device_id_type=MESH_ID)
    ahead, behind = reach[4], reach[-4]

    used = [0, 0, 0]

    def slots(kind, count=1):
        used[kind] += count
        return used[kind] - count

    def remote(src, dst, peer, send, recv):
        return pltpu.make_async_remote_copy(
            src_ref=src,
            dst_ref=dst,
            send_sem=send_sem.at[send],
            recv_sem=recv_sem.at[recv],
            device_id=peer,
            device_id_type=MESH_ID,
        )

    at_mine = pl.multiple_of(parity * tok, tok)
    mine = pl.ds(at_mine, tok)
    closing = []

    def trade(moves, whole):
        send, recv, own = slots(0), slots(1), slots(2)
        for give, keep, place in moves:
            pltpu.make_async_copy(keep, place, own_sem.at[own]).start()
        closing.append(remote(whole, whole, core_peer, send, recv).wait_send)

        def start():
            for give, keep, place in moves:
                remote(give, place, core_peer, send, recv).start()

        def ready():
            pltpu.make_async_copy(whole, whole, own_sem.at[own]).wait()
            remote(whole, whole, core_peer, send, recv).wait_recv()

        return start, ready

    def by_group(src, dst, local_groups):
        size = dst.shape[1] // groups

        def part(core, local):
            at = core * groups * size + group_of[local] * size
            return src.at[:, pl.ds(pl.multiple_of(at, 128), size)]

        moves, first = [], local_groups[0]
        for local in local_groups:
            place = dst.at[mine, local * size : (local + 1) * size]
            moves.append((part(other, local), part(parity, local), place))
        return trade(moves, dst.at[:tok, first * size : (first + len(local_groups)) * size])

    def part_of(src, core, begin, size, total):
        return src.at[:, pl.ds(pl.multiple_of(core * total + begin, 128), size)]

    @pl.when(pair < 2)
    def _():
        kv_s[:, :rows, :] = jnp.zeros((2, rows, kv_width), BF16)

    @pl.when(pair < 1)
    def _():
        kv_s[:, rows : 2 * rows, :] = jnp.zeros((2, rows, kv_width), BF16)

    past_send = (slots(0), slots(0))
    past_recv = [(slots(1), slots(1)) for head in range(kv_heads)]
    loan_send, loan_recv = slots(0), slots(1)

    def head_cols(head):
        return slice(head * ATT_DIM, (head + 1) * ATT_DIM)

    def send_past(head, dst, step, skip, which, recv):
        for k, src in enumerate((k_in, v_in)):
            for core in range(2):
                remote(
                    part_of(src, core, head * ATT_DIM, ATT_DIM, kv_width),
                    dst.at[k, pl.ds(at_mine + skip, tok), :],
                    (base + step + core, tp),
                    which,
                    recv,
                ).start()

    def send_near(head):
        near = kv_s.at[:, :, head_cols(head)]

        @pl.when(reach[2] & ((odd == 0) | (head == 0)))
        def _():
            send_past(head, near, 2, rows, past_send[0], past_recv[head][0])

    def lend():
        @pl.when(odd == 1)
        def _():
            for head in range(1, kv_heads):
                send_past(head, loan_s.at[:, :, head_cols(head - 1)], -2, 0, loan_send, loan_recv)

    def send_far(head):
        @pl.when(reach[4])
        def _():
            far = kv_s.at[:, :, head_cols(head)]
            send_past(head, far, 4, 0, past_send[1], past_recv[head][1])

    def near_loan():
        return kv_s.at[:, rows : 2 * rows, ATT_DIM:]

    def forward():
        @pl.when(odd == 0)
        def _():
            remote(loan_s, loan_s, core_peer, loan_send, loan_recv).wait_recv()

        @pl.when((odd == 0) & ahead)
        def _():
            peer = (index + 4, tp)
            remote(loan_s, near_loan(), peer, loan_send, past_recv[1][0]).start()

    def wait_past(head):
        for which, step, skip in ((0, -2, rows), (1, -4, 0)):

            @pl.when(reach[step])
            def _():
                place = kv_s.at[:, skip : skip + rows, head_cols(head)]
                remote(place, place, core_peer, past_send[which], past_recv[head][which]).wait_recv()

    moves = []
    for local in range(groups):
        place = step_s.at[local * group_heads : (local + 1) * group_heads, mine]

        def step_part(core):
            at = (core * groups + group_of[local]) * group_heads
            return step_in.at[pl.ds(pl.multiple_of(at, 8), group_heads)]

        moves.append((step_part(other), step_part(parity), place))
    start_step, ready_step = trade(moves, step_s.at[:, :tok])
    start_b, ready_b = by_group(b_in, b_s, tuple(range(groups)))
    trade_x = {local: by_group(x_in, x_s, (local,)) for local in (1, 0)}
    start_c, ready_c = by_group(c_in, c_s, tuple(range(groups)))
    moves = []
    for k, src in enumerate((k_in, v_in)):
        give = part_of(src, other, 0, kv_width, kv_width)
        keep = part_of(src, parity, 0, kv_width, kv_width)
        moves.append((give, keep, kv_s.at[k, pl.ds(at_mine + 2 * rows, tok), :]))
    start_kv, ready_kv = trade(moves, kv_s.at[:, 2 * rows : 2 * rows + tok, :])
    q_all = q_s.shape[1]
    give, keep = part_of(q_in, other, 0, q_all, q_all), part_of(q_in, parity, 0, q_all, q_all)
    start_q, ready_q = trade([(give, keep, q_s.at[mine, :])], q_s.at[:tok, :])
    start_gate, ready_gate = by_group(gate_in, gate_s, tuple(range(groups)))

    @pl.when(pair < 2)
    def _():
        behind_s[...] = jnp.zeros_like(behind_s)

    begin = pair * rows
    row_at = begin - 2 * rows + lax.broadcasted_iota(jnp.int32, (1, 3 * rows), 1)
    col_at = begin + lax.broadcasted_iota(jnp.int32, (rows, 1), 0)
    row_doc = jnp.zeros_like(row_at) - 1
    col_doc = jnp.zeros_like(col_at) - 1
    begun, prev_id, last_id = jnp.int32(0), jnp.int32(-1), jnp.int32(-1)
    for j in range(lengths.shape[0]):
        row_doc += (row_at >= begun).astype(jnp.int32)
        col_doc += (col_at >= begun).astype(jnp.int32)
        prev_id += (begin - 1 >= begun).astype(jnp.int32)
        last_id += (begin + rows - 1 >= begun).astype(jnp.int32)
        begun = begun + lengths[j]
    bias_s[...] = jnp.where((row_doc == col_doc) & (row_at <= col_at), 0.0, NEG_LARGE)

    pl.semaphore_wait(barrier, greeted)
    send_near(0)
    start_step()
    start_b()
    send_far(0)
    for local in (1, 0):
        trade_x[local][0]()
    for head in range(1, kv_heads):
        send_near(head)
        send_far(head)
    for start in (start_c, start_kv, start_q, start_gate):
        start()

    ready_step()
    step_t = jnp.concatenate([step_s[...], jnp.zeros((128 - heads, rows), F32)], axis=0)
    step = step_t.T
    rates = []
    for local in range(groups):
        rate = jnp.zeros((1, group_heads), F32)
        for k in range(2 * groups):
            here = parity * groups + group_of[local] == k
            rate = jnp.where(here, rate_ref[:, k * group_heads : (k + 1) * group_heads], rate)
        rates.append(rate)
    rate = jnp.concatenate(rates + [jnp.zeros((1, 128 - heads), F32)], axis=1)
    at = lax.broadcasted_iota(jnp.int32, (rows, rows), 0)
    to = lax.broadcasted_iota(jnp.int32, (rows, rows), 1)
    lower = (to <= at).astype(BF16)
    left, parts = -(step * rate), []
    for k in range(3):
        parts.append(left.astype(BF16)[:, :heads])
        left = left - left.astype(BF16).astype(F32)
    parts.append(jnp.zeros((rows, 128 - 3 * heads), BF16))
    sums = dot(lower, jnp.concatenate(parts, axis=1))
    lane = lax.broadcasted_iota(jnp.int32, (rows, 128), 1)
    sums = sums + pltpu.roll(sums, 128 - heads, 1) + pltpu.roll(sums, 128 - 2 * heads, 1)
    total_decay = jnp.where(lane < heads, sums, 0.0)
    final_sum = total_decay[rows - 1 :, :]
    l_s[...] = total_decay
    lt_s[...] = total_decay.T
    dtt_s[...] = step_t
    tail_s[...] = jnp.where(col_doc == last_id, jnp.exp(final_sum - total_decay) * step, 0.0)
    entry_s[...] = jnp.where(col_doc == prev_id, jnp.exp(total_decay), 0.0)
    passing = (last_id == prev_id).astype(F32)
    t_own[...] = jnp.broadcast_to(jnp.exp(final_sum) * passing, t_own.shape)
    t_trip = remote(t_own, t_beside, beside, slots(0), slots(1))
    t_trip.start()
    closing.append(t_trip.wait_send)

    first_send, first_recv = slots(0), slots(1, pieces)
    merge_send, merge_recv = slots(0), slots(1, pieces)
    pass_send, pass_recv = slots(0), slots(1, pieces)

    def first_trip(k):
        return remote(
            own_s.at[pieces + k], beside_s.at[k], beside, first_send, first_recv + k
        )

    def merge_trip(k):
        return remote(
            merged_s.at[k], behind_s.at[k], (index + 4, tp), merge_send, merge_recv + k
        )

    def pass_trip(k):
        return remote(passed_s.at[k], second_s.at[k], beside, pass_send, pass_recv + k)

    per = 128 // head_size
    lend()
    ready_b()
    for local in (1, 0):
        trade_x[local][1]()
        b_t = b_s[:, local * state : (local + 1) * state].T
        for k in range(local * pieces, (local + 1) * pieces, 2):
            parts = []
            for tile in range(2):
                lead = (k + tile) * PIECE
                wide = spread_heads(tail_s[...], lead // head_size, head_size)
                parts.append((x_s[:, lead : lead + PIECE].astype(F32) * wide).astype(BF16))
            made = dot(b_t, jnp.concatenate(parts, axis=1)).astype(BF16)
            for tile in range(2):
                own_s[k + tile] = made[:, tile * PIECE : (tile + 1) * PIECE]
                if local == 1:
                    first_trip(k + tile - pieces).start()

    ready_c()
    for g in range(groups):
        proj = slice(g * state, (g + 1) * state)
        inter = dot(c_s[:, proj], b_s[:, proj], COLS_LAST)
        for tile in range(group_width // 128):
            lead = g * group_width + tile * 128
            halves = []
            for r in range(0, rows, tok):
                seen = slice(0, r + tok)
                bias = bias_s[r : r + tok, 2 * rows : 2 * rows + r + tok]
                mixing = []
                for h in range(lead // head_size, lead // head_size + per):
                    spread = l_s[r : r + tok, h : h + 1] - lt_s[h : h + 1, seen]
                    w = jnp.exp(spread + bias) * dtt_s[h : h + 1, seen] * inter[r : r + tok, seen]
                    mixing.append(w.astype(BF16))
                both = dot(jnp.concatenate(mixing, axis=0), x_s[seen, lead : lead + 128])
                whole = both[:tok]
                for k in range(1, per):
                    part = both[k * tok : (k + 1) * tok]
                    whole = jnp.where(lane[:tok] >= k * head_size, part, whole)
                y_s[r : r + tok, lead : lead + 128] = whole

    part_rows = rows // 4
    exits = ((tp_peer, 0, 1), (cross_peer, 1, 1), (core_peer, 1, 0))

    def exit_slots():
        return slots(0, 3), slots(1, 3), slots(2)

    def leave(sems, piece_for, home):
        send, recv, own = sems
        for k, (peer, far_core, far_tp) in enumerate(exits):
            src = piece_for(other if far_core else parity, 1 - tp if far_tp else tp)
            remote(src, home, peer, send + k, recv + k).start()
        pltpu.make_async_copy(piece_for(parity, tp), home, own_sem.at[own]).start()

    def settle(sems, whole):
        send, recv, own = sems
        for k, (peer, far_core, far_tp) in enumerate(exits):
            remote(whole, whole, peer, send + k, recv + k).wait()
        pltpu.make_async_copy(whole, whole, own_sem.at[own]).wait()

    raw_exit, attended_exit, sums_exit = exit_slots(), exit_slots(), exit_slots()

    def coefficients():
        t_trip.wait_recv()
        even = jnp.broadcast_to(odd == 0, (8, 128))
        row = lax.broadcasted_iota(jnp.int32, (8, 128), 0)
        for k in range(pieces):
            h = k * PIECE // head_size
            ours = spread_heads(t_own[...], h, head_size)
            theirs = spread_heads(t_beside[...], group_heads + h, head_size)
            values = (
                (1.0, ours),
                (theirs, 1.0),
                (1.0, 0.0),
                (ours, 1.0),
                (0.0, 1.0),
                (1.0, theirs),
            )
            table = jnp.zeros((8, 128), F32)
            for j, (if_even, if_odd) in enumerate(values):
                table = jnp.where(row == j, jnp.where(even, if_even, if_odd), table)
            coef_s[:, k * PIECE : (k + 1) * PIECE] = table

    def blend(left, right, k, row):
        cols = slice(k * PIECE, (k + 1) * PIECE)
        total = left[k].astype(F32) * coef_s[row : row + 1, cols]
        total += right[k].astype(F32) * coef_s[row + 1 : row + 2, cols]
        return total.astype(BF16)

    def merge(k):
        first_trip(k).wait_recv()
        merged_s[k] = blend(beside_s, own_s, k, 0)

        @pl.when(ahead)
        def _():
            merge_trip(k).start()

    def pass_on(k):
        @pl.when(behind)
        def _():
            merge_trip(k).wait_recv()

        passed_s[k] = blend(own_s, behind_s, k, 2)
        pass_trip(k).start()

    scale = LOG2E * ATT_DIM ** (-0.5)
    ready_kv()
    ready_q()
    step_no = 0
    for kv_head in range(kv_heads):
        kv_cols = slice(kv_head * ATT_DIM, (kv_head + 1) * ATT_DIM)
        wait_past(kv_head)
        for lead in range(kv_head * q_width, (kv_head + 1) * q_width, HEADS_AT_ONCE * ATT_DIM):
            for r in range(0, rows, tok):
                seen = slice(r, r + 2 * rows + tok)
                asked = jnp.concatenate(
                    [
                        q_s[r : r + tok, lead + h * ATT_DIM : lead + (h + 1) * ATT_DIM]
                        for h in range(HEADS_AT_ONCE)
                    ],
                    axis=0,
                )
                scores = dot(asked, kv_s[0, seen, kv_cols], COLS_LAST)
                bias = bias_s[r : r + tok, seen]
                scores = scores + jnp.concatenate([bias] * HEADS_AT_ONCE, axis=0)
                top = jnp.max(scores, axis=1, keepdims=True)
                probs = jnp.exp2((scores - top) * scale)
                total = jnp.sum(probs, axis=1, keepdims=True)
                summed = dot(probs.astype(BF16), kv_s[1, seen, kv_cols]) / total
                for h in range(HEADS_AT_ONCE):
                    part = summed[h * tok : (h + 1) * tok].astype(BF16)
                    for side in range(2):
                        owned = part[side * part_rows : (side + 1) * part_rows]
                        cols = slice(h * ATT_DIM, (h + 1) * ATT_DIM)
                        attended_s[step_no, r // tok * 2 + side, :, cols] = owned
            size = HEADS_AT_ONCE * ATT_DIM
            at = pl.multiple_of((tp * 2 + parity) * q_all + lead, 128)
            home = attended_out.at[:, pl.ds(at, size)]
            here = attended_s.at[step_no]
            leave(attended_exit, lambda core, side: here.at[core * 2 + side], home)
            if step_no == 0:
                forward()
            for k in range(len(MERGE_AFTER)):
                if MERGE_AFTER[k] == step_no:
                    if k == 0:
                        coefficients()
                    merge(k)
            for k in range(len(PASS_AFTER)):
                if PASS_AFTER[k] == step_no:
                    pass_on(k)
            step_no += 1

    ones = jnp.ones((8, 128), F32)
    squares = [jnp.zeros((rows, 128), F32)] * groups

    def finish(local, first, count):
        carried = []
        for k in range(first, first + count):
            if local == 0:
                carried.append(blend(beside_s, behind_s, k, 4))
            else:
                pass_trip(k).wait_recv()
                carried.append(second_s[k])
        proj = slice(local * state, (local + 1) * state)
        incoming = dot(c_s[:, proj], jnp.concatenate(carried, axis=1))
        lead = local * group_width + first * PIECE
        square = squares[local]
        for tile in range(0, count * PIECE, 128):
            cols = slice(lead + tile, lead + tile + 128)
            wide = spread_heads(entry_s[...], cols.start // head_size, head_size)
            z = gate_s[:, cols].astype(F32)
            total = y_s[:, cols] + incoming[:, tile : tile + 128] * wide
            total = total * (z / (1.0 + jnp.exp(-z)))
            square += total * total
            at = parity * width + group_of[local] * group_width + first * PIECE + tile
            gain = weight_ref[:, pl.ds(pl.multiple_of(at, 128), 128)]
            done = (total * gain).astype(BF16)
            for rank in range(4):
                owned = done[rank * part_rows : (rank + 1) * part_rows]
                raw_s[rank, cols.start // PIECE] = owned
        squares[local] = square
        at = ((tp * 2 + parity) * groups + group_of[local]) * pieces + first
        here = pl.ds(lead // PIECE, count)
        leave(
            raw_exit,
            lambda core, side: raw_s.at[core * 2 + side, here],
            raw_out.at[pl.ds(at, count)],
        )
        if first + count == pieces:
            here = slice(local * 8, local * 8 + 8)
            sums_s[here, :] = dot(ones, square, COLS_LAST, lax.Precision.HIGHEST)
            at = ((tp * 2 + parity) * groups + group_of[local]) * 8
            home = sums_out.at[pl.ds(pl.multiple_of(at, 8), 8), :]

            def half(core, side):
                return sums_s.at[here, pl.ds(pl.multiple_of(core * tok, tok), tok)]

            leave(sums_exit, half, home)

    ready_gate()
    merged, passed = len(MERGE_AFTER), len(PASS_AFTER)
    for k in range(0, pieces, 2):
        while passed < k + 2:
            pass_on(passed)
            passed += 1
        finish(0, k, 2)
        if merged < pieces:
            merge(merged)
            merged += 1
        if passed < pieces:
            pass_on(passed)
            passed += 1
    for k in range(pieces):
        finish(1, k, 1)

    assert used == [send_sem.shape[0], recv_sem.shape[0], own_sem.shape[0]], used
    for close in closing:
        close()
    sent = kv_s.at[:, :rows, :]

    @pl.when(ahead)
    def _():
        remote(sent, sent, core_peer, past_send[1], past_recv[0][1]).wait_send()

    @pl.when(odd == 0)
    def _():
        remote(sent, sent, core_peer, past_send[0], past_recv[0][0]).wait_send()

    @pl.when((odd == 1) & reach[2])
    def _():
        part = kv_s.at[:, :rows, :ATT_DIM]
        remote(part, part, core_peer, past_send[0], past_recv[0][0]).wait_send()

    @pl.when((odd == 1) | ahead)
    def _():
        remote(loan_s, loan_s, core_peer, loan_send, loan_recv).wait_send()

    half = own_s.at[:pieces]
    remote(half, half, beside, first_send, first_recv).wait_send()
    remote(half, half, beside, pass_send, pass_recv).wait_send()

    @pl.when(ahead)
    def _():
        remote(half, half, beside, merge_send, merge_recv).wait_send()

    settle(attended_exit, attended_s.at[:, 0])
    settle(raw_exit, raw_s.at[0])
    settle(sums_exit, sums_s.at[:, :tok])


def scale_kernel(raw, sums, attended, mixed_out, attended_out, mixed_s, sem):
    tp = lax.axis_index("tp")
    rows, width = mixed_s.shape
    group_width = width // GROUPS
    whole = pltpu.make_async_copy(attended, attended_out, sem.at[GROUPS])
    whole.start()
    squares = sums[...]
    squares = jnp.concatenate([squares, jnp.zeros((128 - squares.shape[0], 128), F32)], axis=0).T
    squares = jnp.where(tp == 0, squares[:rows], squares[rows:])
    factor = lax.rsqrt(squares * (1.0 / group_width) + 1e-05)
    copies = [whole]
    for g in range(GROUPS):
        for k in range(g * group_width // PIECE, (g + 1) * group_width // PIECE):
            scaled = raw[k].astype(F32) * factor[:, 8 * g : 8 * g + 1]
            mixed_s[:, k * PIECE : (k + 1) * PIECE] = scaled.astype(BF16)
        cols = slice(g * group_width, (g + 1) * group_width)
        copy = pltpu.make_async_copy(mixed_s.at[:, cols], mixed_out.at[:, cols], sem.at[g])
        copy.start()
        copies.append(copy)
    for copy in copies:
        copy.wait()


def local_pair(
    doc_lengths,
    ssm_x,
    ssm_gate,
    ssm_b,
    ssm_c,
    step_size,
    decay_rate,
    norm_weight,
    queries,
    keys,
    values,
):
    tok, width = ssm_x.shape
    rows, half = 2 * tok, width // 2
    groups = step_size.shape[1] * GROUPS // HEADS // 2
    state = ssm_b.shape[1] // (2 * groups)
    kv_half = keys.shape[1] // 2
    q_half = queries.shape[1] // 2
    pieces = half // PIECE
    any_spec = pl.BlockSpec(memory_space=pl.ANY)
    vmem_spec = pl.BlockSpec(memory_space=pltpu.VMEM)
    part = rows // 4
    group_pieces = pieces // groups
    step_width = HEADS_AT_ONCE * ATT_DIM
    state_piece = pltpu.VMEM((group_pieces, state, PIECE), BF16)
    scratch = [
        pltpu.VMEM((rows, half), BF16),
        pltpu.VMEM((rows, half), BF16),
        pltpu.VMEM((rows, groups * state), BF16),
        pltpu.VMEM((rows, groups * state), BF16),
        pltpu.VMEM((step_size.shape[1] // 2, rows), F32),
        pltpu.VMEM((rows, q_half), BF16),
        pltpu.VMEM((2, 3 * rows, kv_half), BF16),
        pltpu.VMEM((pieces, state, PIECE), BF16),
        state_piece,
        state_piece,
        state_piece,
        state_piece,
        state_piece,
        pltpu.VMEM((8, 128), F32),
        pltpu.VMEM((8, 128), F32),
        pltpu.VMEM((8, half // groups), F32),
        pltpu.VMEM((2, rows, kv_half - ATT_DIM), BF16),
        pltpu.VMEM((rows, half), F32),
        pltpu.VMEM((4, pieces, part, PIECE), BF16),
        pltpu.VMEM((8 * groups, rows), F32),
        pltpu.VMEM((q_half // step_width, 4, part, step_width), BF16),
        pltpu.VMEM((rows, 3 * rows), F32),
        pltpu.VMEM((rows, 128), F32),
        pltpu.VMEM((128, rows), F32),
        pltpu.VMEM((128, rows), F32),
        pltpu.VMEM((rows, 128), F32),
        pltpu.VMEM((rows, 128), F32),
        pltpu.SemaphoreType.DMA((24,)),
        pltpu.SemaphoreType.DMA((19 + kv_half // ATT_DIM * 2 + 3 * group_pieces,)),
        pltpu.SemaphoreType.DMA((11,)),
    ]
    raw, sums, attended = pl.pallas_call(
        functools.partial(pair_kernel, lax.axis_size("ctx")),
        out_shape=(
            pltpu.VMEM((4 * pieces, part, PIECE), BF16),
            pltpu.VMEM((8 * GROUPS, tok), F32),
            pltpu.VMEM((part, 4 * q_half), BF16),
        ),
        in_specs=[pl.BlockSpec(memory_space=pltpu.SMEM)] + [any_spec] * 8 + [vmem_spec] * 2,
        out_specs=(vmem_spec, vmem_spec, vmem_spec),
        scratch_shapes=scratch,
        compiler_params=pltpu.CompilerParams(collective_id=0, has_side_effects=True),
    )(
        doc_lengths,
        ssm_x,
        ssm_gate,
        ssm_b,
        ssm_c,
        step_size.T,
        queries,
        keys,
        values,
        decay_rate[None, :],
        norm_weight[None, :],
    )
    return pl.pallas_call(
        scale_kernel,
        out_shape=(
            jax.ShapeDtypeStruct((part, 4 * half), BF16),
            jax.ShapeDtypeStruct(attended.shape, BF16),
        ),
        in_specs=[vmem_spec] * 3,
        out_specs=(any_spec, any_spec),
        scratch_shapes=[pltpu.VMEM((part, 4 * half), BF16), pltpu.SemaphoreType.DMA((GROUPS + 1,))],
    )(*[pltpu.with_memory_space_constraint(a, pltpu.VMEM) for a in (raw, sums, attended)])


def solution(mesh):
    tp = mesh.shape["tp"]
    paired = tp == 2 and mesh.shape["ctx"] % 4 == 0 and mesh.shape["ctx"] > 4 and GROUPS // tp % 2 == 0
    return jax.shard_map(
        local_pair if paired else local_any,
        mesh=mesh,
        in_specs=(
            P(),
            P("ctx", "tp"),
            P("ctx", "tp"),
            P("ctx", "tp"),
            P("ctx", "tp"),
            P("ctx", "tp"),
            P("tp"),
            P("tp"),
            P("ctx", "tp"),
            P("ctx", "tp"),
            P("ctx", "tp"),
        ),
        out_specs=(P(("ctx", "tp"), None), P(("ctx", "tp"), None)),
        check_vma=False,
    )
```

```python
import functools

import jax
import jax.numpy as jnp
from jax import lax
from jax.experimental import pallas as pl
from jax.experimental.pallas import tpu as pltpu
from jax.sharding import PartitionSpec as P

HEADS = 128
GROUPS = 8
ATT_DIM = 128
DOC_DEVS = 4


NEG_LARGE = -1e30


def for_sending(x):
    return jax.tree.map(lambda a: a.astype(jnp.bfloat16) if a.dtype == jnp.float32 else a, x)


def passed_along(block, axis, distance):
    devices = range(lax.axis_size(axis))
    route = [(i - distance, i) for i in devices if i - distance in devices]
    return lax.ppermute(block, axis, route)


def doc_starts(doc_lengths):
    return jnp.cumsum(doc_lengths) - doc_lengths


def doc_index(positions, starts):
    return jnp.sum((starts[None, :] <= positions[:, None]).astype(jnp.int32), axis=1) - 1


def block_terms(ssm_x, ssm_b, ssm_c, step_size, decay_rate, doc_ids, prev_id, group_heads):
    tok_rows = ssm_x.shape[0]
    head_count = step_size.shape[1]
    group_count = head_count // group_heads
    head_size = ssm_x.shape[1] // head_count
    state_size = ssm_b.shape[1] // group_count
    inputs = ssm_x.reshape(tok_rows, group_count, group_heads, head_size)
    in_proj = ssm_b.reshape(tok_rows, group_count, state_size)
    out_proj = ssm_c.reshape(tok_rows, group_count, state_size)
    log_decay = -(step_size * decay_rate[None, :])
    cumulative = jnp.cumsum(log_decay, axis=0)
    same_doc = doc_ids[:, None] == doc_ids[None, :]
    causal = jnp.arange(tok_rows)[:, None] >= jnp.arange(tok_rows)[None, :]
    allowed = (same_doc & causal)[None]
    spread = cumulative.T[:, :, None] - cumulative.T[:, None, :]
    weights = (
        jnp.where(allowed, jnp.exp(jnp.where(allowed, spread, 0.0)), 0.0) * step_size.T[:, None, :]
    )
    intersection = jnp.einsum("tgn,sgn->gts", out_proj, in_proj, preferred_element_type=jnp.float32)
    mixing = (
        weights.reshape(group_count, group_heads, tok_rows, tok_rows) * intersection[:, None]
    ).astype(jnp.bfloat16)
    y_intra = jnp.einsum("ghts,sghp->tghp", mixing, inputs, preferred_element_type=jnp.float32)
    final_sum = cumulative[-1]
    tail = (
        jnp.exp(final_sum[None, :] - cumulative)
        * step_size
        * (doc_ids == doc_ids[-1]).astype(jnp.float32)[:, None]
    )
    scaled = (
        inputs.astype(jnp.float32) * tail.reshape(tok_rows, group_count, group_heads)[..., None]
    ).astype(jnp.bfloat16)
    state_local = jnp.einsum("sghp,sgn->ghpn", scaled, in_proj, preferred_element_type=jnp.float32)
    entry = jnp.exp(cumulative) * (doc_ids == prev_id).astype(jnp.float32)[:, None]
    transmit = jnp.exp(final_sum) * (doc_ids[-1] == prev_id).astype(jnp.float32)
    return (y_intra, state_local, entry, transmit.reshape(group_count, group_heads))


def finish_rows(y_intra, entry, carried, ssm_c, ssm_gate, norm_weight):
    tok_rows, group_count, group_heads, head_size = y_intra.shape
    out_proj = ssm_c.reshape(tok_rows, group_count, -1).astype(jnp.float32)
    incoming = jnp.einsum("tgn,ghpn->tghp", out_proj, carried, precision=lax.Precision.HIGHEST)
    mixer_out = y_intra + incoming * entry.reshape(tok_rows, group_count, group_heads)[..., None]
    gate_vals = ssm_gate.reshape(tok_rows, group_count, group_heads, head_size).astype(jnp.float32)
    gated = (mixer_out * jax.nn.silu(gate_vals)).reshape(
        tok_rows, group_count, group_heads * head_size
    )
    factor = lax.rsqrt(jnp.mean(gated * gated, axis=2, keepdims=True) + 1e-05)
    return ((gated * factor).reshape(tok_rows, -1) * norm_weight[None, :]).astype(jnp.bfloat16)


def chain_states(earlier, later):
    return (earlier[0] * later[0], later[0][:, :, None, None] * earlier[1] + later[1])


def attention_update(
    carry, query_rows, key_block, value_block, key_pos, query_pos, query_doc, starts
):
    running_max, running_sum, running_acc = carry
    block_rows = key_block.shape[0]
    kv_local = key_block.shape[1] // ATT_DIM
    key_heads = key_block.reshape(block_rows, kv_local, ATT_DIM)
    value_heads = value_block.reshape(block_rows, kv_local, ATT_DIM)
    key_doc = doc_index(key_pos, starts)
    allowed = (query_doc[:, None] == key_doc[None, :]) & (key_pos[None, :] <= query_pos[:, None])
    scores = jnp.einsum(
        "tngd,knd->ngtk", query_rows, key_heads, preferred_element_type=jnp.float32
    ) * ATT_DIM ** (-0.5)
    scores = jnp.where(allowed[None, None], scores, -jnp.inf)
    new_max = jnp.maximum(running_max, jnp.max(scores, axis=3))
    probs = jnp.exp(scores - new_max[..., None])
    factor = jnp.exp(running_max - new_max)
    new_sum = running_sum * factor + jnp.sum(probs, axis=3)
    weighted = jnp.einsum(
        "ngtk,knd->ngtd",
        probs.astype(jnp.bfloat16),
        value_heads,
        preferred_element_type=jnp.float32,
    )
    return (new_max, new_sum, running_acc * factor[..., None] + weighted)


def local_any(
    doc_lengths,
    ssm_x,
    ssm_gate,
    ssm_b,
    ssm_c,
    step_size,
    decay_rate,
    norm_weight,
    queries,
    keys,
    values,
):
    tok_rows = ssm_x.shape[0]
    ctx_index = lax.axis_index("ctx")
    begin = ctx_index * tok_rows
    positions = begin + jnp.arange(tok_rows, dtype=jnp.int32)
    starts = doc_starts(doc_lengths)
    doc_ids = doc_index(positions, starts)
    prev_id = doc_index(jnp.reshape(begin - 1, (1,)), starts)[0]
    group_heads = HEADS // GROUPS
    y_intra, state_local, entry, transmit = block_terms(
        ssm_x, ssm_b, ssm_c, step_size, decay_rate, doc_ids, prev_id, group_heads
    )
    merged = (transmit, state_local)
    for level_bit in range(DOC_DEVS.bit_length() - 1):
        earlier = passed_along(
            (for_sending(merged[0]), for_sending(merged[1])), "ctx", 1 << level_bit
        )
        merged = chain_states(earlier, merged)
    carried = passed_along(merged[1], "ctx", 1)
    mixed_rows = finish_rows(y_intra, entry, carried, ssm_c, ssm_gate, norm_weight)
    kv_local = keys.shape[1] // ATT_DIM
    q_groups = queries.shape[1] // (kv_local * ATT_DIM)
    query_rows = queries.reshape(tok_rows, kv_local, q_groups, ATT_DIM)
    floor_start = jnp.max(jnp.where(starts <= begin, starts, 0))
    query_last = begin + tok_rows - 1
    carry_shape = (kv_local, q_groups, tok_rows)
    initial = (
        jnp.full(carry_shape, NEG_LARGE, jnp.float32),
        jnp.zeros(carry_shape, jnp.float32),
        jnp.zeros(carry_shape + (ATT_DIM,), jnp.float32),
    )

    def visit(carry, key_block, value_block, key_begin):
        block_rows = key_block.shape[0]
        needed = (key_begin <= query_last) & (key_begin + block_rows - 1 >= floor_start)

        def update(inner):
            key_pos = key_begin + jnp.arange(block_rows, dtype=jnp.int32)
            return attention_update(
                inner, query_rows, key_block, value_block, key_pos, positions, doc_ids, starts
            )

        def unchanged(inner):
            return inner

        return lax.cond(needed, update, unchanged, carry)

    totals = visit(initial, keys, values, begin)
    for hop_count in range(1, DOC_DEVS + 1):
        near_keys, near_values = passed_along((keys, values), "ctx", hop_count)
        totals = visit(totals, near_keys, near_values, begin - hop_count * tok_rows)
    final_out = totals[2] / totals[1][..., None]
    attended_rows = (
        jnp.transpose(final_out, (2, 0, 1, 3)).reshape(tok_rows, -1).astype(jnp.bfloat16)
    )
    mixed_local, attended_local = (
        lax.all_to_all(mixed_rows, "tp", split_axis=0, concat_axis=1, tiled=True),
        lax.all_to_all(attended_rows, "tp", split_axis=0, concat_axis=1, tiled=True),
    )
    return (mixed_local, attended_local)


LOG2E = 1.4426950408889634
F32 = jnp.float32
BF16 = jnp.bfloat16
MESH_ID = pl.DeviceIdType.MESH
COLS_LAST = (((1,), (1,)), ((), ()))
ROWS_FIRST = (((0,), (0,)), ((), ()))
PIECE = 128
HEADS_AT_ONCE = 2
MERGE_AFTER = (3, 5)
PASS_AFTER = (7,)


def dot(a, b, dims=(((1,), (0,)), ((), ())), precision=None):
    return lax.dot_general(a, b, dims, precision=precision, preferred_element_type=F32)


def spread_heads(columns, head, head_size):
    lane = lax.broadcasted_iota(jnp.int32, (columns.shape[0], 128), 1)
    wide = jnp.broadcast_to(columns[:, head : head + 1], lane.shape)
    for k in range(1, 128 // head_size):
        wide = jnp.where(lane >= k * head_size, columns[:, head + k : head + k + 1], wide)
    return wide


def pair_kernel(
    n,
    lengths,
    x_in,
    gate_in,
    b_in,
    c_in,
    step_in,
    q_in,
    k_in,
    v_in,
    rate_ref,
    weight_ref,
    raw_out,
    sums_out,
    attended_out,
    x_s,
    gate_s,
    b_s,
    c_s,
    step_s,
    q_s,
    kv_s,
    own_s,
    beside_s,
    merged_s,
    behind_s,
    passed_s,
    second_s,
    t_own,
    t_beside,
    coef_s,
    loan_s,
    y_s,
    raw_s,
    sums_s,
    attended_s,
    bias_s,
    l_s,
    lt_s,
    dtt_s,
    tail_s,
    entry_s,
    send_sem,
    recv_sem,
    own_sem,
):
    index = lax.axis_index("ctx")
    tp = lax.axis_index("tp")
    parity, pair = lax.rem(index, 2), lax.div(index, 2)
    odd = lax.rem(pair, 2)
    base = index - parity
    other = 1 - parity
    tok = x_in.shape[0]
    rows = 2 * tok
    width = x_s.shape[1]
    group_heads = HEADS // GROUPS
    heads = step_in.shape[0] // 2
    groups = heads // group_heads
    group_width = width // groups
    state = b_s.shape[1] // groups
    head_size = width // heads
    kv_width = kv_s.shape[2]
    kv_heads = kv_width // ATT_DIM
    q_width = q_s.shape[1] // kv_heads
    pieces = group_width // PIECE
    group_of = (odd, 1 - odd)

    core_peer = (base + other, tp)
    tp_peer = (index, 1 - tp)
    cross_peer = (base + other, 1 - tp)
    beside = (index + 2 - 4 * odd, tp)
    barrier = pltpu.get_barrier_semaphore()
    ahead, behind = base + 4 < n, base >= 4
    fed = (odd == 1) | behind
    feeds = (odd == 0) | behind
    greeted = jnp.int32(3)

    def greet(peer):
        pl.semaphore_signal(barrier, inc=1, device_id=peer, device_id_type=MESH_ID)

    for step in (2, 4, -2, -4):
        there = (base + step >= 0) & (base + step < n)
        greeted += 2 * there.astype(jnp.int32)

        @pl.when(there)
        def _():
            for core in range(2):
                greet((base + step + core, tp))

    for peer in (core_peer, tp_peer, cross_peer):
        greet(peer)

    used = [0, 0, 0]

    def slots(kind, count=1):
        used[kind] += count
        return used[kind] - count

    def remote(src, dst, peer, send, recv):
        return pltpu.make_async_remote_copy(
            src_ref=src,
            dst_ref=dst,
            send_sem=send_sem.at[send],
            recv_sem=recv_sem.at[recv],
            device_id=peer,
            device_id_type=MESH_ID,
        )

    at_mine = pl.multiple_of(parity * tok, tok)
    mine = pl.ds(at_mine, tok)

    trade_send, trade_own = slots(0), slots(2)
    step_send, step_own = slots(0), slots(2)

    def trade(moves, whole, recv, send=trade_send, own=trade_own):
        for give, keep, place in moves:
            pltpu.make_async_copy(keep, place, own_sem.at[own]).start()

        def start():
            for give, keep, place in moves:
                remote(give, place, core_peer, send, recv).start()

        def ready():
            remote(whole, whole, core_peer, send, recv).wait_recv()

        return start, ready

    def by_group(src, dst, local_groups):
        size = dst.shape[1] // groups

        def part(core, local):
            at = core * groups * size + group_of[local] * size
            return src.at[:, pl.ds(pl.multiple_of(at, 128), size)]

        moves, first = [], local_groups[0]
        for local in local_groups:
            place = dst.at[mine, local * size : (local + 1) * size]
            moves.append((part(other, local), part(parity, local), place))
        whole = dst.at[:tok, first * size : (first + len(local_groups)) * size]
        return trade(moves, whole, slots(1))

    def part_of(src, core, begin, size, total):
        return src.at[:, pl.ds(pl.multiple_of(core * total + begin, 128), size)]

    @pl.when(pair < 2)
    def _():
        kv_s[:, :rows, :] = jnp.zeros((2, rows, kv_width), BF16)

    @pl.when(pair < 1)
    def _():
        kv_s[:, rows : 2 * rows, :] = jnp.zeros((2, rows, kv_width), BF16)
        second_s[...] = jnp.zeros_like(second_s)

    @pl.when((odd == 0) & jnp.logical_not(ahead))
    def _():
        beside_s[...] = jnp.zeros_like(beside_s)

    near_send, far_send = slots(0), slots(0)
    near_recv = [slots(1) for head in range(kv_heads)]
    far_recv = [slots(1) for head in range(kv_heads)]
    early = base + 8 < n
    items = []
    for head in range(1, kv_heads):
        items += [(0, head, early), (1, head, early & ((base + 12 < n) | (base < 4)))]
    item_send, loan_recv = slots(0, len(items)), slots(1, len(items))

    def head_cols(head):
        return slice(head * ATT_DIM, (head + 1) * ATT_DIM)

    def send_part(k, head, dst, step, skip, send, recv):
        for core in range(2):
            remote(
                part_of((k_in, v_in)[k], core, head * ATT_DIM, ATT_DIM, kv_width),
                dst.at[pl.ds(at_mine + skip, tok), :],
                (base + step + core, tp),
                send,
                recv,
            ).start()

    def send_near():
        @pl.when(odd == 0)
        def _():
            for head in range(kv_heads):
                for k in range(2):
                    near = kv_s.at[k, :, head_cols(head)]
                    send_part(k, head, near, 2, rows, near_send, near_recv[head])

        @pl.when((odd == 1) & ahead)
        def _():
            for k in range(2):
                near = kv_s.at[k, :, head_cols(0)]
                send_part(k, 0, near, 2, rows, near_send, near_recv[0])

        for j, (k, head, lent) in enumerate(items):

            @pl.when((odd == 1) & lent)
            def _():
                send_part(k, head, loan_s.at[j], -2, 0, item_send + j, loan_recv + j)

    def send_rest():
        for j, (k, head, lent) in enumerate(items):

            @pl.when((odd == 1) & ahead & jnp.logical_not(lent))
            def _():
                near = kv_s.at[k, :, head_cols(head)]
                send_part(k, head, near, 2, rows, item_send + j, near_recv[head])

    def send_far(head):
        @pl.when(ahead)
        def _():
            for k in range(2):
                far = kv_s.at[k, :, head_cols(head)]
                send_part(k, head, far, 4, 0, far_send, far_recv[head])

    def arrived(place, recv):
        remote(place, place, core_peer, far_send, recv).wait_recv()

    def forward():
        for j, (k, head, lent) in enumerate(items):

            @pl.when((odd == 0) & lent)
            def _():
                arrived(loan_s.at[j], loan_recv + j)
                near = kv_s.at[k, rows : 2 * rows, head_cols(head)]
                peer = (index + 4, tp)
                remote(loan_s.at[j], near, peer, item_send + j, near_recv[head]).start()

    def wait_past(head):
        @pl.when(fed)
        def _():
            arrived(kv_s.at[:, rows : 2 * rows, head_cols(head)], near_recv[head])

        @pl.when(behind)
        def _():
            arrived(kv_s.at[:, :rows, head_cols(head)], far_recv[head])

    moves = []
    for local in range(groups):
        place = step_s.at[local * group_heads : (local + 1) * group_heads, mine]

        def step_part(core):
            at = (core * groups + group_of[local]) * group_heads
            return step_in.at[pl.ds(pl.multiple_of(at, 8), group_heads)]

        moves.append((step_part(other), step_part(parity), place))
    start_step, ready_step = trade(moves, step_s.at[:, :tok], slots(1), step_send, step_own)
    start_b, ready_b = by_group(b_in, b_s, tuple(range(groups)))
    trade_x = {local: by_group(x_in, x_s, (local,)) for local in (1, 0)}
    start_c, ready_c = by_group(c_in, c_s, tuple(range(groups)))
    moves = []
    for k, src in enumerate((k_in, v_in)):
        give = part_of(src, other, 0, kv_width, kv_width)
        keep = part_of(src, parity, 0, kv_width, kv_width)
        moves.append((give, keep, kv_s.at[k, pl.ds(at_mine + 2 * rows, tok), :]))
    ready_kvq = slots(1)
    start_kv, _ = trade(moves, kv_s.at[:, :tok, :], ready_kvq)
    q_all = q_s.shape[1]
    give, keep = part_of(q_in, other, 0, q_all, q_all), part_of(q_in, parity, 0, q_all, q_all)
    start_q, _ = trade([(give, keep, q_s.at[mine, :])], q_s.at[:tok, :], ready_kvq)
    start_gate, ready_gate = by_group(gate_in, gate_s, tuple(range(groups)))

    @pl.when(pair < 2)
    def _():
        behind_s[...] = jnp.zeros_like(behind_s)

    begin = pair * rows
    row_at = begin - 2 * rows + lax.broadcasted_iota(jnp.int32, (1, 3 * rows), 1)
    col_at = begin + lax.broadcasted_iota(jnp.int32, (rows, 1), 0)
    row_doc = jnp.zeros_like(row_at) - 1
    col_doc = jnp.zeros_like(col_at) - 1
    begun, prev_id, last_id = jnp.int32(0), jnp.int32(-1), jnp.int32(-1)
    for j in range(lengths.shape[0]):
        row_doc += (row_at >= begun).astype(jnp.int32)
        col_doc += (col_at >= begun).astype(jnp.int32)
        prev_id += (begin - 1 >= begun).astype(jnp.int32)
        last_id += (begin + rows - 1 >= begun).astype(jnp.int32)
        begun = begun + lengths[j]
    bias_s[...] = jnp.where((row_doc == col_doc) & (row_at <= col_at), 0.0, NEG_LARGE)

    pl.semaphore_wait(barrier, greeted)
    send_near()
    start_step()
    start_b()
    send_far(0)
    for local in (1, 0):
        trade_x[local][0]()
    for start in (start_c, start_kv, start_q, start_gate):
        start()

    ready_step()
    pltpu.make_async_copy(step_s.at[:, :tok], step_s.at[:, :tok], own_sem.at[step_own]).wait()
    step_t = jnp.concatenate([step_s[...], jnp.zeros((128 - heads, rows), F32)], axis=0)
    step = step_t.T
    rates = []
    for local in range(groups):
        rate = jnp.zeros((1, group_heads), F32)
        for k in range(2 * groups):
            here = parity * groups + group_of[local] == k
            rate = jnp.where(here, rate_ref[:, k * group_heads : (k + 1) * group_heads], rate)
        rates.append(rate)
    rate = jnp.concatenate(rates + [jnp.zeros((1, 128 - heads), F32)], axis=1)
    at = lax.broadcasted_iota(jnp.int32, (rows, rows), 0)
    to = lax.broadcasted_iota(jnp.int32, (rows, rows), 1)
    lower = (to <= at).astype(BF16)
    left, parts = -(step * rate), []
    for k in range(3):
        parts.append(left.astype(BF16)[:, :heads])
        left = left - left.astype(BF16).astype(F32)
    parts.append(jnp.zeros((rows, 128 - 3 * heads), BF16))
    sums = dot(lower, jnp.concatenate(parts, axis=1))
    lane = lax.broadcasted_iota(jnp.int32, (rows, 128), 1)
    sums = sums + pltpu.roll(sums, 128 - heads, 1) + pltpu.roll(sums, 128 - 2 * heads, 1)
    total_decay = jnp.where(lane < heads, sums, 0.0)
    final_sum = total_decay[rows - 1 :, :]
    l_s[...] = total_decay
    lt_s[...] = total_decay.T
    dtt_s[...] = step_t
    tail_s[...] = jnp.where(col_doc == last_id, jnp.exp(final_sum - total_decay) * step, 0.0)
    entry_s[...] = jnp.where(col_doc == prev_id, jnp.exp(total_decay), 0.0)
    passing = (last_id == prev_id).astype(F32)
    t_own[...] = jnp.broadcast_to(jnp.exp(final_sum) * passing, t_own.shape)
    t_trip = remote(t_own, t_beside, beside, slots(0), slots(1))
    t_trip.start()

    pairs = pieces // 2
    first_send, first_recv = slots(0), slots(1, pairs)
    merge_send, merge_recv = slots(0), slots(1, pairs)
    pass_send, pass_recv = slots(0), slots(1, pairs + 1)

    def two(k):
        return slice(2 * k, 2 * k + 2)

    def first_trip(k):
        src = own_s.at[pieces + 2 * k : pieces + 2 * k + 2]
        return remote(src, beside_s.at[two(k)], beside, first_send, first_recv + k)

    def merge_trip(k):
        src, peer = merged_s.at[two(k)], (index + 4, tp)
        return remote(src, behind_s.at[two(k)], peer, merge_send, merge_recv + k)

    def pass_trip(begin, count):
        span = slice(begin, begin + count)
        recv = pass_recv + (begin // 2 if count == 2 else begin - pieces + pairs + 1)
        return remote(passed_s.at[span], second_s.at[span], beside, pass_send, recv)

    def pass_trips(k):
        if k < pairs - 1:
            return [pass_trip(2 * k, 2)]
        return [pass_trip(2 * k, 1), pass_trip(2 * k + 1, 1)]

    traded = 2 * groups * state // 128 + 2 * width // 128 + q_all // 128 + 2 * kv_width // 128
    traded_ref = y_s.at[: traded * tok * 128 * 2 // (width * 4)]

    per = 128 // head_size
    pltpu.make_async_copy(traded_ref, traded_ref, own_sem.at[trade_own]).wait()
    ready_b()
    for local in (1, 0):
        trade_x[local][1]()
        b_t = b_s[:, local * state : (local + 1) * state].T
        for k in range(local * pieces, (local + 1) * pieces, 2):
            parts = []
            for tile in range(2):
                lead = (k + tile) * PIECE
                wide = spread_heads(tail_s[...], lead // head_size, head_size)
                parts.append((x_s[:, lead : lead + PIECE].astype(F32) * wide).astype(BF16))
            made = dot(b_t, jnp.concatenate(parts, axis=1)).astype(BF16)
            for tile in range(2):
                own_s[k + tile] = made[:, tile * PIECE : (tile + 1) * PIECE]
        if local == 1:

            @pl.when((odd == 0) | ahead)
            def _():
                for k in range(pairs):
                    first_trip(k).start()

    for head in range(1, kv_heads):
        send_far(head)
    send_rest()
    ready_c()
    for g in range(groups):
        proj = slice(g * state, (g + 1) * state)
        inter = dot(c_s[:, proj], b_s[:, proj], COLS_LAST)
        for tile in range(group_width // 128):
            lead = g * group_width + tile * 128
            halves = []
            for r in range(0, rows, tok):
                seen = slice(0, r + tok)
                bias = bias_s[r : r + tok, 2 * rows : 2 * rows + r + tok]
                mixing = []
                for h in range(lead // head_size, lead // head_size + per):
                    spread = l_s[r : r + tok, h : h + 1] - lt_s[h : h + 1, seen]
                    w = jnp.exp(spread + bias) * dtt_s[h : h + 1, seen] * inter[r : r + tok, seen]
                    mixing.append(w.astype(BF16))
                both = dot(jnp.concatenate(mixing, axis=0), x_s[seen, lead : lead + 128])
                whole = both[:tok]
                for k in range(1, per):
                    part = both[k * tok : (k + 1) * tok]
                    whole = jnp.where(lane[:tok] >= k * head_size, part, whole)
                y_s[r : r + tok, lead : lead + 128] = whole

    part_rows = rows // 4
    exits = ((tp_peer, 0, 1), (cross_peer, 1, 1), (core_peer, 1, 0))

    exit_send, exit_recv, exit_own = slots(0), slots(1), slots(2)
    sums_send, sums_recv, sums_own = slots(0), slots(1), slots(2)

    def leave(piece_for, home, send=exit_send, recv=exit_recv, own=exit_own):
        for peer, far_core, far_tp in exits:
            src = piece_for(other if far_core else parity, 1 - tp if far_tp else tp)
            remote(src, home, peer, send, recv).start()
        pltpu.make_async_copy(piece_for(parity, tp), home, own_sem.at[own]).start()

    def settle(thrice, once, send, recv, own):
        remote(thrice, thrice, core_peer, send, recv).wait()
        pltpu.make_async_copy(once, once, own_sem.at[own]).wait()

    def coefficients():
        t_trip.wait_recv()
        even = jnp.broadcast_to(odd == 0, (8, 128))
        row = lax.broadcasted_iota(jnp.int32, (8, 128), 0)
        for k in range(pieces):
            h = k * PIECE // head_size
            ours = spread_heads(t_own[...], h, head_size)
            theirs = spread_heads(t_beside[...], group_heads + h, head_size)
            values = (
                (1.0, ours),
                (theirs, 1.0),
                (1.0, 0.0),
                (ours, 1.0),
                (0.0, 1.0),
                (1.0, theirs),
            )
            table = jnp.zeros((8, 128), F32)
            for j, (if_even, if_odd) in enumerate(values):
                table = jnp.where(row == j, jnp.where(even, if_even, if_odd), table)
            coef_s[:, k * PIECE : (k + 1) * PIECE] = table

    def blend(left, right, k, row):
        cols = slice(k * PIECE, (k + 1) * PIECE)
        total = left[k].astype(F32) * coef_s[row : row + 1, cols]
        total += right[k].astype(F32) * coef_s[row + 1 : row + 2, cols]
        return total.astype(BF16)

    def merge(k):
        pl.when((odd == 1) | ahead)(first_trip(k).wait_recv)
        for j in (2 * k, 2 * k + 1):
            merged_s[j] = blend(beside_s, own_s, j, 0)

        @pl.when(ahead)
        def _():
            merge_trip(k).start()

    def pass_on(k):
        @pl.when(behind)
        def _():
            merge_trip(k).wait_recv()

        @pl.when(feeds)
        def _():
            for j in (2 * k, 2 * k + 1):
                passed_s[j] = blend(own_s, behind_s, j, 2)
            for trip in pass_trips(k):
                trip.start()

    scale = LOG2E * ATT_DIM ** (-0.5)
    kvq = y_s.at[: (2 * kv_width + q_all) * tok * 2 // (width * 4)]
    arrived(kvq, ready_kvq)
    step_no = 0
    for kv_head in range(kv_heads):
        kv_cols = slice(kv_head * ATT_DIM, (kv_head + 1) * ATT_DIM)
        wait_past(kv_head)
        for lead in range(kv_head * q_width, (kv_head + 1) * q_width, HEADS_AT_ONCE * ATT_DIM):
            for r in range(0, rows, tok):
                seen = slice(r, r + 2 * rows + tok)
                asked = jnp.concatenate(
                    [
                        q_s[r : r + tok, lead + h * ATT_DIM : lead + (h + 1) * ATT_DIM]
                        for h in range(HEADS_AT_ONCE)
                    ],
                    axis=0,
                )
                scores = dot(asked, kv_s[0, seen, kv_cols], COLS_LAST)
                bias = bias_s[r : r + tok, seen]
                scores = scores + jnp.concatenate([bias] * HEADS_AT_ONCE, axis=0)
                top = jnp.max(scores, axis=1, keepdims=True)
                probs = jnp.exp2((scores - top) * scale)
                total = jnp.sum(probs, axis=1, keepdims=True)
                summed = dot(probs.astype(BF16), kv_s[1, seen, kv_cols]) / total
                for h in range(HEADS_AT_ONCE):
                    part = summed[h * tok : (h + 1) * tok].astype(BF16)
                    for side in range(2):
                        owned = part[side * part_rows : (side + 1) * part_rows]
                        cols = slice(h * ATT_DIM, (h + 1) * ATT_DIM)
                        attended_s[step_no, r // tok * 2 + side, :, cols] = owned
            size = HEADS_AT_ONCE * ATT_DIM
            at = pl.multiple_of((tp * 2 + parity) * q_all + lead, 128)
            home = attended_out.at[:, pl.ds(at, size)]
            here = attended_s.at[step_no]
            leave(lambda core, side: here.at[core * 2 + side], home)
            if step_no == 0:
                forward()
            for k in range(len(MERGE_AFTER)):
                if MERGE_AFTER[k] == step_no:
                    if k == 0:
                        coefficients()
                    merge(k)
            for k in range(len(PASS_AFTER)):
                if PASS_AFTER[k] == step_no:
                    pass_on(k)
            step_no += 1

    ones = jnp.ones((8, 256), BF16)
    squares = [jnp.zeros((rows, 128), F32)] * groups

    def finish(local, first, count):
        lead = local * group_width + first * PIECE
        ready, fed_by = [], []
        for tile in range(0, count * PIECE, 128):
            cols = slice(lead + tile, lead + tile + 128)
            wide = spread_heads(entry_s[...], cols.start // head_size, head_size)
            z = gate_s[:, cols].astype(F32)
            z = z / (1.0 + jnp.exp(-z))
            ready.append(y_s[:, cols] * z)
            fed_by.append(wide * z)
        if local == 1:
            pl.when(fed)(pass_trip(first, count).wait_recv)
        carried = []
        for k in range(first, first + count):
            carried.append(blend(beside_s, behind_s, k, 4) if local == 0 else second_s[k])
        proj = slice(local * state, (local + 1) * state)
        incoming = dot(c_s[:, proj], jnp.concatenate(carried, axis=1))
        square = squares[local]
        for tile in range(0, count * PIECE, 128):
            cols = slice(lead + tile, lead + tile + 128)
            total = ready[tile // 128] + incoming[:, tile : tile + 128] * fed_by[tile // 128]
            square += total * total
            at = parity * width + group_of[local] * group_width + first * PIECE + tile
            gain = weight_ref[:, pl.ds(pl.multiple_of(at, 128), 128)]
            done = (total * gain).astype(BF16)
            for rank in range(4):
                owned = done[rank * part_rows : (rank + 1) * part_rows]
                raw_s[rank, cols.start // PIECE] = owned
        squares[local] = square
        at = ((tp * 2 + parity) * groups + group_of[local]) * pieces + first
        here = pl.ds(lead // PIECE, count)
        leave(
            lambda core, side: raw_s.at[core * 2 + side, here],
            raw_out.at[pl.ds(at, count)],
        )
        if first + count == pieces:
            here = slice(local * 8, local * 8 + 8)
            high = square.astype(BF16)
            halves = [high, (square - high.astype(F32)).astype(BF16)]
            sums_s[here, :] = dot(ones, jnp.concatenate(halves, axis=1), COLS_LAST)
            at = ((tp * 2 + parity) * groups + group_of[local]) * 8
            home = sums_out.at[pl.ds(pl.multiple_of(at, 8), 8), :]

            def half(core, side):
                return sums_s.at[here, pl.ds(pl.multiple_of(core * tok, tok), tok)]

            leave(half, home, sums_send, sums_recv, sums_own)

    ready_gate()
    merged, passed = len(MERGE_AFTER), len(PASS_AFTER)
    for k in range(pairs):
        while passed <= k:
            pass_on(passed)
            passed += 1
        finish(0, 2 * k, 2)
        while merged < pairs:
            merge(merged)
            merged += 1
    for k in range(pairs - 1):
        finish(1, 2 * k, 2)
    finish(1, pieces - 2, 1)
    finish(1, pieces - 1, 1)

    assert used == [send_sem.shape[0], recv_sem.shape[0], own_sem.shape[0]], used
    t_trip.wait_send()
    remote(traded_ref, traded_ref, core_peer, trade_send, loan_recv).wait_send()
    given = step_s.at[:, :tok]
    remote(given, given, core_peer, step_send, loan_recv).wait_send()
    sent = kv_s.at[:, :rows, :]

    @pl.when(ahead)
    def _():
        remote(sent, sent, core_peer, far_send, loan_recv).wait_send()

    for j, (k, head, lent) in enumerate(items):

        @pl.when(lent | ((odd == 1) & ahead))
        def _():
            remote(loan_s.at[j], loan_s.at[j], core_peer, item_send + j, loan_recv).wait_send()

    @pl.when(odd == 0)
    def _():
        remote(sent, sent, core_peer, near_send, loan_recv).wait_send()

    @pl.when((odd == 1) & ahead)
    def _():
        part = kv_s.at[:, :rows, head_cols(0)]
        remote(part, part, core_peer, near_send, loan_recv).wait_send()

    half = own_s.at[:pieces]
    pl.when((odd == 0) | ahead)(remote(half, half, beside, first_send, first_recv).wait_send)
    pl.when(feeds)(remote(half, half, beside, pass_send, pass_recv).wait_send)

    @pl.when(ahead)
    def _():
        remote(half, half, beside, merge_send, merge_recv).wait_send()

    left = (width + q_all) * part_rows * 2 // (width * 4)
    settle(y_s.at[: 3 * left], y_s.at[:left], exit_send, exit_recv, exit_own)
    left = 8 * groups
    settle(l_s.at[: 3 * left], l_s.at[:left], sums_send, sums_recv, sums_own)


def scale_kernel(raw, sums, attended, mixed_out, attended_out, mixed_s, sem):
    tp = lax.axis_index("tp")
    rows, width = mixed_s.shape
    group_width = width // GROUPS
    copies = []
    for k in range(0, rows, 16):
        part = slice(k, k + 16)
        copy = pltpu.make_async_copy(
            attended.at[part], attended_out.at[part], sem.at[GROUPS + k // 16]
        )
        copy.start()
        copies.append(copy)
    squares = sums[...]
    squares = jnp.concatenate([squares, jnp.zeros((128 - squares.shape[0], 128), F32)], axis=0).T
    squares = jnp.where(tp == 0, squares[:rows], squares[rows:])
    factor = lax.rsqrt(squares * (1.0 / group_width) + 1e-05)
    for g in range(GROUPS):
        for k in range(g * group_width // PIECE, (g + 1) * group_width // PIECE):
            scaled = raw[k].astype(F32) * factor[:, 8 * g : 8 * g + 1]
            mixed_s[:, k * PIECE : (k + 1) * PIECE] = scaled.astype(BF16)
        cols = slice(g * group_width, (g + 1) * group_width)
        copy = pltpu.make_async_copy(mixed_s.at[:, cols], mixed_out.at[:, cols], sem.at[g])
        copy.start()
        copies.append(copy)
    for copy in copies:
        copy.wait()


def local_pair(
    doc_lengths,
    ssm_x,
    ssm_gate,
    ssm_b,
    ssm_c,
    step_size,
    decay_rate,
    norm_weight,
    queries,
    keys,
    values,
):
    tok, width = ssm_x.shape
    rows, half = 2 * tok, width // 2
    groups = step_size.shape[1] * GROUPS // HEADS // 2
    state = ssm_b.shape[1] // (2 * groups)
    kv_half = keys.shape[1] // 2
    q_half = queries.shape[1] // 2
    pieces = half // PIECE
    any_spec = pl.BlockSpec(memory_space=pl.ANY)
    vmem_spec = pl.BlockSpec(memory_space=pltpu.VMEM)
    part = rows // 4
    group_pieces = pieces // groups
    items = 2 * kv_half // ATT_DIM - 2
    step_width = HEADS_AT_ONCE * ATT_DIM
    state_piece = pltpu.VMEM((group_pieces, state, PIECE), BF16)
    scratch = [
        pltpu.VMEM((rows, half), BF16),
        pltpu.VMEM((rows, half), BF16),
        pltpu.VMEM((rows, groups * state), BF16),
        pltpu.VMEM((rows, groups * state), BF16),
        pltpu.VMEM((step_size.shape[1] // 2, rows), F32),
        pltpu.VMEM((rows, q_half), BF16),
        pltpu.VMEM((2, 3 * rows, kv_half), BF16),
        pltpu.VMEM((pieces, state, PIECE), BF16),
        state_piece,
        state_piece,
        state_piece,
        state_piece,
        state_piece,
        pltpu.VMEM((8, 128), F32),
        pltpu.VMEM((8, 128), F32),
        pltpu.VMEM((8, half // groups), F32),
        pltpu.VMEM((items, rows, ATT_DIM), BF16),
        pltpu.VMEM((rows, half), F32),
        pltpu.VMEM((4, pieces, part, PIECE), BF16),
        pltpu.VMEM((8 * groups, rows), F32),
        pltpu.VMEM((q_half // step_width, 4, part, step_width), BF16),
        pltpu.VMEM((rows, 3 * rows), F32),
        pltpu.VMEM((rows, 128), F32),
        pltpu.VMEM((128, rows), F32),
        pltpu.VMEM((128, rows), F32),
        pltpu.VMEM((rows, 128), F32),
        pltpu.VMEM((rows, 128), F32),
        pltpu.SemaphoreType.DMA((10 + items,)),
        pltpu.SemaphoreType.DMA((11 + kv_half // ATT_DIM * 2 + items + 3 * group_pieces // 2,)),
        pltpu.SemaphoreType.DMA((4,)),
    ]
    raw, sums, attended = pl.pallas_call(
        functools.partial(pair_kernel, lax.axis_size("ctx")),
        out_shape=(
            pltpu.VMEM((4 * pieces, part, PIECE), BF16),
            pltpu.VMEM((8 * GROUPS, tok), F32),
            pltpu.VMEM((part, 4 * q_half), BF16),
        ),
        in_specs=[pl.BlockSpec(memory_space=pltpu.SMEM)] + [any_spec] * 8 + [vmem_spec] * 2,
        out_specs=(vmem_spec, vmem_spec, vmem_spec),
        scratch_shapes=scratch,
        compiler_params=pltpu.CompilerParams(collective_id=0, has_side_effects=True),
    )(
        doc_lengths,
        ssm_x,
        ssm_gate,
        ssm_b,
        ssm_c,
        step_size.T,
        queries,
        keys,
        values,
        decay_rate[None, :],
        norm_weight[None, :],
    )
    return pl.pallas_call(
        scale_kernel,
        out_shape=(
            jax.ShapeDtypeStruct((part, 4 * half), BF16),
            jax.ShapeDtypeStruct(attended.shape, BF16),
        ),
        in_specs=[vmem_spec] * 3,
        out_specs=(any_spec, any_spec),
        scratch_shapes=[pltpu.VMEM((part, 4 * half), BF16), pltpu.SemaphoreType.DMA((GROUPS + part // 16,))],
    )(*[pltpu.with_memory_space_constraint(a, pltpu.VMEM) for a in (raw, sums, attended)])


def solution(mesh):
    tp = mesh.shape["tp"]
    paired = tp == 2 and mesh.shape["ctx"] % 4 == 0 and mesh.shape["ctx"] > 4 and GROUPS // tp % 2 == 0
    return jax.shard_map(
        local_pair if paired else local_any,
        mesh=mesh,
        in_specs=(
            P(),
            P("ctx", "tp"),
            P("ctx", "tp"),
            P("ctx", "tp"),
            P("ctx", "tp"),
            P("ctx", "tp"),
            P("tp"),
            P("tp"),
            P("ctx", "tp"),
            P("ctx", "tp"),
            P("ctx", "tp"),
        ),
        out_specs=(P(("ctx", "tp"), None), P(("ctx", "tp"), None)),
        check_vma=False,
    )
```

```python
import functools

import jax
import jax.numpy as jnp
from jax import lax
from jax.experimental import pallas as pl
from jax.experimental.pallas import tpu as pltpu
from jax.sharding import PartitionSpec as P

HEADS = 128
GROUPS = 8
ATT_DIM = 128
DOC_DEVS = 4


NEG_LARGE = -1e30


def for_sending(x):
    return jax.tree.map(lambda a: a.astype(jnp.bfloat16) if a.dtype == jnp.float32 else a, x)


def passed_along(block, axis, distance):
    devices = range(lax.axis_size(axis))
    route = [(i - distance, i) for i in devices if i - distance in devices]
    return lax.ppermute(block, axis, route)


def doc_starts(doc_lengths):
    return jnp.cumsum(doc_lengths) - doc_lengths


def doc_index(positions, starts):
    return jnp.sum((starts[None, :] <= positions[:, None]).astype(jnp.int32), axis=1) - 1


def block_terms(ssm_x, ssm_b, ssm_c, step_size, decay_rate, doc_ids, prev_id, group_heads):
    tok_rows = ssm_x.shape[0]
    head_count = step_size.shape[1]
    group_count = head_count // group_heads
    head_size = ssm_x.shape[1] // head_count
    state_size = ssm_b.shape[1] // group_count
    inputs = ssm_x.reshape(tok_rows, group_count, group_heads, head_size)
    in_proj = ssm_b.reshape(tok_rows, group_count, state_size)
    out_proj = ssm_c.reshape(tok_rows, group_count, state_size)
    log_decay = -(step_size * decay_rate[None, :])
    cumulative = jnp.cumsum(log_decay, axis=0)
    same_doc = doc_ids[:, None] == doc_ids[None, :]
    causal = jnp.arange(tok_rows)[:, None] >= jnp.arange(tok_rows)[None, :]
    allowed = (same_doc & causal)[None]
    spread = cumulative.T[:, :, None] - cumulative.T[:, None, :]
    weights = (
        jnp.where(allowed, jnp.exp(jnp.where(allowed, spread, 0.0)), 0.0) * step_size.T[:, None, :]
    )
    intersection = jnp.einsum("tgn,sgn->gts", out_proj, in_proj, preferred_element_type=jnp.float32)
    mixing = (
        weights.reshape(group_count, group_heads, tok_rows, tok_rows) * intersection[:, None]
    ).astype(jnp.bfloat16)
    y_intra = jnp.einsum("ghts,sghp->tghp", mixing, inputs, preferred_element_type=jnp.float32)
    final_sum = cumulative[-1]
    tail = (
        jnp.exp(final_sum[None, :] - cumulative)
        * step_size
        * (doc_ids == doc_ids[-1]).astype(jnp.float32)[:, None]
    )
    scaled = (
        inputs.astype(jnp.float32) * tail.reshape(tok_rows, group_count, group_heads)[..., None]
    ).astype(jnp.bfloat16)
    state_local = jnp.einsum("sghp,sgn->ghpn", scaled, in_proj, preferred_element_type=jnp.float32)
    entry = jnp.exp(cumulative) * (doc_ids == prev_id).astype(jnp.float32)[:, None]
    transmit = jnp.exp(final_sum) * (doc_ids[-1] == prev_id).astype(jnp.float32)
    return (y_intra, state_local, entry, transmit.reshape(group_count, group_heads))


def finish_rows(y_intra, entry, carried, ssm_c, ssm_gate, norm_weight):
    tok_rows, group_count, group_heads, head_size = y_intra.shape
    out_proj = ssm_c.reshape(tok_rows, group_count, -1).astype(jnp.float32)
    incoming = jnp.einsum("tgn,ghpn->tghp", out_proj, carried, precision=lax.Precision.HIGHEST)
    mixer_out = y_intra + incoming * entry.reshape(tok_rows, group_count, group_heads)[..., None]
    gate_vals = ssm_gate.reshape(tok_rows, group_count, group_heads, head_size).astype(jnp.float32)
    gated = (mixer_out * jax.nn.silu(gate_vals)).reshape(
        tok_rows, group_count, group_heads * head_size
    )
    factor = lax.rsqrt(jnp.mean(gated * gated, axis=2, keepdims=True) + 1e-05)
    return ((gated * factor).reshape(tok_rows, -1) * norm_weight[None, :]).astype(jnp.bfloat16)


def chain_states(earlier, later):
    return (earlier[0] * later[0], later[0][:, :, None, None] * earlier[1] + later[1])


def attention_update(
    carry, query_rows, key_block, value_block, key_pos, query_pos, query_doc, starts
):
    running_max, running_sum, running_acc = carry
    block_rows = key_block.shape[0]
    kv_local = key_block.shape[1] // ATT_DIM
    key_heads = key_block.reshape(block_rows, kv_local, ATT_DIM)
    value_heads = value_block.reshape(block_rows, kv_local, ATT_DIM)
    key_doc = doc_index(key_pos, starts)
    allowed = (query_doc[:, None] == key_doc[None, :]) & (key_pos[None, :] <= query_pos[:, None])
    scores = jnp.einsum(
        "tngd,knd->ngtk", query_rows, key_heads, preferred_element_type=jnp.float32
    ) * ATT_DIM ** (-0.5)
    scores = jnp.where(allowed[None, None], scores, -jnp.inf)
    new_max = jnp.maximum(running_max, jnp.max(scores, axis=3))
    probs = jnp.exp(scores - new_max[..., None])
    factor = jnp.exp(running_max - new_max)
    new_sum = running_sum * factor + jnp.sum(probs, axis=3)
    weighted = jnp.einsum(
        "ngtk,knd->ngtd",
        probs.astype(jnp.bfloat16),
        value_heads,
        preferred_element_type=jnp.float32,
    )
    return (new_max, new_sum, running_acc * factor[..., None] + weighted)


def local_any(
    doc_lengths,
    ssm_x,
    ssm_gate,
    ssm_b,
    ssm_c,
    step_size,
    decay_rate,
    norm_weight,
    queries,
    keys,
    values,
):
    tok_rows = ssm_x.shape[0]
    ctx_index = lax.axis_index("ctx")
    begin = ctx_index * tok_rows
    positions = begin + jnp.arange(tok_rows, dtype=jnp.int32)
    starts = doc_starts(doc_lengths)
    doc_ids = doc_index(positions, starts)
    prev_id = doc_index(jnp.reshape(begin - 1, (1,)), starts)[0]
    group_heads = HEADS // GROUPS
    y_intra, state_local, entry, transmit = block_terms(
        ssm_x, ssm_b, ssm_c, step_size, decay_rate, doc_ids, prev_id, group_heads
    )
    merged = (transmit, state_local)
    for level_bit in range(DOC_DEVS.bit_length() - 1):
        earlier = passed_along(
            (for_sending(merged[0]), for_sending(merged[1])), "ctx", 1 << level_bit
        )
        merged = chain_states(earlier, merged)
    carried = passed_along(merged[1], "ctx", 1)
    mixed_rows = finish_rows(y_intra, entry, carried, ssm_c, ssm_gate, norm_weight)
    kv_local = keys.shape[1] // ATT_DIM
    q_groups = queries.shape[1] // (kv_local * ATT_DIM)
    query_rows = queries.reshape(tok_rows, kv_local, q_groups, ATT_DIM)
    floor_start = jnp.max(jnp.where(starts <= begin, starts, 0))
    query_last = begin + tok_rows - 1
    carry_shape = (kv_local, q_groups, tok_rows)
    initial = (
        jnp.full(carry_shape, NEG_LARGE, jnp.float32),
        jnp.zeros(carry_shape, jnp.float32),
        jnp.zeros(carry_shape + (ATT_DIM,), jnp.float32),
    )

    def visit(carry, key_block, value_block, key_begin):
        block_rows = key_block.shape[0]
        needed = (key_begin <= query_last) & (key_begin + block_rows - 1 >= floor_start)

        def update(inner):
            key_pos = key_begin + jnp.arange(block_rows, dtype=jnp.int32)
            return attention_update(
                inner, query_rows, key_block, value_block, key_pos, positions, doc_ids, starts
            )

        def unchanged(inner):
            return inner

        return lax.cond(needed, update, unchanged, carry)

    totals = visit(initial, keys, values, begin)
    for hop_count in range(1, DOC_DEVS + 1):
        near_keys, near_values = passed_along((keys, values), "ctx", hop_count)
        totals = visit(totals, near_keys, near_values, begin - hop_count * tok_rows)
    final_out = totals[2] / totals[1][..., None]
    attended_rows = (
        jnp.transpose(final_out, (2, 0, 1, 3)).reshape(tok_rows, -1).astype(jnp.bfloat16)
    )
    mixed_local, attended_local = (
        lax.all_to_all(mixed_rows, "tp", split_axis=0, concat_axis=1, tiled=True),
        lax.all_to_all(attended_rows, "tp", split_axis=0, concat_axis=1, tiled=True),
    )
    return (mixed_local, attended_local)


LOG2E = 1.4426950408889634
F32 = jnp.float32
BF16 = jnp.bfloat16
MESH_ID = pl.DeviceIdType.MESH
COLS_LAST = (((1,), (1,)), ((), ()))
ROWS_FIRST = (((0,), (0,)), ((), ()))
PIECE = 128
HEADS_AT_ONCE = 2
MERGE_AFTER = (3, 5)
PASS_AFTER = (7,)


def dot(a, b, dims=(((1,), (0,)), ((), ())), precision=None):
    return lax.dot_general(a, b, dims, precision=precision, preferred_element_type=F32)


def spread_heads(columns, head, head_size):
    lane = lax.broadcasted_iota(jnp.int32, (columns.shape[0], 128), 1)
    wide = jnp.broadcast_to(columns[:, head : head + 1], lane.shape)
    for k in range(1, 128 // head_size):
        wide = jnp.where(lane >= k * head_size, columns[:, head + k : head + k + 1], wide)
    return wide


def pair_kernel(
    n,
    lengths_in,
    x_in,
    gate_in,
    b_in,
    c_in,
    step_in,
    q_in,
    k_in,
    v_in,
    rate_in,
    weight_in,
    raw_out,
    sums_out,
    attended_out,
    x_s,
    gate_s,
    b_s,
    c_s,
    step_s,
    q_s,
    kv_s,
    own_s,
    beside_s,
    merged_s,
    behind_s,
    passed_s,
    second_s,
    t_own,
    t_beside,
    coef_s,
    loan_s,
    lengths,
    rate_ref,
    weight_ref,
    y_s,
    raw_s,
    sums_s,
    attended_s,
    bias_s,
    l_s,
    lt_s,
    dtt_s,
    tail_s,
    entry_s,
    send_sem,
    recv_sem,
    own_sem,
):
    index = lax.axis_index("ctx")
    tp = lax.axis_index("tp")
    parity, pair = lax.rem(index, 2), lax.div(index, 2)
    odd = lax.rem(pair, 2)
    base = index - parity
    other = 1 - parity
    tok = x_in.shape[0]
    rows = 2 * tok
    width = x_s.shape[1]
    group_heads = HEADS // GROUPS
    heads = step_in.shape[0] // 2
    groups = heads // group_heads
    group_width = width // groups
    state = b_s.shape[1] // groups
    head_size = width // heads
    kv_width = kv_s.shape[2]
    kv_heads = kv_width // ATT_DIM
    q_width = q_s.shape[1] // kv_heads
    pieces = group_width // PIECE
    group_of = (odd, 1 - odd)

    core_peer = (base + other, tp)
    tp_peer = (index, 1 - tp)
    cross_peer = (base + other, 1 - tp)
    beside = (index + 2 - 4 * odd, tp)
    barrier = pltpu.get_barrier_semaphore()
    ahead, behind = base + 4 < n, base >= 4
    fed = (odd == 1) | behind
    feeds = (odd == 0) | behind
    greeted = jnp.int32(3)

    def greet(peer):
        pl.semaphore_signal(barrier, inc=1, device_id=peer, device_id_type=MESH_ID)

    for step in (2, 4, -2, -4):
        there = (base + step >= 0) & (base + step < n)
        greeted += 2 * there.astype(jnp.int32)

        @pl.when(there)
        def _():
            for core in range(2):
                greet((base + step + core, tp))

    for peer in (core_peer, tp_peer, cross_peer):
        greet(peer)

    small = ((lengths_in, lengths), (rate_in, rate_ref), (weight_in, weight_ref))
    small = [pltpu.make_async_copy(src, dst, own_sem.at[k]) for k, (src, dst) in enumerate(small)]
    for copy in small:
        copy.start()
    used = [0, 0, len(small)]

    def slots(kind, count=1):
        used[kind] += count
        return used[kind] - count

    def remote(src, dst, peer, send, recv):
        return pltpu.make_async_remote_copy(
            src_ref=src,
            dst_ref=dst,
            send_sem=send_sem.at[send],
            recv_sem=recv_sem.at[recv],
            device_id=peer,
            device_id_type=MESH_ID,
        )

    at_mine = pl.multiple_of(parity * tok, tok)
    mine = pl.ds(at_mine, tok)

    trade_send, trade_own = slots(0), slots(2)
    step_send, step_own = slots(0), slots(2)

    def trade(moves, whole, recv, send=trade_send, own=trade_own):
        for give, keep, place in moves:
            pltpu.make_async_copy(keep, place, own_sem.at[own]).start()

        def start():
            for give, keep, place in moves:
                remote(give, place, core_peer, send, recv).start()

        def ready():
            remote(whole, whole, core_peer, send, recv).wait_recv()

        return start, ready

    def by_group(src, dst, local_groups):
        size = dst.shape[1] // groups

        def part(core, local):
            at = core * groups * size + group_of[local] * size
            return src.at[:, pl.ds(pl.multiple_of(at, 128), size)]

        moves, first = [], local_groups[0]
        for local in local_groups:
            place = dst.at[mine, local * size : (local + 1) * size]
            moves.append((part(other, local), part(parity, local), place))
        whole = dst.at[:tok, first * size : (first + len(local_groups)) * size]
        return trade(moves, whole, slots(1))

    def part_of(src, core, begin, size, total):
        return src.at[:, pl.ds(pl.multiple_of(core * total + begin, 128), size)]

    @pl.when(pair < 2)
    def _():
        kv_s[:, :rows, :] = jnp.zeros((2, rows, kv_width), BF16)

    @pl.when(pair < 1)
    def _():
        kv_s[:, rows : 2 * rows, :] = jnp.zeros((2, rows, kv_width), BF16)
        second_s[...] = jnp.zeros_like(second_s)

    @pl.when((odd == 0) & jnp.logical_not(ahead))
    def _():
        beside_s[...] = jnp.zeros_like(beside_s)

    near_send, far_send = slots(0), slots(0)
    near_recv = [slots(1) for head in range(kv_heads)]
    far_recv = [slots(1) for head in range(kv_heads)]
    early = base + 8 < n
    items = []
    for head in range(1, kv_heads):
        items += [(0, head, early), (1, head, early & ((base + 12 < n) | (base < 4)))]
    item_send, loan_recv = slots(0, len(items)), slots(1, len(items))

    def head_cols(head):
        return slice(head * ATT_DIM, (head + 1) * ATT_DIM)

    def send_part(k, head, dst, step, skip, send, recv):
        for core in range(2):
            remote(
                part_of((k_in, v_in)[k], core, head * ATT_DIM, ATT_DIM, kv_width),
                dst.at[pl.ds(at_mine + skip, tok), :],
                (base + step + core, tp),
                send,
                recv,
            ).start()

    def send_near():
        @pl.when(odd == 0)
        def _():
            for head in range(kv_heads):
                for k in range(2):
                    near = kv_s.at[k, :, head_cols(head)]
                    send_part(k, head, near, 2, rows, near_send, near_recv[head])

        @pl.when((odd == 1) & ahead)
        def _():
            for k in range(2):
                near = kv_s.at[k, :, head_cols(0)]
                send_part(k, 0, near, 2, rows, near_send, near_recv[0])

        for j, (k, head, lent) in enumerate(items):

            @pl.when((odd == 1) & lent)
            def _():
                send_part(k, head, loan_s.at[j], -2, 0, item_send + j, loan_recv + j)

    def send_rest():
        for j, (k, head, lent) in enumerate(items):

            @pl.when((odd == 1) & ahead & jnp.logical_not(lent))
            def _():
                near = kv_s.at[k, :, head_cols(head)]
                send_part(k, head, near, 2, rows, item_send + j, near_recv[head])

    def send_far(head):
        @pl.when(ahead)
        def _():
            for k in range(2):
                far = kv_s.at[k, :, head_cols(head)]
                send_part(k, head, far, 4, 0, far_send, far_recv[head])

    def arrived(place, recv):
        remote(place, place, core_peer, far_send, recv).wait_recv()

    def forward():
        for j, (k, head, lent) in enumerate(items):

            @pl.when((odd == 0) & lent)
            def _():
                arrived(loan_s.at[j], loan_recv + j)
                near = kv_s.at[k, rows : 2 * rows, head_cols(head)]
                peer = (index + 4, tp)
                remote(loan_s.at[j], near, peer, item_send + j, near_recv[head]).start()

    def wait_past(head):
        @pl.when(fed)
        def _():
            arrived(kv_s.at[:, rows : 2 * rows, head_cols(head)], near_recv[head])

        @pl.when(behind)
        def _():
            arrived(kv_s.at[:, :rows, head_cols(head)], far_recv[head])

    moves = []
    for local in range(groups):
        place = step_s.at[local * group_heads : (local + 1) * group_heads, mine]

        def step_part(core):
            at = (core * groups + group_of[local]) * group_heads
            return step_in.at[pl.ds(pl.multiple_of(at, 8), group_heads)]

        moves.append((step_part(other), step_part(parity), place))
    start_step, ready_step = trade(moves, step_s.at[:, :tok], slots(1), step_send, step_own)
    start_b, ready_b = by_group(b_in, b_s, tuple(range(groups)))
    trade_x = {local: by_group(x_in, x_s, (local,)) for local in (1, 0)}
    start_c, ready_c = by_group(c_in, c_s, tuple(range(groups)))
    moves = []
    for k, src in enumerate((k_in, v_in)):
        give = part_of(src, other, 0, kv_width, kv_width)
        keep = part_of(src, parity, 0, kv_width, kv_width)
        moves.append((give, keep, kv_s.at[k, pl.ds(at_mine + 2 * rows, tok), :]))
    ready_kvq = slots(1)
    start_kv, _ = trade(moves, kv_s.at[:, :tok, :], ready_kvq)
    q_all = q_s.shape[1]
    give, keep = part_of(q_in, other, 0, q_all, q_all), part_of(q_in, parity, 0, q_all, q_all)
    start_q, _ = trade([(give, keep, q_s.at[mine, :])], q_s.at[:tok, :], ready_kvq)
    start_gate, ready_gate = by_group(gate_in, gate_s, tuple(range(groups)))

    @pl.when(pair < 2)
    def _():
        behind_s[...] = jnp.zeros_like(behind_s)

    small[0].wait()
    begin = pair * rows
    row_at = begin - 2 * rows + lax.broadcasted_iota(jnp.int32, (1, 3 * rows), 1)
    col_at = begin + lax.broadcasted_iota(jnp.int32, (rows, 1), 0)
    row_doc = jnp.zeros_like(row_at) - 1
    col_doc = jnp.zeros_like(col_at) - 1
    begun, prev_id, last_id = jnp.int32(0), jnp.int32(-1), jnp.int32(-1)
    for j in range(lengths.shape[0]):
        row_doc += (row_at >= begun).astype(jnp.int32)
        col_doc += (col_at >= begun).astype(jnp.int32)
        prev_id += (begin - 1 >= begun).astype(jnp.int32)
        last_id += (begin + rows - 1 >= begun).astype(jnp.int32)
        begun = begun + lengths[j]
    bias_s[...] = jnp.where((row_doc == col_doc) & (row_at <= col_at), 0.0, NEG_LARGE)

    pl.semaphore_wait(barrier, greeted)
    send_near()
    start_step()
    start_b()
    send_far(0)
    for local in (1, 0):
        trade_x[local][0]()
    for start in (start_c, start_kv, start_q, start_gate):
        start()

    small[1].wait()
    small[2].wait()
    ready_step()
    pltpu.make_async_copy(step_s.at[:, :tok], step_s.at[:, :tok], own_sem.at[step_own]).wait()
    step_t = jnp.concatenate([step_s[...], jnp.zeros((128 - heads, rows), F32)], axis=0)
    step = step_t.T
    rates = []
    for local in range(groups):
        rate = jnp.zeros((1, group_heads), F32)
        for k in range(2 * groups):
            here = parity * groups + group_of[local] == k
            rate = jnp.where(here, rate_ref[:, k * group_heads : (k + 1) * group_heads], rate)
        rates.append(rate)
    rate = jnp.concatenate(rates + [jnp.zeros((1, 128 - heads), F32)], axis=1)
    at = lax.broadcasted_iota(jnp.int32, (rows, rows), 0)
    to = lax.broadcasted_iota(jnp.int32, (rows, rows), 1)
    lower = (to <= at).astype(BF16)
    left, parts = -(step * rate), []
    for k in range(3):
        parts.append(left.astype(BF16)[:, :heads])
        left = left - left.astype(BF16).astype(F32)
    parts.append(jnp.zeros((rows, 128 - 3 * heads), BF16))
    sums = dot(lower, jnp.concatenate(parts, axis=1))
    lane = lax.broadcasted_iota(jnp.int32, (rows, 128), 1)
    sums = sums + pltpu.roll(sums, 128 - heads, 1) + pltpu.roll(sums, 128 - 2 * heads, 1)
    total_decay = jnp.where(lane < heads, sums, 0.0)
    final_sum = total_decay[rows - 1 :, :]
    l_s[...] = total_decay
    lt_s[...] = total_decay.T
    dtt_s[...] = step_t
    tail_s[...] = jnp.where(col_doc == last_id, jnp.exp(final_sum - total_decay) * step, 0.0)
    entry_s[...] = jnp.where(col_doc == prev_id, jnp.exp(total_decay), 0.0)
    passing = (last_id == prev_id).astype(F32)
    t_own[...] = jnp.broadcast_to(jnp.exp(final_sum) * passing, t_own.shape)
    t_trip = remote(t_own, t_beside, beside, slots(0), slots(1))
    t_trip.start()

    pairs = pieces // 2
    first_send, first_recv = slots(0), slots(1, pairs)
    merge_send, merge_recv = slots(0), slots(1, pairs)
    pass_send, pass_recv = slots(0), slots(1, pairs + 1)

    def two(k):
        return slice(2 * k, 2 * k + 2)

    def first_trip(k):
        src = own_s.at[pieces + 2 * k : pieces + 2 * k + 2]
        return remote(src, beside_s.at[two(k)], beside, first_send, first_recv + k)

    def merge_trip(k):
        src, peer = merged_s.at[two(k)], (index + 4, tp)
        return remote(src, behind_s.at[two(k)], peer, merge_send, merge_recv + k)

    def pass_trip(begin, count):
        span = slice(begin, begin + count)
        recv = pass_recv + (begin // 2 if count == 2 else begin - pieces + pairs + 1)
        return remote(passed_s.at[span], second_s.at[span], beside, pass_send, recv)

    def pass_trips(k):
        if k < pairs - 1:
            return [pass_trip(2 * k, 2)]
        return [pass_trip(2 * k, 1), pass_trip(2 * k + 1, 1)]

    traded = 2 * groups * state // 128 + 2 * width // 128 + q_all // 128 + 2 * kv_width // 128
    traded_ref = y_s.at[: traded * tok * 128 * 2 // (width * 4)]

    per = 128 // head_size
    pltpu.make_async_copy(traded_ref, traded_ref, own_sem.at[trade_own]).wait()
    ready_b()
    for local in (1, 0):
        trade_x[local][1]()
        b_t = b_s[:, local * state : (local + 1) * state].T
        for k in range(local * pieces, (local + 1) * pieces, 2):
            parts = []
            for tile in range(2):
                lead = (k + tile) * PIECE
                wide = spread_heads(tail_s[...], lead // head_size, head_size)
                parts.append((x_s[:, lead : lead + PIECE].astype(F32) * wide).astype(BF16))
            made = dot(b_t, jnp.concatenate(parts, axis=1)).astype(BF16)
            for tile in range(2):
                own_s[k + tile] = made[:, tile * PIECE : (tile + 1) * PIECE]
        if local == 1:

            @pl.when((odd == 0) | ahead)
            def _():
                for k in range(pairs):
                    first_trip(k).start()

    send_rest()
    for head in range(1, kv_heads):
        send_far(head)
    ready_c()

    def intra():
        for g in range(groups):
            proj = slice(g * state, (g + 1) * state)
            inter = dot(c_s[:, proj], b_s[:, proj], COLS_LAST)
            for tile in range(group_width // 128):
                lead = g * group_width + tile * 128
                halves = []
                for r in range(0, rows, tok):
                    seen = slice(0, r + tok)
                    bias = bias_s[r : r + tok, 2 * rows : 2 * rows + r + tok]
                    mixing = []
                    for h in range(lead // head_size, lead // head_size + per):
                        spread = l_s[r : r + tok, h : h + 1] - lt_s[h : h + 1, seen]
                        w = jnp.exp(spread + bias) * dtt_s[h : h + 1, seen] * inter[r : r + tok, seen]
                        mixing.append(w.astype(BF16))
                    both = dot(jnp.concatenate(mixing, axis=0), x_s[seen, lead : lead + 128])
                    whole = both[:tok]
                    for k in range(1, per):
                        part = both[k * tok : (k + 1) * tok]
                        whole = jnp.where(lane[:tok] >= k * head_size, part, whole)
                    y_s[r : r + tok, lead : lead + 128] = whole

    part_rows = rows // 4
    exits = ((tp_peer, 0, 1), (cross_peer, 1, 1), (core_peer, 1, 0))

    exit_send, exit_recv, exit_own = slots(0), slots(1), slots(2)
    sums_send, sums_recv, sums_own = slots(0), slots(1), slots(2)

    def leave(piece_for, home, send=exit_send, recv=exit_recv, own=exit_own):
        for peer, far_core, far_tp in exits:
            src = piece_for(other if far_core else parity, 1 - tp if far_tp else tp)
            remote(src, home, peer, send, recv).start()
        pltpu.make_async_copy(piece_for(parity, tp), home, own_sem.at[own]).start()

    def settle(thrice, once, send, recv, own):
        remote(thrice, thrice, core_peer, send, recv).wait()
        pltpu.make_async_copy(once, once, own_sem.at[own]).wait()

    def coefficients():
        t_trip.wait_recv()
        even = jnp.broadcast_to(odd == 0, (8, 128))
        row = lax.broadcasted_iota(jnp.int32, (8, 128), 0)
        for k in range(pieces):
            h = k * PIECE // head_size
            ours = spread_heads(t_own[...], h, head_size)
            theirs = spread_heads(t_beside[...], group_heads + h, head_size)
            values = (
                (1.0, ours),
                (theirs, 1.0),
                (1.0, 0.0),
                (ours, 1.0),
                (0.0, 1.0),
                (1.0, theirs),
            )
            table = jnp.zeros((8, 128), F32)
            for j, (if_even, if_odd) in enumerate(values):
                table = jnp.where(row == j, jnp.where(even, if_even, if_odd), table)
            coef_s[:, k * PIECE : (k + 1) * PIECE] = table

    def blend(left, right, k, row):
        cols = slice(k * PIECE, (k + 1) * PIECE)
        total = left[k].astype(F32) * coef_s[row : row + 1, cols]
        total += right[k].astype(F32) * coef_s[row + 1 : row + 2, cols]
        return total.astype(BF16)

    def merge(k):
        pl.when((odd == 1) | ahead)(first_trip(k).wait_recv)
        for j in (2 * k, 2 * k + 1):
            merged_s[j] = blend(beside_s, own_s, j, 0)

        @pl.when(ahead)
        def _():
            merge_trip(k).start()

    def pass_on(k):
        @pl.when(behind)
        def _():
            merge_trip(k).wait_recv()

        @pl.when(feeds)
        def _():
            for j in (2 * k, 2 * k + 1):
                passed_s[j] = blend(own_s, behind_s, j, 2)
            for trip in pass_trips(k):
                trip.start()

    scale = LOG2E * ATT_DIM ** (-0.5)
    kvq = y_s.at[: (2 * kv_width + q_all) * tok * 2 // (width * 4)]
    arrived(kvq, ready_kvq)
    def attend(kv_head):
        step_no = kv_head * q_width // (HEADS_AT_ONCE * ATT_DIM)
        kv_cols = slice(kv_head * ATT_DIM, (kv_head + 1) * ATT_DIM)
        wait_past(kv_head)
        for lead in range(kv_head * q_width, (kv_head + 1) * q_width, HEADS_AT_ONCE * ATT_DIM):
            for r in range(0, rows, tok):
                seen = slice(r, r + 2 * rows + tok)
                asked = jnp.concatenate(
                    [
                        q_s[r : r + tok, lead + h * ATT_DIM : lead + (h + 1) * ATT_DIM]
                        for h in range(HEADS_AT_ONCE)
                    ],
                    axis=0,
                )
                scores = dot(asked, kv_s[0, seen, kv_cols], COLS_LAST)
                bias = bias_s[r : r + tok, seen]
                scores = scores + jnp.concatenate([bias] * HEADS_AT_ONCE, axis=0)
                top = jnp.max(scores, axis=1, keepdims=True)
                probs = jnp.exp2((scores - top) * scale)
                total = jnp.sum(probs, axis=1, keepdims=True)
                summed = dot(probs.astype(BF16), kv_s[1, seen, kv_cols]) / total
                for h in range(HEADS_AT_ONCE):
                    part = summed[h * tok : (h + 1) * tok].astype(BF16)
                    for side in range(2):
                        owned = part[side * part_rows : (side + 1) * part_rows]
                        cols = slice(h * ATT_DIM, (h + 1) * ATT_DIM)
                        attended_s[step_no, r // tok * 2 + side, :, cols] = owned
            size = HEADS_AT_ONCE * ATT_DIM
            at = pl.multiple_of((tp * 2 + parity) * q_all + lead, 128)
            home = attended_out.at[:, pl.ds(at, size)]
            here = attended_s.at[step_no]
            leave(lambda core, side: here.at[core * 2 + side], home)
            if step_no == 0:
                forward()
            for k in range(len(MERGE_AFTER)):
                if MERGE_AFTER[k] == step_no:
                    if k == 0:
                        coefficients()
                    merge(k)
            for k in range(len(PASS_AFTER)):
                if PASS_AFTER[k] == step_no:
                    pass_on(k)
            step_no += 1

    @pl.loop(0, 2)
    def _(turn):
        attend_now = lax.rem(turn + (pair == 0).astype(jnp.int32), 2) == 1
        pl.when(attend_now)(functools.partial(attend, 0))
        pl.when(jnp.logical_not(attend_now))(intra)

    for kv_head in range(1, kv_heads):
        attend(kv_head)

    ones = jnp.ones((8, 256), BF16)
    squares = [jnp.zeros((rows, 128), F32)] * groups

    def finish(local, first, count):
        lead = local * group_width + first * PIECE
        ready, fed_by = [], []
        for tile in range(0, count * PIECE, 128):
            cols = slice(lead + tile, lead + tile + 128)
            wide = spread_heads(entry_s[...], cols.start // head_size, head_size)
            z = gate_s[:, cols].astype(F32)
            z = z / (1.0 + jnp.exp(-z))
            ready.append(y_s[:, cols] * z)
            fed_by.append(wide * z)
        if local == 1:
            pl.when(fed)(pass_trip(first, count).wait_recv)
        carried = []
        for k in range(first, first + count):
            carried.append(blend(beside_s, behind_s, k, 4) if local == 0 else second_s[k])
        proj = slice(local * state, (local + 1) * state)
        incoming = dot(c_s[:, proj], jnp.concatenate(carried, axis=1))
        square = squares[local]
        for tile in range(0, count * PIECE, 128):
            cols = slice(lead + tile, lead + tile + 128)
            total = ready[tile // 128] + incoming[:, tile : tile + 128] * fed_by[tile // 128]
            square += total * total
            at = parity * width + group_of[local] * group_width + first * PIECE + tile
            gain = weight_ref[:, pl.ds(pl.multiple_of(at, 128), 128)]
            done = (total * gain).astype(BF16)
            for rank in range(4):
                owned = done[rank * part_rows : (rank + 1) * part_rows]
                raw_s[rank, cols.start // PIECE] = owned
        squares[local] = square
        at = ((tp * 2 + parity) * groups + group_of[local]) * pieces + first
        here = pl.ds(lead // PIECE, count)
        leave(
            lambda core, side: raw_s.at[core * 2 + side, here],
            raw_out.at[pl.ds(at, count)],
        )
        if first + count == pieces:
            here = slice(local * 8, local * 8 + 8)
            high = square.astype(BF16)
            halves = [high, (square - high.astype(F32)).astype(BF16)]
            sums_s[here, :] = dot(ones, jnp.concatenate(halves, axis=1), COLS_LAST)
            at = ((tp * 2 + parity) * groups + group_of[local]) * 8
            home = sums_out.at[pl.ds(pl.multiple_of(at, 8), 8), :]

            def half(core, side):
                return sums_s.at[here, pl.ds(pl.multiple_of(core * tok, tok), tok)]

            leave(half, home, sums_send, sums_recv, sums_own)

    ready_gate()
    merged, passed = len(MERGE_AFTER), len(PASS_AFTER)
    for k in range(pairs):
        if k == 2:
            finish(1, 0, 2)
        while passed <= k:
            pass_on(passed)
            passed += 1
        finish(0, 2 * k, 2)
        while merged < pairs:
            merge(merged)
            merged += 1
    for k in range(1, pairs - 1):
        finish(1, 2 * k, 2)
    finish(1, pieces - 2, 1)
    finish(1, pieces - 1, 1)

    assert used == [send_sem.shape[0], recv_sem.shape[0], own_sem.shape[0]], used
    t_trip.wait_send()
    remote(traded_ref, traded_ref, core_peer, trade_send, loan_recv).wait_send()
    given = step_s.at[:, :tok]
    remote(given, given, core_peer, step_send, loan_recv).wait_send()
    sent = kv_s.at[:, :rows, :]

    @pl.when(ahead)
    def _():
        remote(sent, sent, core_peer, far_send, loan_recv).wait_send()

    for j, (k, head, lent) in enumerate(items):

        @pl.when(lent | ((odd == 1) & ahead))
        def _():
            remote(loan_s.at[j], loan_s.at[j], core_peer, item_send + j, loan_recv).wait_send()

    @pl.when(odd == 0)
    def _():
        remote(sent, sent, core_peer, near_send, loan_recv).wait_send()

    @pl.when((odd == 1) & ahead)
    def _():
        part = kv_s.at[:, :rows, head_cols(0)]
        remote(part, part, core_peer, near_send, loan_recv).wait_send()

    half = own_s.at[:pieces]
    pl.when((odd == 0) | ahead)(remote(half, half, beside, first_send, first_recv).wait_send)
    pl.when(feeds)(remote(half, half, beside, pass_send, pass_recv).wait_send)

    @pl.when(ahead)
    def _():
        remote(half, half, beside, merge_send, merge_recv).wait_send()

    left = (width + q_all) * part_rows * 2 // (width * 4)
    settle(y_s.at[: 3 * left], y_s.at[:left], exit_send, exit_recv, exit_own)
    left = 8 * groups
    settle(l_s.at[: 3 * left], l_s.at[:left], sums_send, sums_recv, sums_own)


def scale_kernel(raw, sums, attended, mixed_out, attended_out, mixed_s, sem):
    tp = lax.axis_index("tp")
    rows, width = mixed_s.shape
    group_width = width // GROUPS
    copies = []
    for k in range(0, rows, 16):
        part = slice(k, k + 16)
        copy = pltpu.make_async_copy(
            attended.at[part], attended_out.at[part], sem.at[GROUPS + k // 16]
        )
        copy.start()
        copies.append(copy)
    squares = sums[...]
    squares = jnp.concatenate([squares, jnp.zeros((128 - squares.shape[0], 128), F32)], axis=0).T
    squares = jnp.where(tp == 0, squares[:rows], squares[rows:])
    factor = lax.rsqrt(squares * (1.0 / group_width) + 1e-05)
    for g in range(GROUPS):
        for k in range(g * group_width // PIECE, (g + 1) * group_width // PIECE):
            scaled = raw[k].astype(F32) * factor[:, 8 * g : 8 * g + 1]
            mixed_s[:, k * PIECE : (k + 1) * PIECE] = scaled.astype(BF16)
        cols = slice(g * group_width, (g + 1) * group_width)
        copy = pltpu.make_async_copy(mixed_s.at[:, cols], mixed_out.at[:, cols], sem.at[g])
        copy.start()
        copies.append(copy)
    for copy in copies:
        copy.wait()


def local_pair(
    doc_lengths,
    ssm_x,
    ssm_gate,
    ssm_b,
    ssm_c,
    step_size,
    decay_rate,
    norm_weight,
    queries,
    keys,
    values,
):
    tok, width = ssm_x.shape
    rows, half = 2 * tok, width // 2
    groups = step_size.shape[1] * GROUPS // HEADS // 2
    state = ssm_b.shape[1] // (2 * groups)
    kv_half = keys.shape[1] // 2
    q_half = queries.shape[1] // 2
    pieces = half // PIECE
    any_spec = pl.BlockSpec(memory_space=pl.ANY)
    vmem_spec = pl.BlockSpec(memory_space=pltpu.VMEM)
    part = rows // 4
    group_pieces = pieces // groups
    items = 2 * kv_half // ATT_DIM - 2
    step_width = HEADS_AT_ONCE * ATT_DIM
    state_piece = pltpu.VMEM((group_pieces, state, PIECE), BF16)
    scratch = [
        pltpu.VMEM((rows, half), BF16),
        pltpu.VMEM((rows, half), BF16),
        pltpu.VMEM((rows, groups * state), BF16),
        pltpu.VMEM((rows, groups * state), BF16),
        pltpu.VMEM((step_size.shape[1] // 2, rows), F32),
        pltpu.VMEM((rows, q_half), BF16),
        pltpu.VMEM((2, 3 * rows, kv_half), BF16),
        pltpu.VMEM((pieces, state, PIECE), BF16),
        state_piece,
        state_piece,
        state_piece,
        state_piece,
        state_piece,
        pltpu.VMEM((8, 128), F32),
        pltpu.VMEM((8, 128), F32),
        pltpu.VMEM((8, half // groups), F32),
        pltpu.VMEM((items, rows, ATT_DIM), BF16),
        pltpu.SMEM(doc_lengths.shape, jnp.int32),
        pltpu.VMEM((1, decay_rate.shape[0]), F32),
        pltpu.VMEM((1, norm_weight.shape[0]), F32),
        pltpu.VMEM((rows, half), F32),
        pltpu.VMEM((4, pieces, part, PIECE), BF16),
        pltpu.VMEM((8 * groups, rows), F32),
        pltpu.VMEM((q_half // step_width, 4, part, step_width), BF16),
        pltpu.VMEM((rows, 3 * rows), F32),
        pltpu.VMEM((rows, 128), F32),
        pltpu.VMEM((128, rows), F32),
        pltpu.VMEM((128, rows), F32),
        pltpu.VMEM((rows, 128), F32),
        pltpu.VMEM((rows, 128), F32),
        pltpu.SemaphoreType.DMA((10 + items,)),
        pltpu.SemaphoreType.DMA((11 + kv_half // ATT_DIM * 2 + items + 3 * group_pieces // 2,)),
        pltpu.SemaphoreType.DMA((7,)),
    ]
    raw, sums, attended = pl.pallas_call(
        functools.partial(pair_kernel, lax.axis_size("ctx")),
        out_shape=(
            pltpu.VMEM((4 * pieces, part, PIECE), BF16),
            pltpu.VMEM((8 * GROUPS, tok), F32),
            pltpu.VMEM((part, 4 * q_half), BF16),
        ),
        in_specs=[any_spec] * 11,
        out_specs=(vmem_spec, vmem_spec, vmem_spec),
        scratch_shapes=scratch,
        compiler_params=pltpu.CompilerParams(collective_id=0, has_side_effects=True),
    )(
        doc_lengths,
        ssm_x,
        ssm_gate,
        ssm_b,
        ssm_c,
        step_size.T,
        queries,
        keys,
        values,
        decay_rate[None, :],
        norm_weight[None, :],
    )
    return pl.pallas_call(
        scale_kernel,
        out_shape=(
            jax.ShapeDtypeStruct((part, 4 * half), BF16),
            jax.ShapeDtypeStruct(attended.shape, BF16),
        ),
        in_specs=[vmem_spec] * 3,
        out_specs=(any_spec, any_spec),
        scratch_shapes=[pltpu.VMEM((part, 4 * half), BF16), pltpu.SemaphoreType.DMA((GROUPS + part // 16,))],
    )(*[pltpu.with_memory_space_constraint(a, pltpu.VMEM) for a in (raw, sums, attended)])


def solution(mesh):
    tp = mesh.shape["tp"]
    paired = tp == 2 and mesh.shape["ctx"] % 4 == 0 and mesh.shape["ctx"] > 4 and GROUPS // tp % 2 == 0
    return jax.shard_map(
        local_pair if paired else local_any,
        mesh=mesh,
        in_specs=(
            P(),
            P("ctx", "tp"),
            P("ctx", "tp"),
            P("ctx", "tp"),
            P("ctx", "tp"),
            P("ctx", "tp"),
            P("tp"),
            P("tp"),
            P("ctx", "tp"),
            P("ctx", "tp"),
            P("ctx", "tp"),
        ),
        out_specs=(P(("ctx", "tp"), None), P(("ctx", "tp"), None)),
        check_vma=False,
    )
```

```python
import functools

import jax
import jax.numpy as jnp
from jax import lax
from jax.experimental import pallas as pl
from jax.experimental.pallas import tpu as pltpu
from jax.sharding import PartitionSpec as P

HEADS = 128
GROUPS = 8
ATT_DIM = 128
DOC_DEVS = 4


NEG_LARGE = -1e30


def for_sending(x):
    return jax.tree.map(lambda a: a.astype(jnp.bfloat16) if a.dtype == jnp.float32 else a, x)


def passed_along(block, axis, distance):
    devices = range(lax.axis_size(axis))
    route = [(i - distance, i) for i in devices if i - distance in devices]
    return lax.ppermute(block, axis, route)


def doc_starts(doc_lengths):
    return jnp.cumsum(doc_lengths) - doc_lengths


def doc_index(positions, starts):
    return jnp.sum((starts[None, :] <= positions[:, None]).astype(jnp.int32), axis=1) - 1


def block_terms(ssm_x, ssm_b, ssm_c, step_size, decay_rate, doc_ids, prev_id, group_heads):
    tok_rows = ssm_x.shape[0]
    head_count = step_size.shape[1]
    group_count = head_count // group_heads
    head_size = ssm_x.shape[1] // head_count
    state_size = ssm_b.shape[1] // group_count
    inputs = ssm_x.reshape(tok_rows, group_count, group_heads, head_size)
    in_proj = ssm_b.reshape(tok_rows, group_count, state_size)
    out_proj = ssm_c.reshape(tok_rows, group_count, state_size)
    log_decay = -(step_size * decay_rate[None, :])
    cumulative = jnp.cumsum(log_decay, axis=0)
    same_doc = doc_ids[:, None] == doc_ids[None, :]
    causal = jnp.arange(tok_rows)[:, None] >= jnp.arange(tok_rows)[None, :]
    allowed = (same_doc & causal)[None]
    spread = cumulative.T[:, :, None] - cumulative.T[:, None, :]
    weights = (
        jnp.where(allowed, jnp.exp(jnp.where(allowed, spread, 0.0)), 0.0) * step_size.T[:, None, :]
    )
    intersection = jnp.einsum("tgn,sgn->gts", out_proj, in_proj, preferred_element_type=jnp.float32)
    mixing = (
        weights.reshape(group_count, group_heads, tok_rows, tok_rows) * intersection[:, None]
    ).astype(jnp.bfloat16)
    y_intra = jnp.einsum("ghts,sghp->tghp", mixing, inputs, preferred_element_type=jnp.float32)
    final_sum = cumulative[-1]
    tail = (
        jnp.exp(final_sum[None, :] - cumulative)
        * step_size
        * (doc_ids == doc_ids[-1]).astype(jnp.float32)[:, None]
    )
    scaled = (
        inputs.astype(jnp.float32) * tail.reshape(tok_rows, group_count, group_heads)[..., None]
    ).astype(jnp.bfloat16)
    state_local = jnp.einsum("sghp,sgn->ghpn", scaled, in_proj, preferred_element_type=jnp.float32)
    entry = jnp.exp(cumulative) * (doc_ids == prev_id).astype(jnp.float32)[:, None]
    transmit = jnp.exp(final_sum) * (doc_ids[-1] == prev_id).astype(jnp.float32)
    return (y_intra, state_local, entry, transmit.reshape(group_count, group_heads))


def finish_rows(y_intra, entry, carried, ssm_c, ssm_gate, norm_weight):
    tok_rows, group_count, group_heads, head_size = y_intra.shape
    out_proj = ssm_c.reshape(tok_rows, group_count, -1).astype(jnp.float32)
    incoming = jnp.einsum("tgn,ghpn->tghp", out_proj, carried, precision=lax.Precision.HIGHEST)
    mixer_out = y_intra + incoming * entry.reshape(tok_rows, group_count, group_heads)[..., None]
    gate_vals = ssm_gate.reshape(tok_rows, group_count, group_heads, head_size).astype(jnp.float32)
    gated = (mixer_out * jax.nn.silu(gate_vals)).reshape(
        tok_rows, group_count, group_heads * head_size
    )
    factor = lax.rsqrt(jnp.mean(gated * gated, axis=2, keepdims=True) + 1e-05)
    return ((gated * factor).reshape(tok_rows, -1) * norm_weight[None, :]).astype(jnp.bfloat16)


def chain_states(earlier, later):
    return (earlier[0] * later[0], later[0][:, :, None, None] * earlier[1] + later[1])


def attention_update(
    carry, query_rows, key_block, value_block, key_pos, query_pos, query_doc, starts
):
    running_max, running_sum, running_acc = carry
    block_rows = key_block.shape[0]
    kv_local = key_block.shape[1] // ATT_DIM
    key_heads = key_block.reshape(block_rows, kv_local, ATT_DIM)
    value_heads = value_block.reshape(block_rows, kv_local, ATT_DIM)
    key_doc = doc_index(key_pos, starts)
    allowed = (query_doc[:, None] == key_doc[None, :]) & (key_pos[None, :] <= query_pos[:, None])
    scores = jnp.einsum(
        "tngd,knd->ngtk", query_rows, key_heads, preferred_element_type=jnp.float32
    ) * ATT_DIM ** (-0.5)
    scores = jnp.where(allowed[None, None], scores, -jnp.inf)
    new_max = jnp.maximum(running_max, jnp.max(scores, axis=3))
    probs = jnp.exp(scores - new_max[..., None])
    factor = jnp.exp(running_max - new_max)
    new_sum = running_sum * factor + jnp.sum(probs, axis=3)
    weighted = jnp.einsum(
        "ngtk,knd->ngtd",
        probs.astype(jnp.bfloat16),
        value_heads,
        preferred_element_type=jnp.float32,
    )
    return (new_max, new_sum, running_acc * factor[..., None] + weighted)


def local_any(
    doc_lengths,
    ssm_x,
    ssm_gate,
    ssm_b,
    ssm_c,
    step_size,
    decay_rate,
    norm_weight,
    queries,
    keys,
    values,
):
    tok_rows = ssm_x.shape[0]
    ctx_index = lax.axis_index("ctx")
    begin = ctx_index * tok_rows
    positions = begin + jnp.arange(tok_rows, dtype=jnp.int32)
    starts = doc_starts(doc_lengths)
    doc_ids = doc_index(positions, starts)
    prev_id = doc_index(jnp.reshape(begin - 1, (1,)), starts)[0]
    group_heads = HEADS // GROUPS
    y_intra, state_local, entry, transmit = block_terms(
        ssm_x, ssm_b, ssm_c, step_size, decay_rate, doc_ids, prev_id, group_heads
    )
    merged = (transmit, state_local)
    for level_bit in range(DOC_DEVS.bit_length() - 1):
        earlier = passed_along(
            (for_sending(merged[0]), for_sending(merged[1])), "ctx", 1 << level_bit
        )
        merged = chain_states(earlier, merged)
    carried = passed_along(merged[1], "ctx", 1)
    mixed_rows = finish_rows(y_intra, entry, carried, ssm_c, ssm_gate, norm_weight)
    kv_local = keys.shape[1] // ATT_DIM
    q_groups = queries.shape[1] // (kv_local * ATT_DIM)
    query_rows = queries.reshape(tok_rows, kv_local, q_groups, ATT_DIM)
    floor_start = jnp.max(jnp.where(starts <= begin, starts, 0))
    query_last = begin + tok_rows - 1
    carry_shape = (kv_local, q_groups, tok_rows)
    initial = (
        jnp.full(carry_shape, NEG_LARGE, jnp.float32),
        jnp.zeros(carry_shape, jnp.float32),
        jnp.zeros(carry_shape + (ATT_DIM,), jnp.float32),
    )

    def visit(carry, key_block, value_block, key_begin):
        block_rows = key_block.shape[0]
        needed = (key_begin <= query_last) & (key_begin + block_rows - 1 >= floor_start)

        def update(inner):
            key_pos = key_begin + jnp.arange(block_rows, dtype=jnp.int32)
            return attention_update(
                inner, query_rows, key_block, value_block, key_pos, positions, doc_ids, starts
            )

        def unchanged(inner):
            return inner

        return lax.cond(needed, update, unchanged, carry)

    totals = visit(initial, keys, values, begin)
    for hop_count in range(1, DOC_DEVS + 1):
        near_keys, near_values = passed_along((keys, values), "ctx", hop_count)
        totals = visit(totals, near_keys, near_values, begin - hop_count * tok_rows)
    final_out = totals[2] / totals[1][..., None]
    attended_rows = (
        jnp.transpose(final_out, (2, 0, 1, 3)).reshape(tok_rows, -1).astype(jnp.bfloat16)
    )
    mixed_local, attended_local = (
        lax.all_to_all(mixed_rows, "tp", split_axis=0, concat_axis=1, tiled=True),
        lax.all_to_all(attended_rows, "tp", split_axis=0, concat_axis=1, tiled=True),
    )
    return (mixed_local, attended_local)


LOG2E = 1.4426950408889634
F32 = jnp.float32
BF16 = jnp.bfloat16
MESH_ID = pl.DeviceIdType.MESH
COLS_LAST = (((1,), (1,)), ((), ()))
ROWS_FIRST = (((0,), (0,)), ((), ()))
PIECE = 128
HEADS_AT_ONCE = 2
MERGE_AFTER = (2, 4)
PASS_AFTER = (7,)


def dot(a, b, dims=(((1,), (0,)), ((), ())), precision=None):
    return lax.dot_general(a, b, dims, precision=precision, preferred_element_type=F32)


def spread_heads(columns, head, head_size):
    lane = lax.broadcasted_iota(jnp.int32, (columns.shape[0], 128), 1)
    wide = jnp.broadcast_to(columns[:, head : head + 1], lane.shape)
    for k in range(1, 128 // head_size):
        wide = jnp.where(lane >= k * head_size, columns[:, head + k : head + k + 1], wide)
    return wide


def pair_kernel(
    n,
    lengths_in,
    x_in,
    gate_in,
    b_in,
    c_in,
    step_in,
    q_in,
    k_in,
    v_in,
    rate_in,
    weight_in,
    raw_out,
    sums_out,
    attended_out,
    x_s,
    gate_s,
    b_s,
    c_s,
    step_s,
    q_s,
    kv_s,
    own_s,
    beside_s,
    merged_s,
    behind_s,
    passed_s,
    second_s,
    t_own,
    t_beside,
    coef_s,
    loan_s,
    lengths,
    rate_ref,
    weight_ref,
    y_s,
    raw_s,
    sums_s,
    attended_s,
    bias_s,
    l_s,
    lt_s,
    dtt_s,
    tail_s,
    entry_s,
    send_sem,
    recv_sem,
    own_sem,
):
    index = lax.axis_index("ctx")
    tp = lax.axis_index("tp")
    parity, pair = lax.rem(index, 2), lax.div(index, 2)
    odd = lax.rem(pair, 2)
    base = index - parity
    other = 1 - parity
    tok = x_in.shape[0]
    rows = 2 * tok
    width = x_s.shape[1]
    group_heads = HEADS // GROUPS
    heads = step_in.shape[0] // 2
    groups = heads // group_heads
    group_width = width // groups
    state = b_s.shape[1] // groups
    head_size = width // heads
    kv_width = kv_s.shape[2]
    kv_heads = kv_width // ATT_DIM
    q_width = q_s.shape[1] // kv_heads
    pieces = group_width // PIECE
    group_of = (odd, 1 - odd)

    core_peer = (base + other, tp)
    tp_peer = (index, 1 - tp)
    cross_peer = (base + other, 1 - tp)
    beside = (index + 2 - 4 * odd, tp)
    barrier = pltpu.get_barrier_semaphore()
    ahead, behind = base + 4 < n, base >= 4
    fed = (odd == 1) | behind
    feeds = (odd == 0) | behind
    greeted = jnp.int32(3)

    def greet(peer):
        pl.semaphore_signal(barrier, inc=1, device_id=peer, device_id_type=MESH_ID)

    for step in (2, 4, -2, -4):
        there = (base + step >= 0) & (base + step < n)
        greeted += 2 * there.astype(jnp.int32)

        @pl.when(there)
        def _():
            for core in range(2):
                greet((base + step + core, tp))

    for peer in (core_peer, tp_peer, cross_peer):
        greet(peer)

    small = ((lengths_in, lengths), (rate_in, rate_ref), (weight_in, weight_ref))
    small = [pltpu.make_async_copy(src, dst, own_sem.at[k]) for k, (src, dst) in enumerate(small)]
    for copy in small:
        copy.start()
    used = [0, 0, len(small)]

    def slots(kind, count=1):
        used[kind] += count
        return used[kind] - count

    def remote(src, dst, peer, send, recv):
        return pltpu.make_async_remote_copy(
            src_ref=src,
            dst_ref=dst,
            send_sem=send_sem.at[send],
            recv_sem=recv_sem.at[recv],
            device_id=peer,
            device_id_type=MESH_ID,
        )

    at_mine = pl.multiple_of(parity * tok, tok)
    mine = pl.ds(at_mine, tok)

    trade_send, trade_own = slots(0), slots(2)
    step_send, step_own = slots(0), slots(2)

    def trade(moves, whole, recv, send=trade_send, own=trade_own):
        for give, keep, place in moves:
            pltpu.make_async_copy(keep, place, own_sem.at[own]).start()

        def start():
            for give, keep, place in moves:
                remote(give, place, core_peer, send, recv).start()

        def ready():
            remote(whole, whole, core_peer, send, recv).wait_recv()

        return start, ready

    def by_group(src, dst, local_groups):
        size = dst.shape[1] // groups

        def part(core, local):
            at = core * groups * size + group_of[local] * size
            return src.at[:, pl.ds(pl.multiple_of(at, 128), size)]

        moves, first = [], local_groups[0]
        for local in local_groups:
            place = dst.at[mine, local * size : (local + 1) * size]
            moves.append((part(other, local), part(parity, local), place))
        whole = dst.at[:tok, first * size : (first + len(local_groups)) * size]
        return trade(moves, whole, slots(1))

    def part_of(src, core, begin, size, total):
        return src.at[:, pl.ds(pl.multiple_of(core * total + begin, 128), size)]

    @pl.when(pair < 2)
    def _():
        kv_s[:, :rows, :] = jnp.zeros((2, rows, kv_width), BF16)

    @pl.when(pair < 1)
    def _():
        kv_s[:, rows : 2 * rows, :] = jnp.zeros((2, rows, kv_width), BF16)
        second_s[...] = jnp.zeros_like(second_s)

    @pl.when((odd == 0) & jnp.logical_not(ahead))
    def _():
        beside_s[...] = jnp.zeros_like(beside_s)

    near_send, far_send = slots(0), slots(0)
    near_recv = [slots(1) for head in range(kv_heads)]
    far_recv = [slots(1) for head in range(kv_heads)]
    early = base + 8 < n
    loose = early & ((base + 12 < n) | (base < 4))
    items = []
    for head in range(1, kv_heads):
        items += [(0, head, 0, ahead), (0, head, 1, early)]
        items += [(1, head, 0, loose), (1, head, 1, loose)]
    item_send, loan_recv = slots(0, len(items)), slots(1, len(items))

    def head_cols(head):
        return slice(head * ATT_DIM, (head + 1) * ATT_DIM)

    def send_part(k, head, dst, step, at, send, recv):
        for core in range(2):
            remote(
                part_of((k_in, v_in)[k], core, head * ATT_DIM, ATT_DIM, kv_width),
                dst.at[pl.ds(at, tok), :],
                (base + step + core, tp),
                send,
                recv,
            ).start()

    def send_near():
        @pl.when(odd == 0)
        def _():
            for head in range(kv_heads):
                for k in range(2):
                    near = kv_s.at[k, :, head_cols(head)]
                    send_part(k, head, near, 2, at_mine + rows, near_send, near_recv[head])

        @pl.when((odd == 1) & ahead)
        def _():
            for k in range(2):
                near = kv_s.at[k, :, head_cols(0)]
                send_part(k, 0, near, 2, at_mine + rows, near_send, near_recv[0])

    def send_items(lending):
        for j, (k, head, core, lent) in enumerate(items):
            there = lent if lending else ahead & jnp.logical_not(lent)

            @pl.when((odd == 1) & (parity == core) & there)
            def _():
                if lending:
                    send_part(k, head, loan_s.at[j], -2, 0, item_send + j, loan_recv + j)
                else:
                    near = kv_s.at[k, :, head_cols(head)]
                    send_part(k, head, near, 2, at_mine + rows, item_send + j, near_recv[head])

    def send_far(head):
        @pl.when(ahead)
        def _():
            for k in range(2):
                far = kv_s.at[k, :, head_cols(head)]
                send_part(k, head, far, 4, at_mine, far_send, far_recv[head])

    def arrived(place, recv):
        remote(place, place, core_peer, far_send, recv).wait_recv()

    def forward():
        for j, (k, head, core, lent) in enumerate(items):

            @pl.when((odd == 0) & lent)
            def _():
                arrived(loan_s.at[j], loan_recv + j)
                at = rows + core * tok
                near = kv_s.at[k, at : at + tok, head_cols(head)]
                peer = (index + 4, tp)
                remote(loan_s.at[j], near, peer, item_send + j, near_recv[head]).start()

    def wait_past(head):
        @pl.when(fed)
        def _():
            arrived(kv_s.at[:, rows : 2 * rows, head_cols(head)], near_recv[head])

        @pl.when(behind)
        def _():
            arrived(kv_s.at[:, :rows, head_cols(head)], far_recv[head])

    moves = []
    for local in range(groups):
        place = step_s.at[local * group_heads : (local + 1) * group_heads, mine]

        def step_part(core):
            at = (core * groups + group_of[local]) * group_heads
            return step_in.at[pl.ds(pl.multiple_of(at, 8), group_heads)]

        moves.append((step_part(other), step_part(parity), place))
    start_step, ready_step = trade(moves, step_s.at[:, :tok], slots(1), step_send, step_own)
    start_b, ready_b = by_group(b_in, b_s, tuple(range(groups)))
    trade_x = {local: by_group(x_in, x_s, (local,)) for local in (1, 0)}
    start_c, ready_c = by_group(c_in, c_s, tuple(range(groups)))
    moves = []
    for k, src in enumerate((k_in, v_in)):
        give = part_of(src, other, 0, kv_width, kv_width)
        keep = part_of(src, parity, 0, kv_width, kv_width)
        moves.append((give, keep, kv_s.at[k, pl.ds(at_mine + 2 * rows, tok), :]))
    ready_kvq = slots(1)
    start_kv, _ = trade(moves, kv_s.at[:, :tok, :], ready_kvq)
    q_all = q_s.shape[1]
    give, keep = part_of(q_in, other, 0, q_all, q_all), part_of(q_in, parity, 0, q_all, q_all)
    start_q, _ = trade([(give, keep, q_s.at[mine, :])], q_s.at[:tok, :], ready_kvq)
    start_gate, ready_gate = by_group(gate_in, gate_s, tuple(range(groups)))

    @pl.when(pair < 2)
    def _():
        behind_s[...] = jnp.zeros_like(behind_s)

    small[0].wait()
    begin = pair * rows
    row_at = begin - 2 * rows + lax.broadcasted_iota(jnp.int32, (1, 3 * rows), 1)
    col_at = begin + lax.broadcasted_iota(jnp.int32, (rows, 1), 0)
    row_doc = jnp.zeros_like(row_at) - 1
    col_doc = jnp.zeros_like(col_at) - 1
    begun, prev_id, last_id = jnp.int32(0), jnp.int32(-1), jnp.int32(-1)
    for j in range(lengths.shape[0]):
        row_doc += (row_at >= begun).astype(jnp.int32)
        col_doc += (col_at >= begun).astype(jnp.int32)
        prev_id += (begin - 1 >= begun).astype(jnp.int32)
        last_id += (begin + rows - 1 >= begun).astype(jnp.int32)
        begun = begun + lengths[j]
    bias_s[...] = jnp.where((row_doc == col_doc) & (row_at <= col_at), 0.0, NEG_LARGE)

    pl.semaphore_wait(barrier, greeted)
    send_near()
    send_items(True)
    start_step()
    start_b()
    send_far(0)
    for local in (1, 0):
        trade_x[local][0]()
    for start in (start_c, start_kv, start_q, start_gate):
        start()

    small[1].wait()
    small[2].wait()
    ready_step()
    pltpu.make_async_copy(step_s.at[:, :tok], step_s.at[:, :tok], own_sem.at[step_own]).wait()
    step_t = jnp.concatenate([step_s[...], jnp.zeros((128 - heads, rows), F32)], axis=0)
    step = step_t.T
    rates = []
    for local in range(groups):
        rate = jnp.zeros((1, group_heads), F32)
        for k in range(2 * groups):
            here = parity * groups + group_of[local] == k
            rate = jnp.where(here, rate_ref[:, k * group_heads : (k + 1) * group_heads], rate)
        rates.append(rate)
    rate = jnp.concatenate(rates + [jnp.zeros((1, 128 - heads), F32)], axis=1)
    at = lax.broadcasted_iota(jnp.int32, (rows, rows), 0)
    to = lax.broadcasted_iota(jnp.int32, (rows, rows), 1)
    lower = (to <= at).astype(BF16)
    left, parts = -(step * rate), []
    for k in range(3):
        parts.append(left.astype(BF16)[:, :heads])
        left = left - left.astype(BF16).astype(F32)
    parts.append(jnp.zeros((rows, 128 - 3 * heads), BF16))
    sums = dot(lower, jnp.concatenate(parts, axis=1))
    lane = lax.broadcasted_iota(jnp.int32, (rows, 128), 1)
    sums = sums + pltpu.roll(sums, 128 - heads, 1) + pltpu.roll(sums, 128 - 2 * heads, 1)
    total_decay = jnp.where(lane < heads, sums, 0.0)
    final_sum = total_decay[rows - 1 :, :]
    l_s[...] = total_decay
    lt_s[...] = total_decay.T
    dtt_s[...] = step_t
    tail_s[...] = jnp.where(col_doc == last_id, jnp.exp(final_sum - total_decay) * step, 0.0)
    entry_s[...] = jnp.where(col_doc == prev_id, jnp.exp(total_decay), 0.0)
    passing = (last_id == prev_id).astype(F32)
    t_own[...] = jnp.broadcast_to(jnp.exp(final_sum) * passing, t_own.shape)
    t_trip = remote(t_own, t_beside, beside, slots(0), slots(1))
    t_trip.start()

    pairs = pieces // 2
    first_send, first_recv = slots(0), slots(1, pairs)
    merge_send, merge_recv = slots(0), slots(1, pairs)
    pass_send, pass_recv = slots(0), slots(1, pairs + 1)

    def two(k):
        return slice(2 * k, 2 * k + 2)

    def first_trip(k):
        src = own_s.at[pieces + 2 * k : pieces + 2 * k + 2]
        return remote(src, beside_s.at[two(k)], beside, first_send, first_recv + k)

    def merge_trip(k):
        src, peer = merged_s.at[two(k)], (index + 4, tp)
        return remote(src, behind_s.at[two(k)], peer, merge_send, merge_recv + k)

    def pass_trip(begin, count):
        span = slice(begin, begin + count)
        recv = pass_recv + (begin // 2 if count == 2 else begin - pieces + pairs + 1)
        return remote(passed_s.at[span], second_s.at[span], beside, pass_send, recv)

    def pass_trips(k):
        if k < pairs - 1:
            return [pass_trip(2 * k, 2)]
        return [pass_trip(2 * k, 1), pass_trip(2 * k + 1, 1)]

    traded = 2 * groups * state // 128 + 2 * width // 128 + q_all // 128 + 2 * kv_width // 128
    traded_ref = y_s.at[: traded * tok * 128 * 2 // (width * 4)]

    per = 128 // head_size
    pltpu.make_async_copy(traded_ref, traded_ref, own_sem.at[trade_own]).wait()
    ready_b()
    for local in (1, 0):
        trade_x[local][1]()
        b_t = b_s[:, local * state : (local + 1) * state].T
        for k in range(local * pieces, (local + 1) * pieces, 2):
            parts = []
            for tile in range(2):
                lead = (k + tile) * PIECE
                wide = spread_heads(tail_s[...], lead // head_size, head_size)
                parts.append((x_s[:, lead : lead + PIECE].astype(F32) * wide).astype(BF16))
            made = dot(b_t, jnp.concatenate(parts, axis=1)).astype(BF16)
            for tile in range(2):
                own_s[k + tile] = made[:, tile * PIECE : (tile + 1) * PIECE]
        if local == 1:

            @pl.when((odd == 0) | ahead)
            def _():
                for k in range(pairs):
                    first_trip(k).start()

    send_items(False)
    for head in range(1, kv_heads):
        send_far(head)
    ready_c()

    def intra():
        for g in range(groups):
            proj = slice(g * state, (g + 1) * state)
            inter = dot(c_s[:, proj], b_s[:, proj], COLS_LAST)
            for tile in range(group_width // 128):
                lead = g * group_width + tile * 128
                halves = []
                for r in range(0, rows, tok):
                    seen = slice(0, r + tok)
                    bias = bias_s[r : r + tok, 2 * rows : 2 * rows + r + tok]
                    mixing = []
                    for h in range(lead // head_size, lead // head_size + per):
                        spread = l_s[r : r + tok, h : h + 1] - lt_s[h : h + 1, seen]
                        w = jnp.exp(spread + bias) * dtt_s[h : h + 1, seen] * inter[r : r + tok, seen]
                        mixing.append(w.astype(BF16))
                    both = dot(jnp.concatenate(mixing, axis=0), x_s[seen, lead : lead + 128])
                    whole = both[:tok]
                    for k in range(1, per):
                        part = both[k * tok : (k + 1) * tok]
                        whole = jnp.where(lane[:tok] >= k * head_size, part, whole)
                    y_s[r : r + tok, lead : lead + 128] = whole

    part_rows = rows // 4
    exits = ((tp_peer, 0, 1), (cross_peer, 1, 1), (core_peer, 1, 0))

    exit_send, exit_recv, exit_own = slots(0), slots(1), slots(2)
    sums_send, sums_recv, sums_own = slots(0), slots(1), slots(2)

    def leave(piece_for, home, send=exit_send, recv=exit_recv, own=exit_own):
        for peer, far_core, far_tp in exits:
            src = piece_for(other if far_core else parity, 1 - tp if far_tp else tp)
            remote(src, home, peer, send, recv).start()
        pltpu.make_async_copy(piece_for(parity, tp), home, own_sem.at[own]).start()

    def settle(thrice, once, send, recv, own):
        remote(thrice, thrice, core_peer, send, recv).wait()
        pltpu.make_async_copy(once, once, own_sem.at[own]).wait()

    def coefficients():
        t_trip.wait_recv()
        even = jnp.broadcast_to(odd == 0, (8, 128))
        row = lax.broadcasted_iota(jnp.int32, (8, 128), 0)
        for k in range(pieces):
            h = k * PIECE // head_size
            ours = spread_heads(t_own[...], h, head_size)
            theirs = spread_heads(t_beside[...], group_heads + h, head_size)
            values = (
                (1.0, ours),
                (theirs, 1.0),
                (1.0, 0.0),
                (ours, 1.0),
                (0.0, 1.0),
                (1.0, theirs),
            )
            table = jnp.zeros((8, 128), F32)
            for j, (if_even, if_odd) in enumerate(values):
                table = jnp.where(row == j, jnp.where(even, if_even, if_odd), table)
            coef_s[:, k * PIECE : (k + 1) * PIECE] = table

    def blend(left, right, k, row):
        cols = slice(k * PIECE, (k + 1) * PIECE)
        total = left[k].astype(F32) * coef_s[row : row + 1, cols]
        total += right[k].astype(F32) * coef_s[row + 1 : row + 2, cols]
        return total.astype(BF16)

    def merge(k):
        pl.when((odd == 1) | ahead)(first_trip(k).wait_recv)
        for j in (2 * k, 2 * k + 1):
            merged_s[j] = blend(beside_s, own_s, j, 0)

        @pl.when(ahead)
        def _():
            merge_trip(k).start()

    def pass_on(k):
        @pl.when(behind)
        def _():
            merge_trip(k).wait_recv()

        @pl.when(feeds)
        def _():
            for j in (2 * k, 2 * k + 1):
                passed_s[j] = blend(own_s, behind_s, j, 2)
            for trip in pass_trips(k):
                trip.start()

    scale = LOG2E * ATT_DIM ** (-0.5)
    kvq = y_s.at[: (2 * kv_width + q_all) * tok * 2 // (width * 4)]
    arrived(kvq, ready_kvq)
    def attend_heads(kv_cols, step_no, lead, first, count):
        for r in range(0, rows, tok):
            seen = slice(r, r + 2 * rows + tok)
            asked = []
            for h in range(first, first + count):
                asked.append(q_s[r : r + tok, lead + h * ATT_DIM : lead + (h + 1) * ATT_DIM])
            scores = dot(jnp.concatenate(asked, axis=0), kv_s[0, seen, kv_cols], COLS_LAST)
            scores = scores + jnp.concatenate([bias_s[r : r + tok, seen]] * count, axis=0)
            top = jnp.max(scores, axis=1, keepdims=True)
            probs = jnp.exp2((scores - top) * scale)
            total = jnp.sum(probs, axis=1, keepdims=True)
            summed = dot(probs.astype(BF16), kv_s[1, seen, kv_cols]) / total
            for h in range(count):
                part = summed[h * tok : (h + 1) * tok].astype(BF16)
                for side in range(2):
                    owned = part[side * part_rows : (side + 1) * part_rows]
                    cols = slice((first + h) * ATT_DIM, (first + h + 1) * ATT_DIM)
                    attended_s[step_no, r // tok * 2 + side, :, cols] = owned
        size = count * ATT_DIM
        at = pl.multiple_of((tp * 2 + parity) * q_all + lead + first * ATT_DIM, 128)
        home = attended_out.at[:, pl.ds(at, size)]
        cols = slice(first * ATT_DIM, first * ATT_DIM + size)
        here = attended_s.at[step_no]
        leave(lambda core, side: here.at[core * 2 + side, :, cols], home)

    def attend(kv_head):
        step_no = kv_head * q_width // (HEADS_AT_ONCE * ATT_DIM)
        kv_cols = slice(kv_head * ATT_DIM, (kv_head + 1) * ATT_DIM)
        wait_past(kv_head)
        for lead in range(kv_head * q_width, (kv_head + 1) * q_width, HEADS_AT_ONCE * ATT_DIM):
            attend_heads(kv_cols, step_no, lead, 0, HEADS_AT_ONCE)
            if step_no == 0:
                forward()
            for k in range(len(MERGE_AFTER)):
                if MERGE_AFTER[k] == step_no:
                    if k == 0:
                        coefficients()
                    merge(k)
            for k in range(len(PASS_AFTER)):
                if PASS_AFTER[k] == step_no:
                    pass_on(k)
            step_no += 1

    @pl.loop(0, 2)
    def _(turn):
        attend_now = lax.rem(turn + (pair == 0).astype(jnp.int32), 2) == 1
        pl.when(attend_now)(functools.partial(attend, 0))
        pl.when(jnp.logical_not(attend_now))(intra)

    for kv_head in range(1, kv_heads):
        attend(kv_head)

    ones = jnp.ones((8, 256), BF16)
    squares = [jnp.zeros((rows, 128), F32)] * groups

    def finish(local, first, count):
        lead = local * group_width + first * PIECE
        ready, fed_by = [], []
        for tile in range(0, count * PIECE, 128):
            cols = slice(lead + tile, lead + tile + 128)
            wide = spread_heads(entry_s[...], cols.start // head_size, head_size)
            z = gate_s[:, cols].astype(F32)
            z = z / (1.0 + jnp.exp(-z))
            ready.append(y_s[:, cols] * z)
            fed_by.append(wide * z)
        if local == 1:
            pl.when(fed)(pass_trip(first, count).wait_recv)
        carried = []
        for k in range(first, first + count):
            carried.append(blend(beside_s, behind_s, k, 4) if local == 0 else second_s[k])
        proj = slice(local * state, (local + 1) * state)
        incoming = dot(c_s[:, proj], jnp.concatenate(carried, axis=1))
        square = squares[local]
        for tile in range(0, count * PIECE, 128):
            cols = slice(lead + tile, lead + tile + 128)
            total = ready[tile // 128] + incoming[:, tile : tile + 128] * fed_by[tile // 128]
            square += total * total
            at = parity * width + group_of[local] * group_width + first * PIECE + tile
            gain = weight_ref[:, pl.ds(pl.multiple_of(at, 128), 128)]
            done = (total * gain).astype(BF16)
            for rank in range(4):
                owned = done[rank * part_rows : (rank + 1) * part_rows]
                raw_s[rank, cols.start // PIECE] = owned
        squares[local] = square
        at = ((tp * 2 + parity) * groups + group_of[local]) * pieces + first
        here = pl.ds(lead // PIECE, count)
        leave(
            lambda core, side: raw_s.at[core * 2 + side, here],
            raw_out.at[pl.ds(at, count)],
        )
        if first + count == pieces:
            here = slice(local * 8, local * 8 + 8)
            high = square.astype(BF16)
            halves = [high, (square - high.astype(F32)).astype(BF16)]
            sums_s[here, :] = dot(ones, jnp.concatenate(halves, axis=1), COLS_LAST)
            at = ((tp * 2 + parity) * groups + group_of[local]) * 8
            home = sums_out.at[pl.ds(pl.multiple_of(at, 8), 8), :]

            def half(core, side):
                return sums_s.at[here, pl.ds(pl.multiple_of(core * tok, tok), tok)]

            leave(half, home, sums_send, sums_recv, sums_own)

    ready_gate()
    merged, passed = len(MERGE_AFTER), len(PASS_AFTER)
    for k in range(pairs):
        if k == 2:
            finish(1, 0, 2)
        while passed <= k:
            pass_on(passed)
            passed += 1
        finish(0, 2 * k, 2)
        while merged < pairs:
            merge(merged)
            merged += 1
    for k in range(1, pairs - 1):
        finish(1, 2 * k, 2)
    finish(1, pieces - 2, 1)
    finish(1, pieces - 1, 1)

    assert used == [send_sem.shape[0], recv_sem.shape[0], own_sem.shape[0]], used
    t_trip.wait_send()
    remote(traded_ref, traded_ref, core_peer, trade_send, loan_recv).wait_send()
    given = step_s.at[:, :tok]
    remote(given, given, core_peer, step_send, loan_recv).wait_send()
    sent = kv_s.at[:, :rows, :]

    @pl.when(ahead)
    def _():
        remote(sent, sent, core_peer, far_send, loan_recv).wait_send()

    for j, (k, head, core, lent) in enumerate(items):
        part = kv_s.at[0, :rows, head_cols(0)]
        closing = remote(part, part, core_peer, item_send + j, loan_recv)
        pl.when((odd == 1) & ahead & (parity == core))(closing.wait_send)
        closing = remote(loan_s.at[j], loan_s.at[j], core_peer, item_send + j, loan_recv)
        pl.when((odd == 0) & lent)(closing.wait_send)

    @pl.when(odd == 0)
    def _():
        remote(sent, sent, core_peer, near_send, loan_recv).wait_send()

    @pl.when((odd == 1) & ahead)
    def _():
        part = kv_s.at[:, :rows, head_cols(0)]
        remote(part, part, core_peer, near_send, loan_recv).wait_send()

    half = own_s.at[:pieces]
    pl.when((odd == 0) | ahead)(remote(half, half, beside, first_send, first_recv).wait_send)
    pl.when(feeds)(remote(half, half, beside, pass_send, pass_recv).wait_send)

    @pl.when(ahead)
    def _():
        remote(half, half, beside, merge_send, merge_recv).wait_send()

    left = (width + q_all) * part_rows * 2 // (width * 4)
    settle(y_s.at[: 3 * left], y_s.at[:left], exit_send, exit_recv, exit_own)
    left = 8 * groups
    settle(l_s.at[: 3 * left], l_s.at[:left], sums_send, sums_recv, sums_own)


def scale_kernel(raw, sums, attended, mixed_out, attended_out, mixed_s, sem):
    tp = lax.axis_index("tp")
    rows, width = mixed_s.shape
    group_width = width // GROUPS
    copies = []
    for k in range(0, rows, 16):
        part = slice(k, k + 16)
        copy = pltpu.make_async_copy(
            attended.at[part], attended_out.at[part], sem.at[GROUPS + k // 16]
        )
        copy.start()
        copies.append(copy)
    squares = sums[...]
    squares = jnp.concatenate([squares, jnp.zeros((128 - squares.shape[0], 128), F32)], axis=0).T
    squares = jnp.where(tp == 0, squares[:rows], squares[rows:])
    factor = lax.rsqrt(squares * (1.0 / group_width) + 1e-05)
    for g in range(GROUPS):
        for k in range(g * group_width // PIECE, (g + 1) * group_width // PIECE):
            scaled = raw[k].astype(F32) * factor[:, 8 * g : 8 * g + 1]
            mixed_s[:, k * PIECE : (k + 1) * PIECE] = scaled.astype(BF16)
        cols = slice(g * group_width, (g + 1) * group_width)
        copy = pltpu.make_async_copy(mixed_s.at[:, cols], mixed_out.at[:, cols], sem.at[g])
        copy.start()
        copies.append(copy)
    for copy in copies:
        copy.wait()


def local_pair(
    doc_lengths,
    ssm_x,
    ssm_gate,
    ssm_b,
    ssm_c,
    step_size,
    decay_rate,
    norm_weight,
    queries,
    keys,
    values,
):
    tok, width = ssm_x.shape
    rows, half = 2 * tok, width // 2
    groups = step_size.shape[1] * GROUPS // HEADS // 2
    state = ssm_b.shape[1] // (2 * groups)
    kv_half = keys.shape[1] // 2
    q_half = queries.shape[1] // 2
    pieces = half // PIECE
    any_spec = pl.BlockSpec(memory_space=pl.ANY)
    vmem_spec = pl.BlockSpec(memory_space=pltpu.VMEM)
    part = rows // 4
    group_pieces = pieces // groups
    items = 4 * (kv_half // ATT_DIM - 1)
    step_width = HEADS_AT_ONCE * ATT_DIM
    state_piece = pltpu.VMEM((group_pieces, state, PIECE), BF16)
    scratch = [
        pltpu.VMEM((rows, half), BF16),
        pltpu.VMEM((rows, half), BF16),
        pltpu.VMEM((rows, groups * state), BF16),
        pltpu.VMEM((rows, groups * state), BF16),
        pltpu.VMEM((step_size.shape[1] // 2, rows), F32),
        pltpu.VMEM((rows, q_half), BF16),
        pltpu.VMEM((2, 3 * rows, kv_half), BF16),
        pltpu.VMEM((pieces, state, PIECE), BF16),
        state_piece,
        state_piece,
        state_piece,
        state_piece,
        state_piece,
        pltpu.VMEM((8, 128), F32),
        pltpu.VMEM((8, 128), F32),
        pltpu.VMEM((8, half // groups), F32),
        pltpu.VMEM((items, tok, ATT_DIM), BF16),
        pltpu.SMEM(doc_lengths.shape, jnp.int32),
        pltpu.VMEM((1, decay_rate.shape[0]), F32),
        pltpu.VMEM((1, norm_weight.shape[0]), F32),
        pltpu.VMEM((rows, half), F32),
        pltpu.VMEM((4, pieces, part, PIECE), BF16),
        pltpu.VMEM((8 * groups, rows), F32),
        pltpu.VMEM((q_half // step_width, 4, part, step_width), BF16),
        pltpu.VMEM((rows, 3 * rows), F32),
        pltpu.VMEM((rows, 128), F32),
        pltpu.VMEM((128, rows), F32),
        pltpu.VMEM((128, rows), F32),
        pltpu.VMEM((rows, 128), F32),
        pltpu.VMEM((rows, 128), F32),
        pltpu.SemaphoreType.DMA((10 + items,)),
        pltpu.SemaphoreType.DMA((11 + kv_half // ATT_DIM * 2 + items + 3 * group_pieces // 2,)),
        pltpu.SemaphoreType.DMA((7,)),
    ]
    raw, sums, attended = pl.pallas_call(
        functools.partial(pair_kernel, lax.axis_size("ctx")),
        out_shape=(
            pltpu.VMEM((4 * pieces, part, PIECE), BF16),
            pltpu.VMEM((8 * GROUPS, tok), F32),
            pltpu.VMEM((part, 4 * q_half), BF16),
        ),
        in_specs=[any_spec] * 11,
        out_specs=(vmem_spec, vmem_spec, vmem_spec),
        scratch_shapes=scratch,
        compiler_params=pltpu.CompilerParams(collective_id=0, has_side_effects=True),
    )(
        doc_lengths,
        ssm_x,
        ssm_gate,
        ssm_b,
        ssm_c,
        step_size.T,
        queries,
        keys,
        values,
        decay_rate[None, :],
        norm_weight[None, :],
    )
    return pl.pallas_call(
        scale_kernel,
        out_shape=(
            jax.ShapeDtypeStruct((part, 4 * half), BF16),
            jax.ShapeDtypeStruct(attended.shape, BF16),
        ),
        in_specs=[vmem_spec] * 3,
        out_specs=(any_spec, any_spec),
        scratch_shapes=[pltpu.VMEM((part, 4 * half), BF16), pltpu.SemaphoreType.DMA((GROUPS + part // 16,))],
    )(*[pltpu.with_memory_space_constraint(a, pltpu.VMEM) for a in (raw, sums, attended)])


def solution(mesh):
    tp = mesh.shape["tp"]
    paired = tp == 2 and mesh.shape["ctx"] % 4 == 0 and mesh.shape["ctx"] > 4 and GROUPS // tp % 2 == 0
    return jax.shard_map(
        local_pair if paired else local_any,
        mesh=mesh,
        in_specs=(
            P(),
            P("ctx", "tp"),
            P("ctx", "tp"),
            P("ctx", "tp"),
            P("ctx", "tp"),
            P("ctx", "tp"),
            P("tp"),
            P("tp"),
            P("ctx", "tp"),
            P("ctx", "tp"),
            P("ctx", "tp"),
        ),
        out_specs=(P(("ctx", "tp"), None), P(("ctx", "tp"), None)),
        check_vma=False,
    )
```

```python
import functools

import jax
import jax.numpy as jnp
from jax import lax
from jax.experimental import pallas as pl
from jax.experimental.pallas import tpu as pltpu
from jax.sharding import PartitionSpec as P

HEADS = 128
GROUPS = 8
ATT_DIM = 128
DOC_DEVS = 4


NEG_LARGE = -1e30


def for_sending(x):
    return jax.tree.map(lambda a: a.astype(jnp.bfloat16) if a.dtype == jnp.float32 else a, x)


def passed_along(block, axis, distance):
    devices = range(lax.axis_size(axis))
    route = [(i - distance, i) for i in devices if i - distance in devices]
    return lax.ppermute(block, axis, route)


def doc_starts(doc_lengths):
    return jnp.cumsum(doc_lengths) - doc_lengths


def doc_index(positions, starts):
    return jnp.sum((starts[None, :] <= positions[:, None]).astype(jnp.int32), axis=1) - 1


def block_terms(ssm_x, ssm_b, ssm_c, step_size, decay_rate, doc_ids, prev_id, group_heads):
    tok_rows = ssm_x.shape[0]
    head_count = step_size.shape[1]
    group_count = head_count // group_heads
    head_size = ssm_x.shape[1] // head_count
    state_size = ssm_b.shape[1] // group_count
    inputs = ssm_x.reshape(tok_rows, group_count, group_heads, head_size)
    in_proj = ssm_b.reshape(tok_rows, group_count, state_size)
    out_proj = ssm_c.reshape(tok_rows, group_count, state_size)
    log_decay = -(step_size * decay_rate[None, :])
    cumulative = jnp.cumsum(log_decay, axis=0)
    same_doc = doc_ids[:, None] == doc_ids[None, :]
    causal = jnp.arange(tok_rows)[:, None] >= jnp.arange(tok_rows)[None, :]
    allowed = (same_doc & causal)[None]
    spread = cumulative.T[:, :, None] - cumulative.T[:, None, :]
    weights = (
        jnp.where(allowed, jnp.exp(jnp.where(allowed, spread, 0.0)), 0.0) * step_size.T[:, None, :]
    )
    intersection = jnp.einsum("tgn,sgn->gts", out_proj, in_proj, preferred_element_type=jnp.float32)
    mixing = (
        weights.reshape(group_count, group_heads, tok_rows, tok_rows) * intersection[:, None]
    ).astype(jnp.bfloat16)
    y_intra = jnp.einsum("ghts,sghp->tghp", mixing, inputs, preferred_element_type=jnp.float32)
    final_sum = cumulative[-1]
    tail = (
        jnp.exp(final_sum[None, :] - cumulative)
        * step_size
        * (doc_ids == doc_ids[-1]).astype(jnp.float32)[:, None]
    )
    scaled = (
        inputs.astype(jnp.float32) * tail.reshape(tok_rows, group_count, group_heads)[..., None]
    ).astype(jnp.bfloat16)
    state_local = jnp.einsum("sghp,sgn->ghpn", scaled, in_proj, preferred_element_type=jnp.float32)
    entry = jnp.exp(cumulative) * (doc_ids == prev_id).astype(jnp.float32)[:, None]
    transmit = jnp.exp(final_sum) * (doc_ids[-1] == prev_id).astype(jnp.float32)
    return (y_intra, state_local, entry, transmit.reshape(group_count, group_heads))


def finish_rows(y_intra, entry, carried, ssm_c, ssm_gate, norm_weight):
    tok_rows, group_count, group_heads, head_size = y_intra.shape
    out_proj = ssm_c.reshape(tok_rows, group_count, -1).astype(jnp.float32)
    incoming = jnp.einsum("tgn,ghpn->tghp", out_proj, carried, precision=lax.Precision.HIGHEST)
    mixer_out = y_intra + incoming * entry.reshape(tok_rows, group_count, group_heads)[..., None]
    gate_vals = ssm_gate.reshape(tok_rows, group_count, group_heads, head_size).astype(jnp.float32)
    gated = (mixer_out * jax.nn.silu(gate_vals)).reshape(
        tok_rows, group_count, group_heads * head_size
    )
    factor = lax.rsqrt(jnp.mean(gated * gated, axis=2, keepdims=True) + 1e-05)
    return ((gated * factor).reshape(tok_rows, -1) * norm_weight[None, :]).astype(jnp.bfloat16)


def chain_states(earlier, later):
    return (earlier[0] * later[0], later[0][:, :, None, None] * earlier[1] + later[1])


def attention_update(
    carry, query_rows, key_block, value_block, key_pos, query_pos, query_doc, starts
):
    running_max, running_sum, running_acc = carry
    block_rows = key_block.shape[0]
    kv_local = key_block.shape[1] // ATT_DIM
    key_heads = key_block.reshape(block_rows, kv_local, ATT_DIM)
    value_heads = value_block.reshape(block_rows, kv_local, ATT_DIM)
    key_doc = doc_index(key_pos, starts)
    allowed = (query_doc[:, None] == key_doc[None, :]) & (key_pos[None, :] <= query_pos[:, None])
    scores = jnp.einsum(
        "tngd,knd->ngtk", query_rows, key_heads, preferred_element_type=jnp.float32
    ) * ATT_DIM ** (-0.5)
    scores = jnp.where(allowed[None, None], scores, -jnp.inf)
    new_max = jnp.maximum(running_max, jnp.max(scores, axis=3))
    probs = jnp.exp(scores - new_max[..., None])
    factor = jnp.exp(running_max - new_max)
    new_sum = running_sum * factor + jnp.sum(probs, axis=3)
    weighted = jnp.einsum(
        "ngtk,knd->ngtd",
        probs.astype(jnp.bfloat16),
        value_heads,
        preferred_element_type=jnp.float32,
    )
    return (new_max, new_sum, running_acc * factor[..., None] + weighted)


def local_any(
    doc_lengths,
    ssm_x,
    ssm_gate,
    ssm_b,
    ssm_c,
    step_size,
    decay_rate,
    norm_weight,
    queries,
    keys,
    values,
):
    tok_rows = ssm_x.shape[0]
    ctx_index = lax.axis_index("ctx")
    begin = ctx_index * tok_rows
    positions = begin + jnp.arange(tok_rows, dtype=jnp.int32)
    starts = doc_starts(doc_lengths)
    doc_ids = doc_index(positions, starts)
    prev_id = doc_index(jnp.reshape(begin - 1, (1,)), starts)[0]
    group_heads = HEADS // GROUPS
    y_intra, state_local, entry, transmit = block_terms(
        ssm_x, ssm_b, ssm_c, step_size, decay_rate, doc_ids, prev_id, group_heads
    )
    merged = (transmit, state_local)
    for level_bit in range(DOC_DEVS.bit_length() - 1):
        earlier = passed_along(
            (for_sending(merged[0]), for_sending(merged[1])), "ctx", 1 << level_bit
        )
        merged = chain_states(earlier, merged)
    carried = passed_along(merged[1], "ctx", 1)
    mixed_rows = finish_rows(y_intra, entry, carried, ssm_c, ssm_gate, norm_weight)
    kv_local = keys.shape[1] // ATT_DIM
    q_groups = queries.shape[1] // (kv_local * ATT_DIM)
    query_rows = queries.reshape(tok_rows, kv_local, q_groups, ATT_DIM)
    floor_start = jnp.max(jnp.where(starts <= begin, starts, 0))
    query_last = begin + tok_rows - 1
    carry_shape = (kv_local, q_groups, tok_rows)
    initial = (
        jnp.full(carry_shape, NEG_LARGE, jnp.float32),
        jnp.zeros(carry_shape, jnp.float32),
        jnp.zeros(carry_shape + (ATT_DIM,), jnp.float32),
    )

    def visit(carry, key_block, value_block, key_begin):
        block_rows = key_block.shape[0]
        needed = (key_begin <= query_last) & (key_begin + block_rows - 1 >= floor_start)

        def update(inner):
            key_pos = key_begin + jnp.arange(block_rows, dtype=jnp.int32)
            return attention_update(
                inner, query_rows, key_block, value_block, key_pos, positions, doc_ids, starts
            )

        def unchanged(inner):
            return inner

        return lax.cond(needed, update, unchanged, carry)

    totals = visit(initial, keys, values, begin)
    for hop_count in range(1, DOC_DEVS + 1):
        near_keys, near_values = passed_along((keys, values), "ctx", hop_count)
        totals = visit(totals, near_keys, near_values, begin - hop_count * tok_rows)
    final_out = totals[2] / totals[1][..., None]
    attended_rows = (
        jnp.transpose(final_out, (2, 0, 1, 3)).reshape(tok_rows, -1).astype(jnp.bfloat16)
    )
    mixed_local, attended_local = (
        lax.all_to_all(mixed_rows, "tp", split_axis=0, concat_axis=1, tiled=True),
        lax.all_to_all(attended_rows, "tp", split_axis=0, concat_axis=1, tiled=True),
    )
    return (mixed_local, attended_local)


LOG2E = 1.4426950408889634
F32 = jnp.float32
BF16 = jnp.bfloat16
MESH_ID = pl.DeviceIdType.MESH
COLS_LAST = (((1,), (1,)), ((), ()))
ROWS_FIRST = (((0,), (0,)), ((), ()))
PIECE = 128
HEADS_AT_ONCE = 2
MERGE_AFTER = (2, 4)
PASS_AFTER = (7,)
FIRST_HEAD_ORDER = (
    (0, 0, 1),
    (1, 0, 1),
    (0, 0, 0),
    (0, 1, 1),
    (1, 1, 1),
    (1, 0, 0),
    (0, 1, 0),
    (1, 1, 0),
)


def dot(a, b, dims=(((1,), (0,)), ((), ())), precision=None):
    return lax.dot_general(a, b, dims, precision=precision, preferred_element_type=F32)


def spread_heads(columns, head, head_size):
    lane = lax.broadcasted_iota(jnp.int32, (columns.shape[0], 128), 1)
    wide = jnp.broadcast_to(columns[:, head : head + 1], lane.shape)
    for k in range(1, 128 // head_size):
        wide = jnp.where(lane >= k * head_size, columns[:, head + k : head + k + 1], wide)
    return wide


def pair_kernel(
    n,
    lengths_in,
    x_in,
    gate_in,
    b_in,
    c_in,
    step_in,
    q_in,
    k_in,
    v_in,
    rate_in,
    weight_in,
    raw_out,
    sums_out,
    attended_out,
    x_s,
    gate_s,
    b_s,
    c_s,
    step_s,
    q_s,
    kv_s,
    own_s,
    beside_s,
    merged_s,
    behind_s,
    passed_s,
    second_s,
    t_own,
    t_beside,
    coef_s,
    loan_s,
    lengths,
    rate_ref,
    weight_ref,
    y_s,
    raw_s,
    sums_s,
    attended_s,
    bias_s,
    l_s,
    lt_s,
    dtt_s,
    tail_s,
    entry_s,
    send_sem,
    recv_sem,
    own_sem,
):
    index = lax.axis_index("ctx")
    tp = lax.axis_index("tp")
    parity, pair = lax.rem(index, 2), lax.div(index, 2)
    odd = lax.rem(pair, 2)
    base = index - parity
    other = 1 - parity
    tok = x_in.shape[0]
    rows = 2 * tok
    width = x_s.shape[1]
    group_heads = HEADS // GROUPS
    heads = step_in.shape[0] // 2
    groups = heads // group_heads
    group_width = width // groups
    state = b_s.shape[1] // groups
    head_size = width // heads
    kv_width = kv_s.shape[2]
    kv_heads = kv_width // ATT_DIM
    q_width = q_s.shape[1] // kv_heads
    pieces = group_width // PIECE
    group_of = (odd, 1 - odd)

    core_peer = (base + other, tp)
    tp_peer = (index, 1 - tp)
    cross_peer = (base + other, 1 - tp)
    beside = (index + 2 - 4 * odd, tp)
    barrier = pltpu.get_barrier_semaphore()
    ahead, behind = base + 4 < n, base >= 4
    fed = (odd == 1) | behind
    feeds = (odd == 0) | behind
    greeted = jnp.int32(3)

    def greet(peer):
        pl.semaphore_signal(barrier, inc=1, device_id=peer, device_id_type=MESH_ID)

    for step in (2, 4, -2, -4):
        there = (base + step >= 0) & (base + step < n)
        greeted += 2 * there.astype(jnp.int32)

        @pl.when(there)
        def _():
            for core in range(2):
                greet((base + step + core, tp))

    for peer in (core_peer, tp_peer, cross_peer):
        greet(peer)

    small = ((lengths_in, lengths), (rate_in, rate_ref), (weight_in, weight_ref))
    small = [pltpu.make_async_copy(src, dst, own_sem.at[k]) for k, (src, dst) in enumerate(small)]
    for copy in small:
        copy.start()
    used = [0, 0, len(small)]

    def slots(kind, count=1):
        used[kind] += count
        return used[kind] - count

    def remote(src, dst, peer, send, recv):
        return pltpu.make_async_remote_copy(
            src_ref=src,
            dst_ref=dst,
            send_sem=send_sem.at[send],
            recv_sem=recv_sem.at[recv],
            device_id=peer,
            device_id_type=MESH_ID,
        )

    at_mine = pl.multiple_of(parity * tok, tok)
    mine = pl.ds(at_mine, tok)

    trade_send, trade_own = slots(0), slots(2)
    step_send, step_own = slots(0), slots(2)

    def trade(moves, whole, recv, send=trade_send, own=trade_own):
        for give, keep, place in moves:
            pltpu.make_async_copy(keep, place, own_sem.at[own]).start()

        def start():
            for give, keep, place in moves:
                remote(give, place, core_peer, send, recv).start()

        def ready():
            remote(whole, whole, core_peer, send, recv).wait_recv()

        return start, ready

    def by_group(src, dst, local_groups):
        size = dst.shape[1] // groups

        def part(core, local):
            at = core * groups * size + group_of[local] * size
            return src.at[:, pl.ds(pl.multiple_of(at, 128), size)]

        moves, first = [], local_groups[0]
        for local in local_groups:
            place = dst.at[mine, local * size : (local + 1) * size]
            moves.append((part(other, local), part(parity, local), place))
        whole = dst.at[:tok, first * size : (first + len(local_groups)) * size]
        return trade(moves, whole, slots(1))

    def part_of(src, core, begin, size, total):
        return src.at[:, pl.ds(pl.multiple_of(core * total + begin, 128), size)]

    @pl.when(pair < 2)
    def _():
        kv_s[:, :rows, :] = jnp.zeros((2, rows, kv_width), BF16)

    @pl.when(pair < 1)
    def _():
        kv_s[:, rows : 2 * rows, :] = jnp.zeros((2, rows, kv_width), BF16)
        second_s[...] = jnp.zeros_like(second_s)

    @pl.when((odd == 0) & jnp.logical_not(ahead))
    def _():
        beside_s[...] = jnp.zeros_like(beside_s)

    near_send, far_send = slots(0), slots(0)
    near_recv = [slots(1) for head in range(kv_heads)]
    far_recv = [slots(1) for head in range(kv_heads)]
    early = base + 8 < n
    loose = early & ((base + 12 < n) | (base < 4))
    items = []
    for head in range(1, kv_heads):
        items += [(0, head, 0, ahead), (0, head, 1, early)]
        items += [(1, head, 0, loose), (1, head, 1, loose)]
    item_send, loan_recv = slots(0, len(items)), slots(1, len(items))

    def head_cols(head):
        return slice(head * ATT_DIM, (head + 1) * ATT_DIM)

    def send_part(k, head, dst, step, at, send, recv, cores=(0, 1)):
        for core in cores:
            remote(
                part_of((k_in, v_in)[k], core, head * ATT_DIM, ATT_DIM, kv_width),
                dst.at[pl.ds(at, tok), :],
                (base + step + core, tp),
                send,
                recv,
            ).start()

    def send_near():
        @pl.when(odd == 0)
        def _():
            for head in range(kv_heads):
                for k in range(2):
                    near = kv_s.at[k, :, head_cols(head)]
                    send_part(k, head, near, 2, at_mine + rows, near_send, near_recv[head])

        @pl.when((odd == 1) & ahead)
        def _():
            for k, far, core in FIRST_HEAD_ORDER:
                place = kv_s.at[k, :, head_cols(0)]
                if far:
                    send_part(k, 0, place, 4, at_mine, far_send, far_recv[0], (core,))
                else:
                    send_part(k, 0, place, 2, at_mine + rows, near_send, near_recv[0], (core,))

    def send_items(lending):
        for j, (k, head, core, lent) in enumerate(items):
            there = lent if lending else ahead & jnp.logical_not(lent)

            @pl.when((odd == 1) & (parity == core) & there)
            def _():
                if lending:
                    send_part(k, head, loan_s.at[j], -2, 0, item_send + j, loan_recv + j)
                else:
                    near = kv_s.at[k, :, head_cols(head)]
                    send_part(k, head, near, 2, at_mine + rows, item_send + j, near_recv[head])

    def send_far(head):
        @pl.when(ahead & ((odd == 0) | (head > 0)))
        def _():
            for k in range(2):
                far = kv_s.at[k, :, head_cols(head)]
                send_part(k, head, far, 4, at_mine, far_send, far_recv[head])

    def arrived(place, recv):
        remote(place, place, core_peer, far_send, recv).wait_recv()

    def forward():
        for j, (k, head, core, lent) in enumerate(items):

            @pl.when((odd == 0) & lent)
            def _():
                arrived(loan_s.at[j], loan_recv + j)
                at = rows + core * tok
                near = kv_s.at[k, at : at + tok, head_cols(head)]
                peer = (index + 4, tp)
                remote(loan_s.at[j], near, peer, item_send + j, near_recv[head]).start()

    def wait_past(head):
        @pl.when(fed)
        def _():
            arrived(kv_s.at[:, rows : 2 * rows, head_cols(head)], near_recv[head])

        @pl.when(behind)
        def _():
            arrived(kv_s.at[:, :rows, head_cols(head)], far_recv[head])

    moves = []
    for local in range(groups):
        place = step_s.at[local * group_heads : (local + 1) * group_heads, mine]

        def step_part(core):
            at = (core * groups + group_of[local]) * group_heads
            return step_in.at[pl.ds(pl.multiple_of(at, 8), group_heads)]

        moves.append((step_part(other), step_part(parity), place))
    start_step, ready_step = trade(moves, step_s.at[:, :tok], slots(1), step_send, step_own)
    start_b, ready_b = by_group(b_in, b_s, tuple(range(groups)))
    trade_x = {local: by_group(x_in, x_s, (local,)) for local in (1, 0)}
    start_c, ready_c = by_group(c_in, c_s, tuple(range(groups)))
    moves = []
    for k, src in enumerate((k_in, v_in)):
        give = part_of(src, other, 0, kv_width, kv_width)
        keep = part_of(src, parity, 0, kv_width, kv_width)
        moves.append((give, keep, kv_s.at[k, pl.ds(at_mine + 2 * rows, tok), :]))
    ready_kvq = slots(1)
    start_kv, _ = trade(moves, kv_s.at[:, :tok, :], ready_kvq)
    q_all = q_s.shape[1]
    give, keep = part_of(q_in, other, 0, q_all, q_all), part_of(q_in, parity, 0, q_all, q_all)
    start_q, _ = trade([(give, keep, q_s.at[mine, :])], q_s.at[:tok, :], ready_kvq)
    start_gate, ready_gate = by_group(gate_in, gate_s, tuple(range(groups)))

    @pl.when(pair < 2)
    def _():
        behind_s[...] = jnp.zeros_like(behind_s)

    small[0].wait()
    begin = pair * rows
    row_at = begin - 2 * rows + lax.broadcasted_iota(jnp.int32, (1, 3 * rows), 1)
    col_at = begin + lax.broadcasted_iota(jnp.int32, (rows, 1), 0)
    row_doc = jnp.zeros_like(row_at) - 1
    col_doc = jnp.zeros_like(col_at) - 1
    begun, prev_id, last_id = jnp.int32(0), jnp.int32(-1), jnp.int32(-1)
    for j in range(lengths.shape[0]):
        row_doc += (row_at >= begun).astype(jnp.int32)
        col_doc += (col_at >= begun).astype(jnp.int32)
        prev_id += (begin - 1 >= begun).astype(jnp.int32)
        last_id += (begin + rows - 1 >= begun).astype(jnp.int32)
        begun = begun + lengths[j]
    bias_s[...] = jnp.where((row_doc == col_doc) & (row_at <= col_at), 0.0, NEG_LARGE)

    pl.semaphore_wait(barrier, greeted)
    send_near()
    send_items(True)
    start_step()
    start_b()
    send_far(0)
    for local in (1, 0):
        trade_x[local][0]()
    for start in (start_c, start_kv, start_q, start_gate):
        start()

    small[1].wait()
    small[2].wait()
    ready_step()
    pltpu.make_async_copy(step_s.at[:, :tok], step_s.at[:, :tok], own_sem.at[step_own]).wait()
    step_t = jnp.concatenate([step_s[...], jnp.zeros((128 - heads, rows), F32)], axis=0)
    step = step_t.T
    rates = []
    for local in range(groups):
        rate = jnp.zeros((1, group_heads), F32)
        for k in range(2 * groups):
            here = parity * groups + group_of[local] == k
            rate = jnp.where(here, rate_ref[:, k * group_heads : (k + 1) * group_heads], rate)
        rates.append(rate)
    rate = jnp.concatenate(rates + [jnp.zeros((1, 128 - heads), F32)], axis=1)
    at = lax.broadcasted_iota(jnp.int32, (rows, rows), 0)
    to = lax.broadcasted_iota(jnp.int32, (rows, rows), 1)
    lower = (to <= at).astype(BF16)
    left, parts = -(step * rate), []
    for k in range(3):
        parts.append(left.astype(BF16)[:, :heads])
        left = left - left.astype(BF16).astype(F32)
    parts.append(jnp.zeros((rows, 128 - 3 * heads), BF16))
    sums = dot(lower, jnp.concatenate(parts, axis=1))
    lane = lax.broadcasted_iota(jnp.int32, (rows, 128), 1)
    sums = sums + pltpu.roll(sums, 128 - heads, 1) + pltpu.roll(sums, 128 - 2 * heads, 1)
    total_decay = jnp.where(lane < heads, sums, 0.0)
    final_sum = total_decay[rows - 1 :, :]
    l_s[...] = total_decay
    lt_s[...] = total_decay.T
    dtt_s[...] = step_t
    tail_s[...] = jnp.where(col_doc == last_id, jnp.exp(final_sum - total_decay) * step, 0.0)
    entry_s[...] = jnp.where(col_doc == prev_id, jnp.exp(total_decay), 0.0)
    passing = (last_id == prev_id).astype(F32)
    t_own[...] = jnp.broadcast_to(jnp.exp(final_sum) * passing, t_own.shape)
    t_trip = remote(t_own, t_beside, beside, slots(0), slots(1))
    t_trip.start()

    pairs = pieces // 2
    first_send, first_recv = slots(0), slots(1, pairs)
    merge_send, merge_recv = slots(0), slots(1, pairs)
    pass_send, pass_recv = slots(0), slots(1, pairs + 1)

    def two(k):
        return slice(2 * k, 2 * k + 2)

    def first_trip(k):
        src = own_s.at[pieces + 2 * k : pieces + 2 * k + 2]
        return remote(src, beside_s.at[two(k)], beside, first_send, first_recv + k)

    def merge_trip(k):
        src, peer = merged_s.at[two(k)], (index + 4, tp)
        return remote(src, behind_s.at[two(k)], peer, merge_send, merge_recv + k)

    def pass_trip(begin, count):
        span = slice(begin, begin + count)
        recv = pass_recv + (begin // 2 if count == 2 else begin - pieces + pairs + 1)
        return remote(passed_s.at[span], second_s.at[span], beside, pass_send, recv)

    def pass_trips(k):
        if k < pairs - 1:
            return [pass_trip(2 * k, 2)]
        return [pass_trip(2 * k, 1), pass_trip(2 * k + 1, 1)]

    traded = 2 * groups * state // 128 + 2 * width // 128 + q_all // 128 + 2 * kv_width // 128
    traded_ref = y_s.at[: traded * tok * 128 * 2 // (width * 4)]

    per = 128 // head_size
    pltpu.make_async_copy(traded_ref, traded_ref, own_sem.at[trade_own]).wait()
    ready_b()
    for local in (1, 0):
        trade_x[local][1]()
        b_t = b_s[:, local * state : (local + 1) * state].T
        for k in range(local * pieces, (local + 1) * pieces, 2):
            parts = []
            for tile in range(2):
                lead = (k + tile) * PIECE
                wide = spread_heads(tail_s[...], lead // head_size, head_size)
                parts.append((x_s[:, lead : lead + PIECE].astype(F32) * wide).astype(BF16))
            made = dot(b_t, jnp.concatenate(parts, axis=1)).astype(BF16)
            for tile in range(2):
                own_s[k + tile] = made[:, tile * PIECE : (tile + 1) * PIECE]
        if local == 1:

            @pl.when((odd == 0) | ahead)
            def _():
                for k in range(pairs):
                    first_trip(k).start()

    send_items(False)
    for head in range(1, kv_heads):
        send_far(head)
    ready_c()

    def intra():
        for g in range(groups):
            proj = slice(g * state, (g + 1) * state)
            inter = dot(c_s[:, proj], b_s[:, proj], COLS_LAST)
            for tile in range(group_width // 128):
                lead = g * group_width + tile * 128
                halves = []
                for r in range(0, rows, tok):
                    seen = slice(0, r + tok)
                    bias = bias_s[r : r + tok, 2 * rows : 2 * rows + r + tok]
                    mixing = []
                    for h in range(lead // head_size, lead // head_size + per):
                        spread = l_s[r : r + tok, h : h + 1] - lt_s[h : h + 1, seen]
                        w = jnp.exp(spread + bias) * dtt_s[h : h + 1, seen] * inter[r : r + tok, seen]
                        mixing.append(w.astype(BF16))
                    both = dot(jnp.concatenate(mixing, axis=0), x_s[seen, lead : lead + 128])
                    whole = both[:tok]
                    for k in range(1, per):
                        part = both[k * tok : (k + 1) * tok]
                        whole = jnp.where(lane[:tok] >= k * head_size, part, whole)
                    y_s[r : r + tok, lead : lead + 128] = whole

    part_rows = rows // 4
    exits = ((tp_peer, 0, 1), (cross_peer, 1, 1), (core_peer, 1, 0))

    exit_send, exit_recv, exit_own = slots(0), slots(1), slots(2)
    sums_send, sums_recv, sums_own = slots(0), slots(1), slots(2)

    def leave(piece_for, home, send=exit_send, recv=exit_recv, own=exit_own):
        for peer, far_core, far_tp in exits:
            src = piece_for(other if far_core else parity, 1 - tp if far_tp else tp)
            remote(src, home, peer, send, recv).start()
        pltpu.make_async_copy(piece_for(parity, tp), home, own_sem.at[own]).start()

    def settle(thrice, once, send, recv, own):
        remote(thrice, thrice, core_peer, send, recv).wait()
        pltpu.make_async_copy(once, once, own_sem.at[own]).wait()

    def coefficients():
        t_trip.wait_recv()
        even = jnp.broadcast_to(odd == 0, (8, 128))
        row = lax.broadcasted_iota(jnp.int32, (8, 128), 0)
        for k in range(pieces):
            h = k * PIECE // head_size
            ours = spread_heads(t_own[...], h, head_size)
            theirs = spread_heads(t_beside[...], group_heads + h, head_size)
            values = (
                (1.0, ours),
                (theirs, 1.0),
                (1.0, 0.0),
                (ours, 1.0),
                (0.0, 1.0),
                (1.0, theirs),
            )
            table = jnp.zeros((8, 128), F32)
            for j, (if_even, if_odd) in enumerate(values):
                table = jnp.where(row == j, jnp.where(even, if_even, if_odd), table)
            coef_s[:, k * PIECE : (k + 1) * PIECE] = table

    def blend(left, right, k, row):
        cols = slice(k * PIECE, (k + 1) * PIECE)
        total = left[k].astype(F32) * coef_s[row : row + 1, cols]
        total += right[k].astype(F32) * coef_s[row + 1 : row + 2, cols]
        return total.astype(BF16)

    def merge(k):
        pl.when((odd == 1) | ahead)(first_trip(k).wait_recv)
        for j in (2 * k, 2 * k + 1):
            merged_s[j] = blend(beside_s, own_s, j, 0)

        @pl.when(ahead)
        def _():
            merge_trip(k).start()

    def pass_on(k):
        @pl.when(behind)
        def _():
            merge_trip(k).wait_recv()

        @pl.when(feeds)
        def _():
            for j in (2 * k, 2 * k + 1):
                passed_s[j] = blend(own_s, behind_s, j, 2)
            for trip in pass_trips(k):
                trip.start()

    scale = LOG2E * ATT_DIM ** (-0.5)
    kvq = y_s.at[: (2 * kv_width + q_all) * tok * 2 // (width * 4)]
    arrived(kvq, ready_kvq)
    def attend_heads(kv_cols, step_no, lead, first, count):
        for r in range(0, rows, tok):
            seen = slice(r, r + 2 * rows + tok)
            asked = []
            for h in range(first, first + count):
                asked.append(q_s[r : r + tok, lead + h * ATT_DIM : lead + (h + 1) * ATT_DIM])
            scores = dot(jnp.concatenate(asked, axis=0), kv_s[0, seen, kv_cols], COLS_LAST)
            scores = scores + jnp.concatenate([bias_s[r : r + tok, seen]] * count, axis=0)
            top = jnp.max(scores, axis=1, keepdims=True)
            probs = jnp.exp2((scores - top) * scale)
            total = jnp.sum(probs, axis=1, keepdims=True)
            summed = dot(probs.astype(BF16), kv_s[1, seen, kv_cols]) / total
            for h in range(count):
                part = summed[h * tok : (h + 1) * tok].astype(BF16)
                for side in range(2):
                    owned = part[side * part_rows : (side + 1) * part_rows]
                    cols = slice((first + h) * ATT_DIM, (first + h + 1) * ATT_DIM)
                    attended_s[step_no, r // tok * 2 + side, :, cols] = owned
        size = count * ATT_DIM
        at = pl.multiple_of((tp * 2 + parity) * q_all + lead + first * ATT_DIM, 128)
        home = attended_out.at[:, pl.ds(at, size)]
        cols = slice(first * ATT_DIM, first * ATT_DIM + size)
        here = attended_s.at[step_no]
        leave(lambda core, side: here.at[core * 2 + side, :, cols], home)

    def merge_first():
        coefficients()
        merge(0)

    def attend(kv_head):
        step_no = kv_head * q_width // (HEADS_AT_ONCE * ATT_DIM)
        kv_cols = slice(kv_head * ATT_DIM, (kv_head + 1) * ATT_DIM)
        wait_past(kv_head)
        for lead in range(kv_head * q_width, (kv_head + 1) * q_width, HEADS_AT_ONCE * ATT_DIM):
            attend_heads(kv_cols, step_no, lead, 0, HEADS_AT_ONCE)
            if step_no == 0:
                forward()
            for k in range(len(MERGE_AFTER)):
                if MERGE_AFTER[k] == step_no:
                    if k == 0:
                        pl.when(pair > 0)(merge_first)
                    else:
                        merge(k)
            for k in range(len(PASS_AFTER)):
                if PASS_AFTER[k] == step_no:
                    pass_on(k)
            step_no += 1

    @pl.loop(0, 2)
    def _(turn):
        attend_now = lax.rem(turn + (pair == 0).astype(jnp.int32), 2) == 1
        pl.when(attend_now)(functools.partial(attend, 0))
        pl.when(jnp.logical_not(attend_now))(intra)

    pl.when(pair == 0)(merge_first)
    for kv_head in range(1, kv_heads):
        attend(kv_head)

    ones = jnp.ones((8, 256), BF16)
    squares = [jnp.zeros((rows, 128), F32)] * groups

    def finish(local, first, count):
        lead = local * group_width + first * PIECE
        ready, fed_by = [], []
        for tile in range(0, count * PIECE, 128):
            cols = slice(lead + tile, lead + tile + 128)
            wide = spread_heads(entry_s[...], cols.start // head_size, head_size)
            z = gate_s[:, cols].astype(F32)
            z = z / (1.0 + jnp.exp(-z))
            ready.append(y_s[:, cols] * z)
            fed_by.append(wide * z)
        if local == 1:
            pl.when(fed)(pass_trip(first, count).wait_recv)
        carried = []
        for k in range(first, first + count):
            carried.append(blend(beside_s, behind_s, k, 4) if local == 0 else second_s[k])
        proj = slice(local * state, (local + 1) * state)
        incoming = dot(c_s[:, proj], jnp.concatenate(carried, axis=1))
        square = squares[local]
        for tile in range(0, count * PIECE, 128):
            cols = slice(lead + tile, lead + tile + 128)
            total = ready[tile // 128] + incoming[:, tile : tile + 128] * fed_by[tile // 128]
            square += total * total
            at = parity * width + group_of[local] * group_width + first * PIECE + tile
            gain = weight_ref[:, pl.ds(pl.multiple_of(at, 128), 128)]
            done = (total * gain).astype(BF16)
            for rank in range(4):
                owned = done[rank * part_rows : (rank + 1) * part_rows]
                raw_s[rank, cols.start // PIECE] = owned
        squares[local] = square
        at = ((tp * 2 + parity) * groups + group_of[local]) * pieces + first
        here = pl.ds(lead // PIECE, count)
        leave(
            lambda core, side: raw_s.at[core * 2 + side, here],
            raw_out.at[pl.ds(at, count)],
        )
        if first + count == pieces:
            here = slice(local * 8, local * 8 + 8)
            high = square.astype(BF16)
            halves = [high, (square - high.astype(F32)).astype(BF16)]
            sums_s[here, :] = dot(ones, jnp.concatenate(halves, axis=1), COLS_LAST)
            at = ((tp * 2 + parity) * groups + group_of[local]) * 8
            home = sums_out.at[pl.ds(pl.multiple_of(at, 8), 8), :]

            def half(core, side):
                return sums_s.at[here, pl.ds(pl.multiple_of(core * tok, tok), tok)]

            leave(half, home, sums_send, sums_recv, sums_own)

    ready_gate()
    merged, passed = len(MERGE_AFTER), len(PASS_AFTER)
    for k in range(pairs):
        if k == 2:
            finish(1, 0, 2)
        while passed <= k:
            pass_on(passed)
            passed += 1
        finish(0, 2 * k, 2)
        while merged < pairs:
            merge(merged)
            merged += 1
    for k in range(1, pairs - 1):
        finish(1, 2 * k, 2)
    finish(1, pieces - 2, 1)
    finish(1, pieces - 1, 1)

    assert used == [send_sem.shape[0], recv_sem.shape[0], own_sem.shape[0]], used
    t_trip.wait_send()
    remote(traded_ref, traded_ref, core_peer, trade_send, loan_recv).wait_send()
    given = step_s.at[:, :tok]
    remote(given, given, core_peer, step_send, loan_recv).wait_send()
    sent = kv_s.at[:, :rows, :]

    @pl.when(ahead)
    def _():
        remote(sent, sent, core_peer, far_send, loan_recv).wait_send()

    for j, (k, head, core, lent) in enumerate(items):
        part = kv_s.at[0, :rows, head_cols(0)]
        closing = remote(part, part, core_peer, item_send + j, loan_recv)
        pl.when((odd == 1) & ahead & (parity == core))(closing.wait_send)
        closing = remote(loan_s.at[j], loan_s.at[j], core_peer, item_send + j, loan_recv)
        pl.when((odd == 0) & lent)(closing.wait_send)

    @pl.when(odd == 0)
    def _():
        remote(sent, sent, core_peer, near_send, loan_recv).wait_send()

    @pl.when((odd == 1) & ahead)
    def _():
        part = kv_s.at[:, :rows, head_cols(0)]
        remote(part, part, core_peer, near_send, loan_recv).wait_send()

    half = own_s.at[:pieces]
    pl.when((odd == 0) | ahead)(remote(half, half, beside, first_send, first_recv).wait_send)
    pl.when(feeds)(remote(half, half, beside, pass_send, pass_recv).wait_send)

    @pl.when(ahead)
    def _():
        remote(half, half, beside, merge_send, merge_recv).wait_send()

    left = (width + q_all) * part_rows * 2 // (width * 4)
    settle(y_s.at[: 3 * left], y_s.at[:left], exit_send, exit_recv, exit_own)
    left = 8 * groups
    settle(l_s.at[: 3 * left], l_s.at[:left], sums_send, sums_recv, sums_own)


def scale_kernel(raw, sums, attended, mixed_out, attended_out, mixed_s, sem):
    tp = lax.axis_index("tp")
    rows, width = mixed_s.shape
    group_width = width // GROUPS
    copies = []
    for k in range(0, rows, 16):
        part = slice(k, k + 16)
        copy = pltpu.make_async_copy(
            attended.at[part], attended_out.at[part], sem.at[GROUPS + k // 16]
        )
        copy.start()
        copies.append(copy)
    squares = sums[...]
    squares = jnp.concatenate([squares, jnp.zeros((128 - squares.shape[0], 128), F32)], axis=0).T
    squares = jnp.where(tp == 0, squares[:rows], squares[rows:])
    factor = lax.rsqrt(squares * (1.0 / group_width) + 1e-05)
    for g in range(GROUPS):
        for k in range(g * group_width // PIECE, (g + 1) * group_width // PIECE):
            scaled = raw[k].astype(F32) * factor[:, 8 * g : 8 * g + 1]
            mixed_s[:, k * PIECE : (k + 1) * PIECE] = scaled.astype(BF16)
        cols = slice(g * group_width, (g + 1) * group_width)
        copy = pltpu.make_async_copy(mixed_s.at[:, cols], mixed_out.at[:, cols], sem.at[g])
        copy.start()
        copies.append(copy)
    for copy in copies:
        copy.wait()


def local_pair(
    doc_lengths,
    ssm_x,
    ssm_gate,
    ssm_b,
    ssm_c,
    step_size,
    decay_rate,
    norm_weight,
    queries,
    keys,
    values,
):
    tok, width = ssm_x.shape
    rows, half = 2 * tok, width // 2
    groups = step_size.shape[1] * GROUPS // HEADS // 2
    state = ssm_b.shape[1] // (2 * groups)
    kv_half = keys.shape[1] // 2
    q_half = queries.shape[1] // 2
    pieces = half // PIECE
    any_spec = pl.BlockSpec(memory_space=pl.ANY)
    vmem_spec = pl.BlockSpec(memory_space=pltpu.VMEM)
    part = rows // 4
    group_pieces = pieces // groups
    items = 4 * (kv_half // ATT_DIM - 1)
    step_width = HEADS_AT_ONCE * ATT_DIM
    state_piece = pltpu.VMEM((group_pieces, state, PIECE), BF16)
    scratch = [
        pltpu.VMEM((rows, half), BF16),
        pltpu.VMEM((rows, half), BF16),
        pltpu.VMEM((rows, groups * state), BF16),
        pltpu.VMEM((rows, groups * state), BF16),
        pltpu.VMEM((step_size.shape[1] // 2, rows), F32),
        pltpu.VMEM((rows, q_half), BF16),
        pltpu.VMEM((2, 3 * rows, kv_half), BF16),
        pltpu.VMEM((pieces, state, PIECE), BF16),
        state_piece,
        state_piece,
        state_piece,
        state_piece,
        state_piece,
        pltpu.VMEM((8, 128), F32),
        pltpu.VMEM((8, 128), F32),
        pltpu.VMEM((8, half // groups), F32),
        pltpu.VMEM((items, tok, ATT_DIM), BF16),
        pltpu.SMEM(doc_lengths.shape, jnp.int32),
        pltpu.VMEM((1, decay_rate.shape[0]), F32),
        pltpu.VMEM((1, norm_weight.shape[0]), F32),
        pltpu.VMEM((rows, half), F32),
        pltpu.VMEM((4, pieces, part, PIECE), BF16),
        pltpu.VMEM((8 * groups, rows), F32),
        pltpu.VMEM((q_half // step_width, 4, part, step_width), BF16),
        pltpu.VMEM((rows, 3 * rows), F32),
        pltpu.VMEM((rows, 128), F32),
        pltpu.VMEM((128, rows), F32),
        pltpu.VMEM((128, rows), F32),
        pltpu.VMEM((rows, 128), F32),
        pltpu.VMEM((rows, 128), F32),
        pltpu.SemaphoreType.DMA((10 + items,)),
        pltpu.SemaphoreType.DMA((11 + kv_half // ATT_DIM * 2 + items + 3 * group_pieces // 2,)),
        pltpu.SemaphoreType.DMA((7,)),
    ]
    raw, sums, attended = pl.pallas_call(
        functools.partial(pair_kernel, lax.axis_size("ctx")),
        out_shape=(
            pltpu.VMEM((4 * pieces, part, PIECE), BF16),
            pltpu.VMEM((8 * GROUPS, tok), F32),
            pltpu.VMEM((part, 4 * q_half), BF16),
        ),
        in_specs=[any_spec] * 11,
        out_specs=(vmem_spec, vmem_spec, vmem_spec),
        scratch_shapes=scratch,
        compiler_params=pltpu.CompilerParams(collective_id=0, has_side_effects=True),
    )(
        doc_lengths,
        ssm_x,
        ssm_gate,
        ssm_b,
        ssm_c,
        step_size.T,
        queries,
        keys,
        values,
        decay_rate[None, :],
        norm_weight[None, :],
    )
    return pl.pallas_call(
        scale_kernel,
        out_shape=(
            jax.ShapeDtypeStruct((part, 4 * half), BF16),
            jax.ShapeDtypeStruct(attended.shape, BF16),
        ),
        in_specs=[vmem_spec] * 3,
        out_specs=(any_spec, any_spec),
        scratch_shapes=[pltpu.VMEM((part, 4 * half), BF16), pltpu.SemaphoreType.DMA((GROUPS + part // 16,))],
    )(*[pltpu.with_memory_space_constraint(a, pltpu.VMEM) for a in (raw, sums, attended)])


def solution(mesh):
    tp = mesh.shape["tp"]
    paired = tp == 2 and mesh.shape["ctx"] % 4 == 0 and mesh.shape["ctx"] > 4 and GROUPS // tp % 2 == 0
    return jax.shard_map(
        local_pair if paired else local_any,
        mesh=mesh,
        in_specs=(
            P(),
            P("ctx", "tp"),
            P("ctx", "tp"),
            P("ctx", "tp"),
            P("ctx", "tp"),
            P("ctx", "tp"),
            P("tp"),
            P("tp"),
            P("ctx", "tp"),
            P("ctx", "tp"),
            P("ctx", "tp"),
        ),
        out_specs=(P(("ctx", "tp"), None), P(("ctx", "tp"), None)),
        check_vma=False,
    )
```

```python
import functools

import jax
import jax.numpy as jnp
from jax import lax
from jax.experimental import pallas as pl
from jax.experimental.pallas import tpu as pltpu
from jax.sharding import PartitionSpec as P

HEADS = 128
GROUPS = 8
ATT_DIM = 128
DOC_DEVS = 4


NEG_LARGE = -1e30


def for_sending(x):
    return jax.tree.map(lambda a: a.astype(jnp.bfloat16) if a.dtype == jnp.float32 else a, x)


def passed_along(block, axis, distance):
    devices = range(lax.axis_size(axis))
    route = [(i - distance, i) for i in devices if i - distance in devices]
    return lax.ppermute(block, axis, route)


def doc_starts(doc_lengths):
    return jnp.cumsum(doc_lengths) - doc_lengths


def doc_index(positions, starts):
    return jnp.sum((starts[None, :] <= positions[:, None]).astype(jnp.int32), axis=1) - 1


def block_terms(ssm_x, ssm_b, ssm_c, step_size, decay_rate, doc_ids, prev_id, group_heads):
    tok_rows = ssm_x.shape[0]
    head_count = step_size.shape[1]
    group_count = head_count // group_heads
    head_size = ssm_x.shape[1] // head_count
    state_size = ssm_b.shape[1] // group_count
    inputs = ssm_x.reshape(tok_rows, group_count, group_heads, head_size)
    in_proj = ssm_b.reshape(tok_rows, group_count, state_size)
    out_proj = ssm_c.reshape(tok_rows, group_count, state_size)
    log_decay = -(step_size * decay_rate[None, :])
    cumulative = jnp.cumsum(log_decay, axis=0)
    same_doc = doc_ids[:, None] == doc_ids[None, :]
    causal = jnp.arange(tok_rows)[:, None] >= jnp.arange(tok_rows)[None, :]
    allowed = (same_doc & causal)[None]
    spread = cumulative.T[:, :, None] - cumulative.T[:, None, :]
    weights = (
        jnp.where(allowed, jnp.exp(jnp.where(allowed, spread, 0.0)), 0.0) * step_size.T[:, None, :]
    )
    intersection = jnp.einsum("tgn,sgn->gts", out_proj, in_proj, preferred_element_type=jnp.float32)
    mixing = (
        weights.reshape(group_count, group_heads, tok_rows, tok_rows) * intersection[:, None]
    ).astype(jnp.bfloat16)
    y_intra = jnp.einsum("ghts,sghp->tghp", mixing, inputs, preferred_element_type=jnp.float32)
    final_sum = cumulative[-1]
    tail = (
        jnp.exp(final_sum[None, :] - cumulative)
        * step_size
        * (doc_ids == doc_ids[-1]).astype(jnp.float32)[:, None]
    )
    scaled = (
        inputs.astype(jnp.float32) * tail.reshape(tok_rows, group_count, group_heads)[..., None]
    ).astype(jnp.bfloat16)
    state_local = jnp.einsum("sghp,sgn->ghpn", scaled, in_proj, preferred_element_type=jnp.float32)
    entry = jnp.exp(cumulative) * (doc_ids == prev_id).astype(jnp.float32)[:, None]
    transmit = jnp.exp(final_sum) * (doc_ids[-1] == prev_id).astype(jnp.float32)
    return (y_intra, state_local, entry, transmit.reshape(group_count, group_heads))


def finish_rows(y_intra, entry, carried, ssm_c, ssm_gate, norm_weight):
    tok_rows, group_count, group_heads, head_size = y_intra.shape
    out_proj = ssm_c.reshape(tok_rows, group_count, -1).astype(jnp.float32)
    incoming = jnp.einsum("tgn,ghpn->tghp", out_proj, carried, precision=lax.Precision.HIGHEST)
    mixer_out = y_intra + incoming * entry.reshape(tok_rows, group_count, group_heads)[..., None]
    gate_vals = ssm_gate.reshape(tok_rows, group_count, group_heads, head_size).astype(jnp.float32)
    gated = (mixer_out * jax.nn.silu(gate_vals)).reshape(
        tok_rows, group_count, group_heads * head_size
    )
    factor = lax.rsqrt(jnp.mean(gated * gated, axis=2, keepdims=True) + 1e-05)
    return ((gated * factor).reshape(tok_rows, -1) * norm_weight[None, :]).astype(jnp.bfloat16)


def chain_states(earlier, later):
    return (earlier[0] * later[0], later[0][:, :, None, None] * earlier[1] + later[1])


def attention_update(
    carry, query_rows, key_block, value_block, key_pos, query_pos, query_doc, starts
):
    running_max, running_sum, running_acc = carry
    block_rows = key_block.shape[0]
    kv_local = key_block.shape[1] // ATT_DIM
    key_heads = key_block.reshape(block_rows, kv_local, ATT_DIM)
    value_heads = value_block.reshape(block_rows, kv_local, ATT_DIM)
    key_doc = doc_index(key_pos, starts)
    allowed = (query_doc[:, None] == key_doc[None, :]) & (key_pos[None, :] <= query_pos[:, None])
    scores = jnp.einsum(
        "tngd,knd->ngtk", query_rows, key_heads, preferred_element_type=jnp.float32
    ) * ATT_DIM ** (-0.5)
    scores = jnp.where(allowed[None, None], scores, -jnp.inf)
    new_max = jnp.maximum(running_max, jnp.max(scores, axis=3))
    probs = jnp.exp(scores - new_max[..., None])
    factor = jnp.exp(running_max - new_max)
    new_sum = running_sum * factor + jnp.sum(probs, axis=3)
    weighted = jnp.einsum(
        "ngtk,knd->ngtd",
        probs.astype(jnp.bfloat16),
        value_heads,
        preferred_element_type=jnp.float32,
    )
    return (new_max, new_sum, running_acc * factor[..., None] + weighted)


def local_any(
    doc_lengths,
    ssm_x,
    ssm_gate,
    ssm_b,
    ssm_c,
    step_size,
    decay_rate,
    norm_weight,
    queries,
    keys,
    values,
):
    tok_rows = ssm_x.shape[0]
    ctx_index = lax.axis_index("ctx")
    begin = ctx_index * tok_rows
    positions = begin + jnp.arange(tok_rows, dtype=jnp.int32)
    starts = doc_starts(doc_lengths)
    doc_ids = doc_index(positions, starts)
    prev_id = doc_index(jnp.reshape(begin - 1, (1,)), starts)[0]
    group_heads = HEADS // GROUPS
    y_intra, state_local, entry, transmit = block_terms(
        ssm_x, ssm_b, ssm_c, step_size, decay_rate, doc_ids, prev_id, group_heads
    )
    merged = (transmit, state_local)
    for level_bit in range(DOC_DEVS.bit_length() - 1):
        earlier = passed_along(
            (for_sending(merged[0]), for_sending(merged[1])), "ctx", 1 << level_bit
        )
        merged = chain_states(earlier, merged)
    carried = passed_along(merged[1], "ctx", 1)
    mixed_rows = finish_rows(y_intra, entry, carried, ssm_c, ssm_gate, norm_weight)
    kv_local = keys.shape[1] // ATT_DIM
    q_groups = queries.shape[1] // (kv_local * ATT_DIM)
    query_rows = queries.reshape(tok_rows, kv_local, q_groups, ATT_DIM)
    floor_start = jnp.max(jnp.where(starts <= begin, starts, 0))
    query_last = begin + tok_rows - 1
    carry_shape = (kv_local, q_groups, tok_rows)
    initial = (
        jnp.full(carry_shape, NEG_LARGE, jnp.float32),
        jnp.zeros(carry_shape, jnp.float32),
        jnp.zeros(carry_shape + (ATT_DIM,), jnp.float32),
    )

    def visit(carry, key_block, value_block, key_begin):
        block_rows = key_block.shape[0]
        needed = (key_begin <= query_last) & (key_begin + block_rows - 1 >= floor_start)

        def update(inner):
            key_pos = key_begin + jnp.arange(block_rows, dtype=jnp.int32)
            return attention_update(
                inner, query_rows, key_block, value_block, key_pos, positions, doc_ids, starts
            )

        def unchanged(inner):
            return inner

        return lax.cond(needed, update, unchanged, carry)

    totals = visit(initial, keys, values, begin)
    for hop_count in range(1, DOC_DEVS + 1):
        near_keys, near_values = passed_along((keys, values), "ctx", hop_count)
        totals = visit(totals, near_keys, near_values, begin - hop_count * tok_rows)
    final_out = totals[2] / totals[1][..., None]
    attended_rows = (
        jnp.transpose(final_out, (2, 0, 1, 3)).reshape(tok_rows, -1).astype(jnp.bfloat16)
    )
    mixed_local, attended_local = (
        lax.all_to_all(mixed_rows, "tp", split_axis=0, concat_axis=1, tiled=True),
        lax.all_to_all(attended_rows, "tp", split_axis=0, concat_axis=1, tiled=True),
    )
    return (mixed_local, attended_local)


LOG2E = 1.4426950408889634
F32 = jnp.float32
BF16 = jnp.bfloat16
MESH_ID = pl.DeviceIdType.MESH
COLS_LAST = (((1,), (1,)), ((), ()))
ROWS_FIRST = (((0,), (0,)), ((), ()))
PIECE = 128
HEADS_AT_ONCE = 2
MERGE_AFTER = (2, 4)
PASS_AFTER = (7,)
FIRST_HEAD_ORDER = (
    (0, 0, 1),
    (1, 0, 1),
    (0, 0, 0),
    (0, 1, 1),
    (1, 1, 1),
    (1, 0, 0),
    (0, 1, 0),
    (1, 1, 0),
)


def dot(a, b, dims=(((1,), (0,)), ((), ())), precision=None):
    return lax.dot_general(a, b, dims, precision=precision, preferred_element_type=F32)


def spread_heads(columns, head, head_size):
    lane = lax.broadcasted_iota(jnp.int32, (columns.shape[0], 128), 1)
    wide = jnp.broadcast_to(columns[:, head : head + 1], lane.shape)
    for k in range(1, 128 // head_size):
        wide = jnp.where(lane >= k * head_size, columns[:, head + k : head + k + 1], wide)
    return wide


def pair_kernel(
    n,
    lengths_in,
    x_in,
    gate_in,
    b_in,
    c_in,
    step_in,
    q_in,
    k_in,
    v_in,
    rate_in,
    weight_in,
    raw_out,
    sums_out,
    attended_out,
    x_s,
    gate_s,
    b_s,
    c_s,
    step_s,
    q_s,
    kv_s,
    own_s,
    beside_s,
    merged_s,
    behind_s,
    passed_s,
    second_s,
    t_own,
    t_beside,
    coef_s,
    loan_s,
    lengths,
    rate_ref,
    weight_ref,
    y_s,
    raw_s,
    sums_s,
    attended_s,
    bias_s,
    l_s,
    lt_s,
    dtt_s,
    tail_s,
    entry_s,
    send_sem,
    recv_sem,
    own_sem,
):
    index = lax.axis_index("ctx")
    tp = lax.axis_index("tp")
    parity, pair = lax.rem(index, 2), lax.div(index, 2)
    odd = lax.rem(pair, 2)
    base = index - parity
    other = 1 - parity
    tok = x_in.shape[0]
    rows = 2 * tok
    width = x_s.shape[1]
    group_heads = HEADS // GROUPS
    heads = step_in.shape[0] // 2
    groups = heads // group_heads
    group_width = width // groups
    state = b_s.shape[1] // groups
    head_size = width // heads
    kv_width = kv_s.shape[2]
    kv_heads = kv_width // ATT_DIM
    q_width = q_s.shape[1] // kv_heads
    pieces = group_width // PIECE
    group_of = (odd, 1 - odd)

    core_peer = (base + other, tp)
    tp_peer = (index, 1 - tp)
    cross_peer = (base + other, 1 - tp)
    beside = (index + 2 - 4 * odd, tp)
    barrier = pltpu.get_barrier_semaphore()
    ahead, behind = base + 4 < n, base >= 4
    fed = (odd == 1) | behind
    feeds = (odd == 0) | behind
    greeted = jnp.int32(3)

    def greet(peer):
        pl.semaphore_signal(barrier, inc=1, device_id=peer, device_id_type=MESH_ID)

    for step in (2, 4, -2, -4):
        there = (base + step >= 0) & (base + step < n)
        greeted += 2 * there.astype(jnp.int32)

        @pl.when(there)
        def _():
            for core in range(2):
                greet((base + step + core, tp))

    for peer in (core_peer, tp_peer, cross_peer):
        greet(peer)

    small = ((lengths_in, lengths), (rate_in, rate_ref), (weight_in, weight_ref))
    small = [pltpu.make_async_copy(src, dst, own_sem.at[k]) for k, (src, dst) in enumerate(small)]
    for copy in small:
        copy.start()
    used = [0, 0, len(small)]

    def slots(kind, count=1):
        used[kind] += count
        return used[kind] - count

    def remote(src, dst, peer, send, recv):
        return pltpu.make_async_remote_copy(
            src_ref=src,
            dst_ref=dst,
            send_sem=send_sem.at[send],
            recv_sem=recv_sem.at[recv],
            device_id=peer,
            device_id_type=MESH_ID,
        )

    at_mine = pl.multiple_of(parity * tok, tok)
    mine = pl.ds(at_mine, tok)

    trade_send, trade_own = slots(0), slots(2)
    step_send, step_own = slots(0), slots(2)

    def trade(moves, whole, recv, send=trade_send, own=trade_own):
        for give, keep, place in moves:
            pltpu.make_async_copy(keep, place, own_sem.at[own]).start()

        def start():
            for give, keep, place in moves:
                remote(give, place, core_peer, send, recv).start()

        def ready():
            remote(whole, whole, core_peer, send, recv).wait_recv()

        return start, ready

    def by_group(src, dst, local_groups):
        size = dst.shape[1] // groups

        def part(core, local):
            at = core * groups * size + group_of[local] * size
            return src.at[:, pl.ds(pl.multiple_of(at, 128), size)]

        moves, first = [], local_groups[0]
        for local in local_groups:
            place = dst.at[mine, local * size : (local + 1) * size]
            moves.append((part(other, local), part(parity, local), place))
        whole = dst.at[:tok, first * size : (first + len(local_groups)) * size]
        return trade(moves, whole, slots(1))

    def part_of(src, core, begin, size, total):
        return src.at[:, pl.ds(pl.multiple_of(core * total + begin, 128), size)]

    @pl.when(pair < 2)
    def _():
        kv_s[:, :rows, :] = jnp.zeros((2, rows, kv_width), BF16)

    @pl.when(pair < 1)
    def _():
        kv_s[:, rows : 2 * rows, :] = jnp.zeros((2, rows, kv_width), BF16)
        second_s[...] = jnp.zeros_like(second_s)

    @pl.when((odd == 0) & jnp.logical_not(ahead))
    def _():
        beside_s[...] = jnp.zeros_like(beside_s)

    near_send, far_send = slots(0), slots(0)
    near_recv = [slots(1) for head in range(kv_heads)]
    far_recv = [slots(1) for head in range(kv_heads)]
    early = base + 8 < n
    loose = early & ((base + 12 < n) | (base < 4))
    items = []
    for head in range(1, kv_heads):
        items += [(0, head, 0, ahead), (0, head, 1, early)]
        items += [(1, head, 0, loose), (1, head, 1, loose)]
    item_send, loan_recv = slots(0, len(items)), slots(1, len(items))

    def head_cols(head):
        return slice(head * ATT_DIM, (head + 1) * ATT_DIM)

    def send_part(k, head, dst, step, at, send, recv, cores=(0, 1)):
        for core in cores:
            remote(
                part_of((k_in, v_in)[k], core, head * ATT_DIM, ATT_DIM, kv_width),
                dst.at[pl.ds(at, tok), :],
                (base + step + core, tp),
                send,
                recv,
            ).start()

    def send_near():
        @pl.when(odd == 0)
        def _():
            for head in range(kv_heads):
                for k in range(2):
                    near = kv_s.at[k, :, head_cols(head)]
                    send_part(k, head, near, 2, at_mine + rows, near_send, near_recv[head])

        @pl.when((odd == 1) & ahead)
        def _():
            for k, far, core in FIRST_HEAD_ORDER:
                place = kv_s.at[k, :, head_cols(0)]
                if far:
                    send_part(k, 0, place, 4, at_mine, far_send, far_recv[0], (core,))
                else:
                    send_part(k, 0, place, 2, at_mine + rows, near_send, near_recv[0], (core,))

    def send_items(lending):
        for j, (k, head, core, lent) in enumerate(items):
            there = lent if lending else ahead & jnp.logical_not(lent)

            @pl.when((odd == 1) & (parity == core) & there)
            def _():
                if lending:
                    send_part(k, head, loan_s.at[j], -2, 0, item_send + j, loan_recv + j)
                else:
                    near = kv_s.at[k, :, head_cols(head)]
                    send_part(k, head, near, 2, at_mine + rows, item_send + j, near_recv[head])

    def send_far(head):
        @pl.when(ahead & ((odd == 0) | (head > 0)))
        def _():
            for k in range(2):
                far = kv_s.at[k, :, head_cols(head)]
                send_part(k, head, far, 4, at_mine, far_send, far_recv[head])

    def arrived(place, recv):
        remote(place, place, core_peer, far_send, recv).wait_recv()

    def forward():
        for j, (k, head, core, lent) in enumerate(items):

            @pl.when((odd == 0) & lent)
            def _():
                arrived(loan_s.at[j], loan_recv + j)
                at = rows + core * tok
                near = kv_s.at[k, at : at + tok, head_cols(head)]
                peer = (index + 4, tp)
                remote(loan_s.at[j], near, peer, item_send + j, near_recv[head]).start()

    def wait_past(head):
        @pl.when(fed)
        def _():
            arrived(kv_s.at[:, rows : 2 * rows, head_cols(head)], near_recv[head])

        @pl.when(behind)
        def _():
            arrived(kv_s.at[:, :rows, head_cols(head)], far_recv[head])

    moves = []
    for local in range(groups):
        place = step_s.at[local * group_heads : (local + 1) * group_heads, mine]

        def step_part(core):
            at = (core * groups + group_of[local]) * group_heads
            return step_in.at[pl.ds(pl.multiple_of(at, 8), group_heads)]

        moves.append((step_part(other), step_part(parity), place))
    start_step, ready_step = trade(moves, step_s.at[:, :tok], slots(1), step_send, step_own)
    start_b, ready_b = by_group(b_in, b_s, tuple(range(groups)))
    trade_x = {local: by_group(x_in, x_s, (local,)) for local in (1, 0)}
    start_c, ready_c = by_group(c_in, c_s, tuple(range(groups)))
    moves = []
    for k, src in enumerate((k_in, v_in)):
        give = part_of(src, other, 0, kv_width, kv_width)
        keep = part_of(src, parity, 0, kv_width, kv_width)
        moves.append((give, keep, kv_s.at[k, pl.ds(at_mine + 2 * rows, tok), :]))
    ready_kvq = slots(1)
    start_kv, _ = trade(moves, kv_s.at[:, :tok, :], ready_kvq)
    q_all = q_s.shape[1]
    give, keep = part_of(q_in, other, 0, q_all, q_all), part_of(q_in, parity, 0, q_all, q_all)
    start_q, _ = trade([(give, keep, q_s.at[mine, :])], q_s.at[:tok, :], ready_kvq)
    start_gate, ready_gate = by_group(gate_in, gate_s, tuple(range(groups)))

    @pl.when(pair < 2)
    def _():
        behind_s[...] = jnp.zeros_like(behind_s)

    small[0].wait()
    begin = pair * rows
    row_at = begin - 2 * rows + lax.broadcasted_iota(jnp.int32, (1, 3 * rows), 1)
    col_at = begin + lax.broadcasted_iota(jnp.int32, (rows, 1), 0)
    row_doc = jnp.zeros_like(row_at) - 1
    col_doc = jnp.zeros_like(col_at) - 1
    begun, prev_id, last_id = jnp.int32(0), jnp.int32(-1), jnp.int32(-1)
    for j in range(lengths.shape[0]):
        row_doc += (row_at >= begun).astype(jnp.int32)
        col_doc += (col_at >= begun).astype(jnp.int32)
        prev_id += (begin - 1 >= begun).astype(jnp.int32)
        last_id += (begin + rows - 1 >= begun).astype(jnp.int32)
        begun = begun + lengths[j]
    bias_s[...] = jnp.where((row_doc == col_doc) & (row_at <= col_at), 0.0, NEG_LARGE)

    pl.semaphore_wait(barrier, greeted)
    send_near()
    send_items(True)
    start_step()
    start_b()
    send_far(0)
    for local in (1, 0):
        trade_x[local][0]()
    for start in (start_c, start_kv, start_q, start_gate):
        start()

    small[1].wait()
    small[2].wait()
    ready_step()
    pltpu.make_async_copy(step_s.at[:, :tok], step_s.at[:, :tok], own_sem.at[step_own]).wait()
    step_t = jnp.concatenate([step_s[...], jnp.zeros((128 - heads, rows), F32)], axis=0)
    step = step_t.T
    rates = []
    for local in range(groups):
        rate = jnp.zeros((1, group_heads), F32)
        for k in range(2 * groups):
            here = parity * groups + group_of[local] == k
            rate = jnp.where(here, rate_ref[:, k * group_heads : (k + 1) * group_heads], rate)
        rates.append(rate)
    rate = jnp.concatenate(rates + [jnp.zeros((1, 128 - heads), F32)], axis=1)
    at = lax.broadcasted_iota(jnp.int32, (rows, rows), 0)
    to = lax.broadcasted_iota(jnp.int32, (rows, rows), 1)
    lower = (to <= at).astype(BF16)
    left, parts = -(step * rate), []
    for k in range(3):
        parts.append(left.astype(BF16)[:, :heads])
        left = left - left.astype(BF16).astype(F32)
    parts.append(jnp.zeros((rows, 128 - 3 * heads), BF16))
    sums = dot(lower, jnp.concatenate(parts, axis=1))
    lane = lax.broadcasted_iota(jnp.int32, (rows, 128), 1)
    sums = sums + pltpu.roll(sums, 128 - heads, 1) + pltpu.roll(sums, 128 - 2 * heads, 1)
    total_decay = jnp.where(lane < heads, sums, 0.0)
    final_sum = total_decay[rows - 1 :, :]
    l_s[...] = total_decay
    lt_s[...] = total_decay.T
    dtt_s[...] = step_t
    tail_s[...] = jnp.where(col_doc == last_id, jnp.exp(final_sum - total_decay) * step, 0.0)
    entry_s[...] = jnp.where(col_doc == prev_id, jnp.exp(total_decay), 0.0)
    passing = (last_id == prev_id).astype(F32)
    t_own[...] = jnp.broadcast_to(jnp.exp(final_sum) * passing, t_own.shape)
    t_trip = remote(t_own, t_beside, beside, slots(0), slots(1))
    t_trip.start()

    pairs = pieces // 2
    first_send, first_recv = slots(0), slots(1, pairs)
    merge_send, merge_recv = slots(0), slots(1, pairs)
    pass_send, pass_recv = slots(0), slots(1, pairs + 1)

    def two(k):
        return slice(2 * k, 2 * k + 2)

    def first_trip(k):
        src = own_s.at[pieces + 2 * k : pieces + 2 * k + 2]
        return remote(src, beside_s.at[two(k)], beside, first_send, first_recv + k)

    def merge_trip(k):
        src, peer = merged_s.at[two(k)], (index + 4, tp)
        return remote(src, behind_s.at[two(k)], peer, merge_send, merge_recv + k)

    def pass_trip(begin, count):
        span = slice(begin, begin + count)
        recv = pass_recv + (begin // 2 if count == 2 else begin - pieces + pairs + 1)
        return remote(passed_s.at[span], second_s.at[span], beside, pass_send, recv)

    def pass_trips(k):
        if k < pairs - 1:
            return [pass_trip(2 * k, 2)]
        return [pass_trip(2 * k, 1), pass_trip(2 * k + 1, 1)]

    traded = 2 * groups * state // 128 + 2 * width // 128 + q_all // 128 + 2 * kv_width // 128
    traded_ref = y_s.at[: traded * tok * 128 * 2 // (width * 4)]

    per = 128 // head_size
    pltpu.make_async_copy(traded_ref, traded_ref, own_sem.at[trade_own]).wait()
    ready_b()
    for local in (1, 0):
        trade_x[local][1]()
        b_t = b_s[:, local * state : (local + 1) * state].T
        for k in range(local * pieces, (local + 1) * pieces, 2):
            parts = []
            for tile in range(2):
                lead = (k + tile) * PIECE
                wide = spread_heads(tail_s[...], lead // head_size, head_size)
                parts.append((x_s[:, lead : lead + PIECE].astype(F32) * wide).astype(BF16))
            made = dot(b_t, jnp.concatenate(parts, axis=1)).astype(BF16)
            for tile in range(2):
                own_s[k + tile] = made[:, tile * PIECE : (tile + 1) * PIECE]
        if local == 1:

            @pl.when((odd == 0) | ahead)
            def _():
                for k in range(pairs):
                    first_trip(k).start()

    send_items(False)
    for head in range(1, kv_heads):
        send_far(head)
    ready_c()

    def intra():
        for g in range(groups):
            proj = slice(g * state, (g + 1) * state)
            inter = dot(c_s[:, proj], b_s[:, proj], COLS_LAST)
            for tile in range(group_width // 128):
                lead = g * group_width + tile * 128
                halves = []
                for r in range(0, rows, tok):
                    seen = slice(0, r + tok)
                    bias = bias_s[r : r + tok, 2 * rows : 2 * rows + r + tok]
                    mixing = []
                    for h in range(lead // head_size, lead // head_size + per):
                        spread = l_s[r : r + tok, h : h + 1] - lt_s[h : h + 1, seen]
                        w = jnp.exp(spread + bias) * dtt_s[h : h + 1, seen] * inter[r : r + tok, seen]
                        mixing.append(w.astype(BF16))
                    both = dot(jnp.concatenate(mixing, axis=0), x_s[seen, lead : lead + 128])
                    whole = both[:tok]
                    for k in range(1, per):
                        part = both[k * tok : (k + 1) * tok]
                        whole = jnp.where(lane[:tok] >= k * head_size, part, whole)
                    y_s[r : r + tok, lead : lead + 128] = whole

    part_rows = rows // 4

    exit_send, exit_recv, exit_own = slots(0), slots(1), slots(2)
    sums_send, sums_recv, sums_own = slots(0), slots(1), slots(2)

    def leave(piece_for, home, send=exit_send, recv=exit_recv, own=exit_own):
        for core in (1, 0):
            peer = (base + core, 1 - tp)
            remote(piece_for(core, 1 - tp), home, peer, send, recv).start()
        remote(piece_for(other, tp), home, core_peer, send, recv).start()
        pltpu.make_async_copy(piece_for(parity, tp), home, own_sem.at[own]).start()

    def settle(thrice, once, send, recv, own):
        remote(thrice, thrice, core_peer, send, recv).wait()
        pltpu.make_async_copy(once, once, own_sem.at[own]).wait()

    def coefficients():
        t_trip.wait_recv()
        even = jnp.broadcast_to(odd == 0, (8, 128))
        row = lax.broadcasted_iota(jnp.int32, (8, 128), 0)
        for k in range(pieces):
            h = k * PIECE // head_size
            ours = spread_heads(t_own[...], h, head_size)
            theirs = spread_heads(t_beside[...], group_heads + h, head_size)
            values = (
                (1.0, ours),
                (theirs, 1.0),
                (1.0, 0.0),
                (ours, 1.0),
                (0.0, 1.0),
                (1.0, theirs),
            )
            table = jnp.zeros((8, 128), F32)
            for j, (if_even, if_odd) in enumerate(values):
                table = jnp.where(row == j, jnp.where(even, if_even, if_odd), table)
            coef_s[:, k * PIECE : (k + 1) * PIECE] = table

    def blend(left, right, k, row):
        cols = slice(k * PIECE, (k + 1) * PIECE)
        total = left[k].astype(F32) * coef_s[row : row + 1, cols]
        total += right[k].astype(F32) * coef_s[row + 1 : row + 2, cols]
        return total.astype(BF16)

    def merge(k):
        pl.when((odd == 1) | ahead)(first_trip(k).wait_recv)
        for j in (2 * k, 2 * k + 1):
            merged_s[j] = blend(beside_s, own_s, j, 0)

        @pl.when(ahead)
        def _():
            merge_trip(k).start()

    def pass_on(k):
        @pl.when(behind)
        def _():
            merge_trip(k).wait_recv()

        @pl.when(feeds)
        def _():
            for j in (2 * k, 2 * k + 1):
                passed_s[j] = blend(own_s, behind_s, j, 2)
            for trip in pass_trips(k):
                trip.start()

    scale = LOG2E * ATT_DIM ** (-0.5)
    kvq = y_s.at[: (2 * kv_width + q_all) * tok * 2 // (width * 4)]
    arrived(kvq, ready_kvq)
    def attend_heads(kv_cols, step_no, lead):
        at = pl.multiple_of((tp * 2 + parity) * q_all + lead, 128)
        home = attended_out.at[:, pl.ds(at, HEADS_AT_ONCE * ATT_DIM)]
        here = attended_s.at[step_no]
        for core in range(2):
            r = core * tok
            seen = slice(r, r + 2 * rows + tok)
            asked = []
            for h in range(HEADS_AT_ONCE):
                asked.append(q_s[r : r + tok, lead + h * ATT_DIM : lead + (h + 1) * ATT_DIM])
            scores = dot(jnp.concatenate(asked, axis=0), kv_s[0, seen, kv_cols], COLS_LAST)
            scores = scores + jnp.concatenate([bias_s[r : r + tok, seen]] * HEADS_AT_ONCE, axis=0)
            top = jnp.max(scores, axis=1, keepdims=True)
            probs = jnp.exp2((scores - top) * scale)
            total = jnp.sum(probs, axis=1, keepdims=True)
            summed = dot(probs.astype(BF16), kv_s[1, seen, kv_cols]) / total
            for h in range(HEADS_AT_ONCE):
                part = summed[h * tok : (h + 1) * tok].astype(BF16)
                for side in range(2):
                    owned = part[side * part_rows : (side + 1) * part_rows]
                    cols = slice(h * ATT_DIM, (h + 1) * ATT_DIM)
                    attended_s[step_no, core * 2 + side, :, cols] = owned
            if step_no == 0 or core == 1:
                for half in (core,) if step_no == 0 else (1, 0):
                    src, peer = here.at[half * 2 + 1 - tp], (base + half, 1 - tp)
                    remote(src, home, peer, exit_send, exit_recv).start()
        remote(here.at[other * 2 + tp], home, core_peer, exit_send, exit_recv).start()
        pltpu.make_async_copy(here.at[parity * 2 + tp], home, own_sem.at[exit_own]).start()

    def merge_first():
        coefficients()
        merge(0)

    def attend(kv_head):
        step_no = kv_head * q_width // (HEADS_AT_ONCE * ATT_DIM)
        kv_cols = slice(kv_head * ATT_DIM, (kv_head + 1) * ATT_DIM)
        wait_past(kv_head)
        for lead in range(kv_head * q_width, (kv_head + 1) * q_width, HEADS_AT_ONCE * ATT_DIM):
            attend_heads(kv_cols, step_no, lead)
            if step_no == 0:
                forward()
            for k in range(len(MERGE_AFTER)):
                if MERGE_AFTER[k] == step_no:
                    if k == 0:
                        pl.when(pair > 0)(merge_first)
                    else:
                        merge(k)
            for k in range(len(PASS_AFTER)):
                if PASS_AFTER[k] == step_no:
                    pass_on(k)
            step_no += 1

    @pl.loop(0, 2)
    def _(turn):
        attend_now = lax.rem(turn + (pair == 0).astype(jnp.int32), 2) == 1
        pl.when(attend_now)(functools.partial(attend, 0))
        pl.when(jnp.logical_not(attend_now))(intra)

    pl.when(pair == 0)(merge_first)
    for kv_head in range(1, kv_heads):
        attend(kv_head)

    ones = jnp.ones((8, 256), BF16)
    squares = [jnp.zeros((rows, 128), F32)] * groups

    def finish(local, first, count):
        lead = local * group_width + first * PIECE
        ready, fed_by = [], []
        for tile in range(0, count * PIECE, 128):
            cols = slice(lead + tile, lead + tile + 128)
            wide = spread_heads(entry_s[...], cols.start // head_size, head_size)
            z = gate_s[:, cols].astype(F32)
            z = z / (1.0 + jnp.exp(-z))
            ready.append(y_s[:, cols] * z)
            fed_by.append(wide * z)
        if local == 1:
            pl.when(fed)(pass_trip(first, count).wait_recv)
        carried = []
        for k in range(first, first + count):
            carried.append(blend(beside_s, behind_s, k, 4) if local == 0 else second_s[k])
        proj = slice(local * state, (local + 1) * state)
        incoming = dot(c_s[:, proj], jnp.concatenate(carried, axis=1))
        square = squares[local]
        for tile in range(0, count * PIECE, 128):
            cols = slice(lead + tile, lead + tile + 128)
            total = ready[tile // 128] + incoming[:, tile : tile + 128] * fed_by[tile // 128]
            square += total * total
            at = parity * width + group_of[local] * group_width + first * PIECE + tile
            gain = weight_ref[:, pl.ds(pl.multiple_of(at, 128), 128)]
            done = (total * gain).astype(BF16)
            for rank in range(4):
                owned = done[rank * part_rows : (rank + 1) * part_rows]
                raw_s[rank, cols.start // PIECE] = owned
        squares[local] = square
        at = ((tp * 2 + parity) * groups + group_of[local]) * pieces + first
        here = pl.ds(lead // PIECE, count)
        leave(
            lambda core, side: raw_s.at[core * 2 + side, here],
            raw_out.at[pl.ds(at, count)],
        )
        if first + count == pieces:
            here = slice(local * 8, local * 8 + 8)
            high = square.astype(BF16)
            halves = [high, (square - high.astype(F32)).astype(BF16)]
            sums_s[here, :] = dot(ones, jnp.concatenate(halves, axis=1), COLS_LAST)
            at = ((tp * 2 + parity) * groups + group_of[local]) * 8
            home = sums_out.at[pl.ds(pl.multiple_of(at, 8), 8), :]

            def half(core, side):
                return sums_s.at[here, pl.ds(pl.multiple_of(core * tok, tok), tok)]

            leave(half, home, sums_send, sums_recv, sums_own)

    ready_gate()
    merged, passed = len(MERGE_AFTER), len(PASS_AFTER)
    for k in range(pairs):
        if k == 2:
            finish(1, 0, 2)
        while passed <= k:
            pass_on(passed)
            passed += 1
        finish(0, 2 * k, 2)
        while merged < pairs:
            merge(merged)
            merged += 1
    for k in range(1, pairs - 1):
        finish(1, 2 * k, 2)
    finish(1, pieces - 2, 1)
    finish(1, pieces - 1, 1)

    assert used == [send_sem.shape[0], recv_sem.shape[0], own_sem.shape[0]], used
    t_trip.wait_send()
    remote(traded_ref, traded_ref, core_peer, trade_send, loan_recv).wait_send()
    given = step_s.at[:, :tok]
    remote(given, given, core_peer, step_send, loan_recv).wait_send()
    sent = kv_s.at[:, :rows, :]

    @pl.when(ahead)
    def _():
        remote(sent, sent, core_peer, far_send, loan_recv).wait_send()

    for j, (k, head, core, lent) in enumerate(items):
        part = kv_s.at[0, :rows, head_cols(0)]
        closing = remote(part, part, core_peer, item_send + j, loan_recv)
        pl.when((odd == 1) & ahead & (parity == core))(closing.wait_send)
        closing = remote(loan_s.at[j], loan_s.at[j], core_peer, item_send + j, loan_recv)
        pl.when((odd == 0) & lent)(closing.wait_send)

    @pl.when(odd == 0)
    def _():
        remote(sent, sent, core_peer, near_send, loan_recv).wait_send()

    @pl.when((odd == 1) & ahead)
    def _():
        part = kv_s.at[:, :rows, head_cols(0)]
        remote(part, part, core_peer, near_send, loan_recv).wait_send()

    half = own_s.at[:pieces]
    pl.when((odd == 0) | ahead)(remote(half, half, beside, first_send, first_recv).wait_send)
    pl.when(feeds)(remote(half, half, beside, pass_send, pass_recv).wait_send)

    @pl.when(ahead)
    def _():
        remote(half, half, beside, merge_send, merge_recv).wait_send()

    left = (width + q_all) * part_rows * 2 // (width * 4)
    settle(y_s.at[: 3 * left], y_s.at[:left], exit_send, exit_recv, exit_own)
    left = 8 * groups
    settle(l_s.at[: 3 * left], l_s.at[:left], sums_send, sums_recv, sums_own)


def scale_kernel(raw, sums, attended, mixed_out, attended_out, mixed_s, sem):
    tp = lax.axis_index("tp")
    rows, width = mixed_s.shape
    group_width = width // GROUPS
    copies = []
    for k in range(0, rows, 16):
        part = slice(k, k + 16)
        copy = pltpu.make_async_copy(
            attended.at[part], attended_out.at[part], sem.at[GROUPS + k // 16]
        )
        copy.start()
        copies.append(copy)
    squares = sums[...]
    squares = jnp.concatenate([squares, jnp.zeros((128 - squares.shape[0], 128), F32)], axis=0).T
    squares = jnp.where(tp == 0, squares[:rows], squares[rows:])
    factor = lax.rsqrt(squares * (1.0 / group_width) + 1e-05)
    for g in range(GROUPS):
        for k in range(g * group_width // PIECE, (g + 1) * group_width // PIECE):
            scaled = raw[k].astype(F32) * factor[:, 8 * g : 8 * g + 1]
            mixed_s[:, k * PIECE : (k + 1) * PIECE] = scaled.astype(BF16)
        cols = slice(g * group_width, (g + 1) * group_width)
        copy = pltpu.make_async_copy(mixed_s.at[:, cols], mixed_out.at[:, cols], sem.at[g])
        copy.start()
        copies.append(copy)
    for copy in copies:
        copy.wait()


def local_pair(
    doc_lengths,
    ssm_x,
    ssm_gate,
    ssm_b,
    ssm_c,
    step_size,
    decay_rate,
    norm_weight,
    queries,
    keys,
    values,
):
    tok, width = ssm_x.shape
    rows, half = 2 * tok, width // 2
    groups = step_size.shape[1] * GROUPS // HEADS // 2
    state = ssm_b.shape[1] // (2 * groups)
    kv_half = keys.shape[1] // 2
    q_half = queries.shape[1] // 2
    pieces = half // PIECE
    any_spec = pl.BlockSpec(memory_space=pl.ANY)
    vmem_spec = pl.BlockSpec(memory_space=pltpu.VMEM)
    part = rows // 4
    group_pieces = pieces // groups
    items = 4 * (kv_half // ATT_DIM - 1)
    step_width = HEADS_AT_ONCE * ATT_DIM
    state_piece = pltpu.VMEM((group_pieces, state, PIECE), BF16)
    scratch = [
        pltpu.VMEM((rows, half), BF16),
        pltpu.VMEM((rows, half), BF16),
        pltpu.VMEM((rows, groups * state), BF16),
        pltpu.VMEM((rows, groups * state), BF16),
        pltpu.VMEM((step_size.shape[1] // 2, rows), F32),
        pltpu.VMEM((rows, q_half), BF16),
        pltpu.VMEM((2, 3 * rows, kv_half), BF16),
        pltpu.VMEM((pieces, state, PIECE), BF16),
        state_piece,
        state_piece,
        state_piece,
        state_piece,
        state_piece,
        pltpu.VMEM((8, 128), F32),
        pltpu.VMEM((8, 128), F32),
        pltpu.VMEM((8, half // groups), F32),
        pltpu.VMEM((items, tok, ATT_DIM), BF16),
        pltpu.SMEM(doc_lengths.shape, jnp.int32),
        pltpu.VMEM((1, decay_rate.shape[0]), F32),
        pltpu.VMEM((1, norm_weight.shape[0]), F32),
        pltpu.VMEM((rows, half), F32),
        pltpu.VMEM((4, pieces, part, PIECE), BF16),
        pltpu.VMEM((8 * groups, rows), F32),
        pltpu.VMEM((q_half // step_width, 4, part, step_width), BF16),
        pltpu.VMEM((rows, 3 * rows), F32),
        pltpu.VMEM((rows, 128), F32),
        pltpu.VMEM((128, rows), F32),
        pltpu.VMEM((128, rows), F32),
        pltpu.VMEM((rows, 128), F32),
        pltpu.VMEM((rows, 128), F32),
        pltpu.SemaphoreType.DMA((10 + items,)),
        pltpu.SemaphoreType.DMA((11 + kv_half // ATT_DIM * 2 + items + 3 * group_pieces // 2,)),
        pltpu.SemaphoreType.DMA((7,)),
    ]
    raw, sums, attended = pl.pallas_call(
        functools.partial(pair_kernel, lax.axis_size("ctx")),
        out_shape=(
            pltpu.VMEM((4 * pieces, part, PIECE), BF16),
            pltpu.VMEM((8 * GROUPS, tok), F32),
            pltpu.VMEM((part, 4 * q_half), BF16),
        ),
        in_specs=[any_spec] * 11,
        out_specs=(vmem_spec, vmem_spec, vmem_spec),
        scratch_shapes=scratch,
        compiler_params=pltpu.CompilerParams(collective_id=0, has_side_effects=True),
    )(
        doc_lengths,
        ssm_x,
        ssm_gate,
        ssm_b,
        ssm_c,
        step_size.T,
        queries,
        keys,
        values,
        decay_rate[None, :],
        norm_weight[None, :],
    )
    return pl.pallas_call(
        scale_kernel,
        out_shape=(
            jax.ShapeDtypeStruct((part, 4 * half), BF16),
            jax.ShapeDtypeStruct(attended.shape, BF16),
        ),
        in_specs=[vmem_spec] * 3,
        out_specs=(any_spec, any_spec),
        scratch_shapes=[pltpu.VMEM((part, 4 * half), BF16), pltpu.SemaphoreType.DMA((GROUPS + part // 16,))],
    )(*[pltpu.with_memory_space_constraint(a, pltpu.VMEM) for a in (raw, sums, attended)])


def solution(mesh):
    tp = mesh.shape["tp"]
    paired = tp == 2 and mesh.shape["ctx"] % 4 == 0 and mesh.shape["ctx"] > 4 and GROUPS // tp % 2 == 0
    return jax.shard_map(
        local_pair if paired else local_any,
        mesh=mesh,
        in_specs=(
            P(),
            P("ctx", "tp"),
            P("ctx", "tp"),
            P("ctx", "tp"),
            P("ctx", "tp"),
            P("ctx", "tp"),
            P("tp"),
            P("tp"),
            P("ctx", "tp"),
            P("ctx", "tp"),
            P("ctx", "tp"),
        ),
        out_specs=(P(("ctx", "tp"), None), P(("ctx", "tp"), None)),
        check_vma=False,
    )
```

```python
import functools

import jax
import jax.numpy as jnp
from jax import lax
from jax.experimental import pallas as pl
from jax.experimental.pallas import tpu as pltpu
from jax.sharding import PartitionSpec as P

HEADS = 128
GROUPS = 8
ATT_DIM = 128
DOC_DEVS = 4


NEG_LARGE = -1e30


def for_sending(x):
    return jax.tree.map(lambda a: a.astype(jnp.bfloat16) if a.dtype == jnp.float32 else a, x)


def passed_along(block, axis, distance):
    devices = range(lax.axis_size(axis))
    route = [(i - distance, i) for i in devices if i - distance in devices]
    return lax.ppermute(block, axis, route)


def doc_starts(doc_lengths):
    return jnp.cumsum(doc_lengths) - doc_lengths


def doc_index(positions, starts):
    return jnp.sum((starts[None, :] <= positions[:, None]).astype(jnp.int32), axis=1) - 1


def block_terms(ssm_x, ssm_b, ssm_c, step_size, decay_rate, doc_ids, prev_id, group_heads):
    tok_rows = ssm_x.shape[0]
    head_count = step_size.shape[1]
    group_count = head_count // group_heads
    head_size = ssm_x.shape[1] // head_count
    state_size = ssm_b.shape[1] // group_count
    inputs = ssm_x.reshape(tok_rows, group_count, group_heads, head_size)
    in_proj = ssm_b.reshape(tok_rows, group_count, state_size)
    out_proj = ssm_c.reshape(tok_rows, group_count, state_size)
    log_decay = -(step_size * decay_rate[None, :])
    cumulative = jnp.cumsum(log_decay, axis=0)
    same_doc = doc_ids[:, None] == doc_ids[None, :]
    causal = jnp.arange(tok_rows)[:, None] >= jnp.arange(tok_rows)[None, :]
    allowed = (same_doc & causal)[None]
    spread = cumulative.T[:, :, None] - cumulative.T[:, None, :]
    weights = (
        jnp.where(allowed, jnp.exp(jnp.where(allowed, spread, 0.0)), 0.0) * step_size.T[:, None, :]
    )
    intersection = jnp.einsum("tgn,sgn->gts", out_proj, in_proj, preferred_element_type=jnp.float32)
    mixing = (
        weights.reshape(group_count, group_heads, tok_rows, tok_rows) * intersection[:, None]
    ).astype(jnp.bfloat16)
    y_intra = jnp.einsum("ghts,sghp->tghp", mixing, inputs, preferred_element_type=jnp.float32)
    final_sum = cumulative[-1]
    tail = (
        jnp.exp(final_sum[None, :] - cumulative)
        * step_size
        * (doc_ids == doc_ids[-1]).astype(jnp.float32)[:, None]
    )
    scaled = (
        inputs.astype(jnp.float32) * tail.reshape(tok_rows, group_count, group_heads)[..., None]
    ).astype(jnp.bfloat16)
    state_local = jnp.einsum("sghp,sgn->ghpn", scaled, in_proj, preferred_element_type=jnp.float32)
    entry = jnp.exp(cumulative) * (doc_ids == prev_id).astype(jnp.float32)[:, None]
    transmit = jnp.exp(final_sum) * (doc_ids[-1] == prev_id).astype(jnp.float32)
    return (y_intra, state_local, entry, transmit.reshape(group_count, group_heads))


def finish_rows(y_intra, entry, carried, ssm_c, ssm_gate, norm_weight):
    tok_rows, group_count, group_heads, head_size = y_intra.shape
    out_proj = ssm_c.reshape(tok_rows, group_count, -1).astype(jnp.float32)
    incoming = jnp.einsum("tgn,ghpn->tghp", out_proj, carried, precision=lax.Precision.HIGHEST)
    mixer_out = y_intra + incoming * entry.reshape(tok_rows, group_count, group_heads)[..., None]
    gate_vals = ssm_gate.reshape(tok_rows, group_count, group_heads, head_size).astype(jnp.float32)
    gated = (mixer_out * jax.nn.silu(gate_vals)).reshape(
        tok_rows, group_count, group_heads * head_size
    )
    factor = lax.rsqrt(jnp.mean(gated * gated, axis=2, keepdims=True) + 1e-05)
    return ((gated * factor).reshape(tok_rows, -1) * norm_weight[None, :]).astype(jnp.bfloat16)


def chain_states(earlier, later):
    return (earlier[0] * later[0], later[0][:, :, None, None] * earlier[1] + later[1])


def attention_update(
    carry, query_rows, key_block, value_block, key_pos, query_pos, query_doc, starts
):
    running_max, running_sum, running_acc = carry
    block_rows = key_block.shape[0]
    kv_local = key_block.shape[1] // ATT_DIM
    key_heads = key_block.reshape(block_rows, kv_local, ATT_DIM)
    value_heads = value_block.reshape(block_rows, kv_local, ATT_DIM)
    key_doc = doc_index(key_pos, starts)
    allowed = (query_doc[:, None] == key_doc[None, :]) & (key_pos[None, :] <= query_pos[:, None])
    scores = jnp.einsum(
        "tngd,knd->ngtk", query_rows, key_heads, preferred_element_type=jnp.float32
    ) * ATT_DIM ** (-0.5)
    scores = jnp.where(allowed[None, None], scores, -jnp.inf)
    new_max = jnp.maximum(running_max, jnp.max(scores, axis=3))
    probs = jnp.exp(scores - new_max[..., None])
    factor = jnp.exp(running_max - new_max)
    new_sum = running_sum * factor + jnp.sum(probs, axis=3)
    weighted = jnp.einsum(
        "ngtk,knd->ngtd",
        probs.astype(jnp.bfloat16),
        value_heads,
        preferred_element_type=jnp.float32,
    )
    return (new_max, new_sum, running_acc * factor[..., None] + weighted)


def local_any(
    doc_lengths,
    ssm_x,
    ssm_gate,
    ssm_b,
    ssm_c,
    step_size,
    decay_rate,
    norm_weight,
    queries,
    keys,
    values,
):
    tok_rows = ssm_x.shape[0]
    ctx_index = lax.axis_index("ctx")
    begin = ctx_index * tok_rows
    positions = begin + jnp.arange(tok_rows, dtype=jnp.int32)
    starts = doc_starts(doc_lengths)
    doc_ids = doc_index(positions, starts)
    prev_id = doc_index(jnp.reshape(begin - 1, (1,)), starts)[0]
    group_heads = HEADS // GROUPS
    y_intra, state_local, entry, transmit = block_terms(
        ssm_x, ssm_b, ssm_c, step_size, decay_rate, doc_ids, prev_id, group_heads
    )
    merged = (transmit, state_local)
    for level_bit in range(DOC_DEVS.bit_length() - 1):
        earlier = passed_along(
            (for_sending(merged[0]), for_sending(merged[1])), "ctx", 1 << level_bit
        )
        merged = chain_states(earlier, merged)
    carried = passed_along(merged[1], "ctx", 1)
    mixed_rows = finish_rows(y_intra, entry, carried, ssm_c, ssm_gate, norm_weight)
    kv_local = keys.shape[1] // ATT_DIM
    q_groups = queries.shape[1] // (kv_local * ATT_DIM)
    query_rows = queries.reshape(tok_rows, kv_local, q_groups, ATT_DIM)
    floor_start = jnp.max(jnp.where(starts <= begin, starts, 0))
    query_last = begin + tok_rows - 1
    carry_shape = (kv_local, q_groups, tok_rows)
    initial = (
        jnp.full(carry_shape, NEG_LARGE, jnp.float32),
        jnp.zeros(carry_shape, jnp.float32),
        jnp.zeros(carry_shape + (ATT_DIM,), jnp.float32),
    )

    def visit(carry, key_block, value_block, key_begin):
        block_rows = key_block.shape[0]
        needed = (key_begin <= query_last) & (key_begin + block_rows - 1 >= floor_start)

        def update(inner):
            key_pos = key_begin + jnp.arange(block_rows, dtype=jnp.int32)
            return attention_update(
                inner, query_rows, key_block, value_block, key_pos, positions, doc_ids, starts
            )

        def unchanged(inner):
            return inner

        return lax.cond(needed, update, unchanged, carry)

    totals = visit(initial, keys, values, begin)
    for hop_count in range(1, DOC_DEVS + 1):
        near_keys, near_values = passed_along((keys, values), "ctx", hop_count)
        totals = visit(totals, near_keys, near_values, begin - hop_count * tok_rows)
    final_out = totals[2] / totals[1][..., None]
    attended_rows = (
        jnp.transpose(final_out, (2, 0, 1, 3)).reshape(tok_rows, -1).astype(jnp.bfloat16)
    )
    mixed_local, attended_local = (
        lax.all_to_all(mixed_rows, "tp", split_axis=0, concat_axis=1, tiled=True),
        lax.all_to_all(attended_rows, "tp", split_axis=0, concat_axis=1, tiled=True),
    )
    return (mixed_local, attended_local)


LOG2E = 1.4426950408889634
F32 = jnp.float32
BF16 = jnp.bfloat16
MESH_ID = pl.DeviceIdType.MESH
COLS_LAST = (((1,), (1,)), ((), ()))
ROWS_FIRST = (((0,), (0,)), ((), ()))
PIECE = 128
HEADS_AT_ONCE = 2
MERGE_AFTER = (3, 4)
PASS_AFTER = (7,)
FIRST_HEAD_ORDER = (
    (0, 0, 1),
    (1, 0, 1),
    (0, 0, 0),
    (0, 1, 1),
    (1, 1, 1),
    (1, 0, 0),
    (0, 1, 0),
    (1, 1, 0),
)


def dot(a, b, dims=(((1,), (0,)), ((), ())), precision=None):
    return lax.dot_general(a, b, dims, precision=precision, preferred_element_type=F32)


def spread_heads(columns, head, head_size):
    lane = lax.broadcasted_iota(jnp.int32, (columns.shape[0], 128), 1)
    wide = jnp.broadcast_to(columns[:, head : head + 1], lane.shape)
    for k in range(1, 128 // head_size):
        wide = jnp.where(lane >= k * head_size, columns[:, head + k : head + k + 1], wide)
    return wide


def pair_kernel(
    n,
    lengths_in,
    x_in,
    gate_in,
    b_in,
    c_in,
    step_in,
    q_in,
    k_in,
    v_in,
    rate_in,
    weight_in,
    raw_out,
    sums_out,
    attended_out,
    x_s,
    gate_s,
    b_s,
    c_s,
    step_s,
    q_s,
    kv_s,
    own_s,
    beside_s,
    merged_s,
    behind_s,
    passed_s,
    second_s,
    t_own,
    t_beside,
    coef_s,
    loan_s,
    lengths,
    rate_ref,
    weight_ref,
    y_s,
    raw_s,
    sums_s,
    attended_s,
    bias_s,
    l_s,
    lt_s,
    dtt_s,
    tail_s,
    entry_s,
    send_sem,
    recv_sem,
    own_sem,
):
    index = lax.axis_index("ctx")
    tp = lax.axis_index("tp")
    parity, pair = lax.rem(index, 2), lax.div(index, 2)
    odd = lax.rem(pair, 2)
    base = index - parity
    other = 1 - parity
    tok = x_in.shape[0]
    rows = 2 * tok
    width = x_s.shape[1]
    group_heads = HEADS // GROUPS
    heads = step_in.shape[0] // 2
    groups = heads // group_heads
    group_width = width // groups
    state = b_s.shape[1] // groups
    head_size = width // heads
    kv_width = kv_s.shape[2]
    kv_heads = kv_width // ATT_DIM
    q_width = q_s.shape[1] // kv_heads
    pieces = group_width // PIECE
    group_of = (odd, 1 - odd)

    core_peer = (base + other, tp)
    tp_peer = (index, 1 - tp)
    cross_peer = (base + other, 1 - tp)
    beside = (index + 2 - 4 * odd, tp)
    barrier = pltpu.get_barrier_semaphore()
    ahead, behind = base + 4 < n, base >= 4
    fed = (odd == 1) | behind
    feeds = (odd == 0) | behind
    greeted = jnp.int32(3)

    def greet(peer):
        pl.semaphore_signal(barrier, inc=1, device_id=peer, device_id_type=MESH_ID)

    for step in (2, 4, -2, -4):
        there = (base + step >= 0) & (base + step < n)
        greeted += 2 * there.astype(jnp.int32)

        @pl.when(there)
        def _():
            for core in range(2):
                greet((base + step + core, tp))

    for peer in (core_peer, tp_peer, cross_peer):
        greet(peer)

    small = ((lengths_in, lengths), (rate_in, rate_ref), (weight_in, weight_ref))
    small = [pltpu.make_async_copy(src, dst, own_sem.at[k]) for k, (src, dst) in enumerate(small)]
    for copy in small:
        copy.start()
    used = [0, 0, len(small)]

    def slots(kind, count=1):
        used[kind] += count
        return used[kind] - count

    def remote(src, dst, peer, send, recv):
        return pltpu.make_async_remote_copy(
            src_ref=src,
            dst_ref=dst,
            send_sem=send_sem.at[send],
            recv_sem=recv_sem.at[recv],
            device_id=peer,
            device_id_type=MESH_ID,
        )

    at_mine = pl.multiple_of(parity * tok, tok)
    mine = pl.ds(at_mine, tok)

    trade_send, trade_own = slots(0), slots(2)
    step_send, step_own = slots(0), slots(2)

    def trade(moves, whole, recv, send=trade_send, own=trade_own):
        for give, keep, place in moves:
            pltpu.make_async_copy(keep, place, own_sem.at[own]).start()

        def start():
            for give, keep, place in moves:
                remote(give, place, core_peer, send, recv).start()

        def ready():
            remote(whole, whole, core_peer, send, recv).wait_recv()

        return start, ready

    def by_group(src, dst, local_groups):
        size = dst.shape[1] // groups

        def part(core, local):
            at = core * groups * size + group_of[local] * size
            return src.at[:, pl.ds(pl.multiple_of(at, 128), size)]

        moves, first = [], local_groups[0]
        for local in local_groups:
            place = dst.at[mine, local * size : (local + 1) * size]
            moves.append((part(other, local), part(parity, local), place))
        whole = dst.at[:tok, first * size : (first + len(local_groups)) * size]
        return trade(moves, whole, slots(1))

    def part_of(src, core, begin, size, total):
        return src.at[:, pl.ds(pl.multiple_of(core * total + begin, 128), size)]

    @pl.when(pair < 2)
    def _():
        kv_s[:, :rows, :] = jnp.zeros((2, rows, kv_width), BF16)

    @pl.when(pair < 1)
    def _():
        kv_s[:, rows : 2 * rows, :] = jnp.zeros((2, rows, kv_width), BF16)
        second_s[...] = jnp.zeros_like(second_s)

    @pl.when((odd == 0) & jnp.logical_not(ahead))
    def _():
        beside_s[...] = jnp.zeros_like(beside_s)

    near_send, far_send = slots(0), slots(0)
    near_recv = [slots(1) for head in range(kv_heads)]
    far_recv = [slots(1) for head in range(kv_heads)]
    early = base + 8 < n
    loose = early & ((base + 12 < n) | (base < 4))
    items = []
    for head in range(1, kv_heads):
        items += [(0, head, 0, ahead), (0, head, 1, early)]
        items += [(1, head, 0, loose), (1, head, 1, loose)]
    item_send, loan_recv = slots(0, len(items)), slots(1, len(items))

    def head_cols(head):
        return slice(head * ATT_DIM, (head + 1) * ATT_DIM)

    def send_part(k, head, dst, step, at, send, recv, cores=(0, 1)):
        for core in cores:
            remote(
                part_of((k_in, v_in)[k], core, head * ATT_DIM, ATT_DIM, kv_width),
                dst.at[pl.ds(at, tok), :],
                (base + step + core, tp),
                send,
                recv,
            ).start()

    def send_near():
        @pl.when(odd == 0)
        def _():
            for head in range(kv_heads):
                for k in range(2):
                    near = kv_s.at[k, :, head_cols(head)]
                    send_part(k, head, near, 2, at_mine + rows, near_send, near_recv[head])

        @pl.when((odd == 1) & ahead)
        def _():
            for k, far, core in FIRST_HEAD_ORDER:
                place = kv_s.at[k, :, head_cols(0)]
                if far:
                    send_part(k, 0, place, 4, at_mine, far_send, far_recv[0], (core,))
                else:
                    send_part(k, 0, place, 2, at_mine + rows, near_send, near_recv[0], (core,))

    def send_items(lending):
        for j, (k, head, core, lent) in enumerate(items):
            there = lent if lending else ahead & jnp.logical_not(lent)

            @pl.when((odd == 1) & (parity == core) & there)
            def _():
                if lending:
                    send_part(k, head, loan_s.at[j], -2, 0, item_send + j, loan_recv + j)
                else:
                    near = kv_s.at[k, :, head_cols(head)]
                    send_part(k, head, near, 2, at_mine + rows, item_send + j, near_recv[head])

    def send_far(head):
        @pl.when(ahead & ((odd == 0) | (head > 0)))
        def _():
            for k in range(2):
                far = kv_s.at[k, :, head_cols(head)]
                send_part(k, head, far, 4, at_mine, far_send, far_recv[head])

    def arrived(place, recv):
        remote(place, place, core_peer, far_send, recv).wait_recv()

    def forward():
        for j, (k, head, core, lent) in enumerate(items):

            @pl.when((odd == 0) & lent)
            def _():
                arrived(loan_s.at[j], loan_recv + j)
                at = rows + core * tok
                near = kv_s.at[k, at : at + tok, head_cols(head)]
                peer = (index + 4, tp)
                remote(loan_s.at[j], near, peer, item_send + j, near_recv[head]).start()

    def wait_past(head):
        @pl.when(fed)
        def _():
            arrived(kv_s.at[:, rows : 2 * rows, head_cols(head)], near_recv[head])

        @pl.when(behind)
        def _():
            arrived(kv_s.at[:, :rows, head_cols(head)], far_recv[head])

    moves = []
    for local in range(groups):
        place = step_s.at[local * group_heads : (local + 1) * group_heads, mine]

        def step_part(core):
            at = (core * groups + group_of[local]) * group_heads
            return step_in.at[pl.ds(pl.multiple_of(at, 8), group_heads)]

        moves.append((step_part(other), step_part(parity), place))
    start_step, ready_step = trade(moves, step_s.at[:, :tok], slots(1), step_send, step_own)
    start_b, ready_b = by_group(b_in, b_s, tuple(range(groups)))
    trade_x = {local: by_group(x_in, x_s, (local,)) for local in (1, 0)}
    start_c, ready_c = by_group(c_in, c_s, tuple(range(groups)))
    moves = []
    for k, src in enumerate((k_in, v_in)):
        give = part_of(src, other, 0, kv_width, kv_width)
        keep = part_of(src, parity, 0, kv_width, kv_width)
        moves.append((give, keep, kv_s.at[k, pl.ds(at_mine + 2 * rows, tok), :]))
    ready_kvq = slots(1)
    start_kv, _ = trade(moves, kv_s.at[:, :tok, :], ready_kvq)
    q_all = q_s.shape[1]
    give, keep = part_of(q_in, other, 0, q_all, q_all), part_of(q_in, parity, 0, q_all, q_all)
    start_q, _ = trade([(give, keep, q_s.at[mine, :])], q_s.at[:tok, :], ready_kvq)
    start_gate, ready_gate = by_group(gate_in, gate_s, tuple(range(groups)))

    @pl.when(pair < 2)
    def _():
        behind_s[...] = jnp.zeros_like(behind_s)

    small[0].wait()
    begin = pair * rows
    row_at = begin - 2 * rows + lax.broadcasted_iota(jnp.int32, (1, 3 * rows), 1)
    col_at = begin + lax.broadcasted_iota(jnp.int32, (rows, 1), 0)
    row_doc = jnp.zeros_like(row_at) - 1
    col_doc = jnp.zeros_like(col_at) - 1
    begun, prev_id, last_id = jnp.int32(0), jnp.int32(-1), jnp.int32(-1)
    for j in range(lengths.shape[0]):
        row_doc += (row_at >= begun).astype(jnp.int32)
        col_doc += (col_at >= begun).astype(jnp.int32)
        prev_id += (begin - 1 >= begun).astype(jnp.int32)
        last_id += (begin + rows - 1 >= begun).astype(jnp.int32)
        begun = begun + lengths[j]
    bias_s[...] = jnp.where((row_doc == col_doc) & (row_at <= col_at), 0.0, NEG_LARGE)

    pl.semaphore_wait(barrier, greeted)
    send_near()
    send_items(True)
    start_step()
    start_b()
    send_far(0)
    for local in (1, 0):
        trade_x[local][0]()
    for start in (start_c, start_kv, start_q, start_gate):
        start()

    small[1].wait()
    small[2].wait()
    ready_step()
    pltpu.make_async_copy(step_s.at[:, :tok], step_s.at[:, :tok], own_sem.at[step_own]).wait()
    step_t = jnp.concatenate([step_s[...], jnp.zeros((128 - heads, rows), F32)], axis=0)
    step = step_t.T
    rates = []
    for local in range(groups):
        rate = jnp.zeros((1, group_heads), F32)
        for k in range(2 * groups):
            here = parity * groups + group_of[local] == k
            rate = jnp.where(here, rate_ref[:, k * group_heads : (k + 1) * group_heads], rate)
        rates.append(rate)
    rate = jnp.concatenate(rates + [jnp.zeros((1, 128 - heads), F32)], axis=1)
    at = lax.broadcasted_iota(jnp.int32, (rows, rows), 0)
    to = lax.broadcasted_iota(jnp.int32, (rows, rows), 1)
    lower = (to <= at).astype(BF16)
    left, parts = -(step * rate), []
    for k in range(3):
        parts.append(left.astype(BF16)[:, :heads])
        left = left - left.astype(BF16).astype(F32)
    parts.append(jnp.zeros((rows, 128 - 3 * heads), BF16))
    sums = dot(lower, jnp.concatenate(parts, axis=1))
    lane = lax.broadcasted_iota(jnp.int32, (rows, 128), 1)
    sums = sums + pltpu.roll(sums, 128 - heads, 1) + pltpu.roll(sums, 128 - 2 * heads, 1)
    total_decay = jnp.where(lane < heads, sums, 0.0)
    final_sum = total_decay[rows - 1 :, :]
    l_s[...] = total_decay
    lt_s[...] = total_decay.T
    dtt_s[...] = step_t
    tail_s[...] = jnp.where(col_doc == last_id, jnp.exp(final_sum - total_decay) * step, 0.0)
    entry_s[...] = jnp.where(col_doc == prev_id, jnp.exp(total_decay), 0.0)
    passing = (last_id == prev_id).astype(F32)
    t_own[...] = jnp.broadcast_to(jnp.exp(final_sum) * passing, t_own.shape)
    t_trip = remote(t_own, t_beside, beside, slots(0), slots(1))
    t_trip.start()

    pairs = pieces // 2
    first_send, first_recv = slots(0), slots(1, pairs)
    merge_send, merge_recv = slots(0), slots(1, pairs)
    pass_send, pass_recv = slots(0), slots(1, pairs + 1)

    def two(k):
        return slice(2 * k, 2 * k + 2)

    def first_trip(k):
        src = own_s.at[pieces + 2 * k : pieces + 2 * k + 2]
        return remote(src, beside_s.at[two(k)], beside, first_send, first_recv + k)

    def merge_trip(k):
        src, peer = merged_s.at[two(k)], (index + 4, tp)
        return remote(src, behind_s.at[two(k)], peer, merge_send, merge_recv + k)

    def pass_trip(begin, count):
        span = slice(begin, begin + count)
        recv = pass_recv + (begin // 2 if count == 2 else begin - pieces + pairs + 1)
        return remote(passed_s.at[span], second_s.at[span], beside, pass_send, recv)

    def pass_trips(k):
        if k < pairs - 1:
            return [pass_trip(2 * k, 2)]
        return [pass_trip(2 * k, 1), pass_trip(2 * k + 1, 1)]

    traded = 2 * groups * state // 128 + 2 * width // 128 + q_all // 128 + 2 * kv_width // 128
    traded_ref = y_s.at[: traded * tok * 128 * 2 // (width * 4)]

    per = 128 // head_size
    pltpu.make_async_copy(traded_ref, traded_ref, own_sem.at[trade_own]).wait()
    ready_b()
    for local in (1, 0):
        trade_x[local][1]()
        b_t = b_s[:, local * state : (local + 1) * state].T
        for k in range(local * pieces, (local + 1) * pieces, 2):
            parts = []
            for tile in range(2):
                lead = (k + tile) * PIECE
                wide = spread_heads(tail_s[...], lead // head_size, head_size)
                parts.append((x_s[:, lead : lead + PIECE].astype(F32) * wide).astype(BF16))
            made = dot(b_t, jnp.concatenate(parts, axis=1)).astype(BF16)
            for tile in range(2):
                own_s[k + tile] = made[:, tile * PIECE : (tile + 1) * PIECE]
        if local == 1:

            @pl.when((odd == 0) | ahead)
            def _():
                for k in range(pairs):
                    first_trip(k).start()

    send_items(False)
    for head in range(1, kv_heads):
        send_far(head)
    ready_c()

    def intra():
        for g in range(groups):
            proj = slice(g * state, (g + 1) * state)
            inter = dot(c_s[:, proj], b_s[:, proj], COLS_LAST)
            for tile in range(group_width // 128):
                lead = g * group_width + tile * 128
                halves = []
                for r in range(0, rows, tok):
                    seen = slice(0, r + tok)
                    bias = bias_s[r : r + tok, 2 * rows : 2 * rows + r + tok]
                    mixing = []
                    for h in range(lead // head_size, lead // head_size + per):
                        spread = l_s[r : r + tok, h : h + 1] - lt_s[h : h + 1, seen]
                        w = jnp.exp(spread + bias) * dtt_s[h : h + 1, seen] * inter[r : r + tok, seen]
                        mixing.append(w.astype(BF16))
                    both = dot(jnp.concatenate(mixing, axis=0), x_s[seen, lead : lead + 128])
                    whole = both[:tok]
                    for k in range(1, per):
                        part = both[k * tok : (k + 1) * tok]
                        whole = jnp.where(lane[:tok] >= k * head_size, part, whole)
                    y_s[r : r + tok, lead : lead + 128] = whole

    part_rows = rows // 4

    exit_send, exit_recv, exit_own = slots(0), slots(1), slots(2)
    sums_send, sums_recv, sums_own = slots(0), slots(1), slots(2)

    def leave(piece_for, home, send=exit_send, recv=exit_recv, own=exit_own):
        for core in (1, 0):
            peer = (base + core, 1 - tp)
            remote(piece_for(core, 1 - tp), home, peer, send, recv).start()
        remote(piece_for(other, tp), home, core_peer, send, recv).start()
        pltpu.make_async_copy(piece_for(parity, tp), home, own_sem.at[own]).start()

    def settle(thrice, once, send, recv, own):
        remote(thrice, thrice, core_peer, send, recv).wait()
        pltpu.make_async_copy(once, once, own_sem.at[own]).wait()

    def coefficients():
        t_trip.wait_recv()
        even = jnp.broadcast_to(odd == 0, (8, 128))
        row = lax.broadcasted_iota(jnp.int32, (8, 128), 0)
        for k in range(pieces):
            h = k * PIECE // head_size
            ours = spread_heads(t_own[...], h, head_size)
            theirs = spread_heads(t_beside[...], group_heads + h, head_size)
            values = (
                (1.0, ours),
                (theirs, 1.0),
                (1.0, 0.0),
                (ours, 1.0),
                (0.0, 1.0),
                (1.0, theirs),
            )
            table = jnp.zeros((8, 128), F32)
            for j, (if_even, if_odd) in enumerate(values):
                table = jnp.where(row == j, jnp.where(even, if_even, if_odd), table)
            coef_s[:, k * PIECE : (k + 1) * PIECE] = table

    def blend(left, right, k, row):
        cols = slice(k * PIECE, (k + 1) * PIECE)
        total = left[k].astype(F32) * coef_s[row : row + 1, cols]
        total += right[k].astype(F32) * coef_s[row + 1 : row + 2, cols]
        return total.astype(BF16)

    def merge(k):
        pl.when((odd == 1) | ahead)(first_trip(k).wait_recv)
        for j in (2 * k, 2 * k + 1):
            merged_s[j] = blend(beside_s, own_s, j, 0)

        @pl.when(ahead)
        def _():
            merge_trip(k).start()

    def pass_on(k):
        @pl.when(behind)
        def _():
            merge_trip(k).wait_recv()

        @pl.when(feeds)
        def _():
            for j in (2 * k, 2 * k + 1):
                passed_s[j] = blend(own_s, behind_s, j, 2)
            for trip in pass_trips(k):
                trip.start()

    scale = LOG2E * ATT_DIM ** (-0.5)
    kvq = y_s.at[: (2 * kv_width + q_all) * tok * 2 // (width * 4)]
    arrived(kvq, ready_kvq)
    def attend_heads(kv_cols, step_no, lead):
        at = pl.multiple_of((tp * 2 + parity) * q_all + lead, 128)
        home = attended_out.at[:, pl.ds(at, HEADS_AT_ONCE * ATT_DIM)]
        here = attended_s.at[step_no]
        for core in range(2):
            r = core * tok
            seen = slice(r, r + 2 * rows + tok)
            asked = []
            for h in range(HEADS_AT_ONCE):
                asked.append(q_s[r : r + tok, lead + h * ATT_DIM : lead + (h + 1) * ATT_DIM])
            scores = dot(jnp.concatenate(asked, axis=0), kv_s[0, seen, kv_cols], COLS_LAST)
            scores = scores + jnp.concatenate([bias_s[r : r + tok, seen]] * HEADS_AT_ONCE, axis=0)
            top = jnp.max(scores, axis=1, keepdims=True)
            probs = jnp.exp2((scores - top) * scale)
            total = jnp.sum(probs, axis=1, keepdims=True)
            summed = dot(probs.astype(BF16), kv_s[1, seen, kv_cols]) / total
            for h in range(HEADS_AT_ONCE):
                part = summed[h * tok : (h + 1) * tok].astype(BF16)
                for side in range(2):
                    owned = part[side * part_rows : (side + 1) * part_rows]
                    cols = slice(h * ATT_DIM, (h + 1) * ATT_DIM)
                    attended_s[step_no, core * 2 + side, :, cols] = owned
            if step_no == 0 or core == 1:
                for half in (core,) if step_no == 0 else (1, 0):
                    src, peer = here.at[half * 2 + 1 - tp], (base + half, 1 - tp)
                    remote(src, home, peer, exit_send, exit_recv).start()
        remote(here.at[other * 2 + tp], home, core_peer, exit_send, exit_recv).start()
        pltpu.make_async_copy(here.at[parity * 2 + tp], home, own_sem.at[exit_own]).start()

    def merge_first():
        coefficients()
        merge(0)

    def attend(kv_head):
        step_no = kv_head * q_width // (HEADS_AT_ONCE * ATT_DIM)
        kv_cols = slice(kv_head * ATT_DIM, (kv_head + 1) * ATT_DIM)
        wait_past(kv_head)
        for lead in range(kv_head * q_width, (kv_head + 1) * q_width, HEADS_AT_ONCE * ATT_DIM):
            attend_heads(kv_cols, step_no, lead)
            if step_no == 0:
                forward()
            for k in range(len(MERGE_AFTER)):
                if MERGE_AFTER[k] == step_no:
                    if k == 0:
                        pl.when(pair > 0)(merge_first)
                    else:
                        merge(k)
            for k in range(len(PASS_AFTER)):
                if PASS_AFTER[k] == step_no:
                    pass_on(k)
            step_no += 1

    @pl.loop(0, 2)
    def _(turn):
        attend_now = lax.rem(turn + (pair == 0).astype(jnp.int32), 2) == 1
        pl.when(attend_now)(functools.partial(attend, 0))
        pl.when(jnp.logical_not(attend_now))(intra)

    pl.when(pair == 0)(merge_first)
    for kv_head in range(1, kv_heads):
        attend(kv_head)

    ones = jnp.ones((8, 256), BF16)
    squares = [jnp.zeros((rows, 128), F32)] * groups

    def finish(local, first, count):
        lead = local * group_width + first * PIECE
        ready, fed_by = [], []
        for tile in range(0, count * PIECE, 128):
            cols = slice(lead + tile, lead + tile + 128)
            wide = spread_heads(entry_s[...], cols.start // head_size, head_size)
            z = gate_s[:, cols].astype(F32)
            z = z / (1.0 + jnp.exp(-z))
            ready.append(y_s[:, cols] * z)
            fed_by.append(wide * z)
        if local == 1:
            pl.when(fed)(pass_trip(first, count).wait_recv)
        carried = []
        for k in range(first, first + count):
            carried.append(blend(beside_s, behind_s, k, 4) if local == 0 else second_s[k])
        proj = slice(local * state, (local + 1) * state)
        incoming = dot(c_s[:, proj], jnp.concatenate(carried, axis=1))
        square = squares[local]
        for tile in range(0, count * PIECE, 128):
            cols = slice(lead + tile, lead + tile + 128)
            total = ready[tile // 128] + incoming[:, tile : tile + 128] * fed_by[tile // 128]
            square += total * total
            at = parity * width + group_of[local] * group_width + first * PIECE + tile
            gain = weight_ref[:, pl.ds(pl.multiple_of(at, 128), 128)]
            done = (total * gain).astype(BF16)
            for rank in range(4):
                owned = done[rank * part_rows : (rank + 1) * part_rows]
                raw_s[rank, cols.start // PIECE] = owned
        squares[local] = square
        at = ((tp * 2 + parity) * groups + group_of[local]) * pieces + first
        here = pl.ds(lead // PIECE, count)
        leave(
            lambda core, side: raw_s.at[core * 2 + side, here],
            raw_out.at[pl.ds(at, count)],
        )
        if first + count == pieces:
            here = slice(local * 8, local * 8 + 8)
            high = square.astype(BF16)
            halves = [high, (square - high.astype(F32)).astype(BF16)]
            sums_s[here, :] = dot(ones, jnp.concatenate(halves, axis=1), COLS_LAST)
            at = ((tp * 2 + parity) * groups + group_of[local]) * 8
            home = sums_out.at[pl.ds(pl.multiple_of(at, 8), 8), :]

            def half(core, side):
                return sums_s.at[here, pl.ds(pl.multiple_of(core * tok, tok), tok)]

            leave(half, home, sums_send, sums_recv, sums_own)

    ready_gate()
    merged, passed = len(MERGE_AFTER), len(PASS_AFTER)
    for k in range(pairs):
        if k == 2:
            finish(1, 0, 2)
        while passed <= k:
            pass_on(passed)
            passed += 1
        finish(0, 2 * k, 2)
        while merged < pairs:
            merge(merged)
            merged += 1
    for k in range(1, pairs - 1):
        finish(1, 2 * k, 2)
    finish(1, pieces - 2, 1)
    finish(1, pieces - 1, 1)

    assert used == [send_sem.shape[0], recv_sem.shape[0], own_sem.shape[0]], used
    t_trip.wait_send()
    remote(traded_ref, traded_ref, core_peer, trade_send, loan_recv).wait_send()
    given = step_s.at[:, :tok]
    remote(given, given, core_peer, step_send, loan_recv).wait_send()
    sent = kv_s.at[:, :rows, :]

    @pl.when(ahead)
    def _():
        remote(sent, sent, core_peer, far_send, loan_recv).wait_send()

    for j, (k, head, core, lent) in enumerate(items):
        part = kv_s.at[0, :rows, head_cols(0)]
        closing = remote(part, part, core_peer, item_send + j, loan_recv)
        pl.when((odd == 1) & ahead & (parity == core))(closing.wait_send)
        closing = remote(loan_s.at[j], loan_s.at[j], core_peer, item_send + j, loan_recv)
        pl.when((odd == 0) & lent)(closing.wait_send)

    @pl.when(odd == 0)
    def _():
        remote(sent, sent, core_peer, near_send, loan_recv).wait_send()

    @pl.when((odd == 1) & ahead)
    def _():
        part = kv_s.at[:, :rows, head_cols(0)]
        remote(part, part, core_peer, near_send, loan_recv).wait_send()

    half = own_s.at[:pieces]
    pl.when((odd == 0) | ahead)(remote(half, half, beside, first_send, first_recv).wait_send)
    pl.when(feeds)(remote(half, half, beside, pass_send, pass_recv).wait_send)

    @pl.when(ahead)
    def _():
        remote(half, half, beside, merge_send, merge_recv).wait_send()

    left = (width + q_all) * part_rows * 2 // (width * 4)
    settle(y_s.at[: 3 * left], y_s.at[:left], exit_send, exit_recv, exit_own)
    left = 8 * groups
    settle(l_s.at[: 3 * left], l_s.at[:left], sums_send, sums_recv, sums_own)


def scale_kernel(raw, sums, attended, mixed_out, attended_out, mixed_s, sem):
    tp = lax.axis_index("tp")
    rows, width = mixed_s.shape
    group_width = width // GROUPS
    copies = []
    for k in range(0, rows, 16):
        part = slice(k, k + 16)
        copy = pltpu.make_async_copy(
            attended.at[part], attended_out.at[part], sem.at[GROUPS + k // 16]
        )
        copy.start()
        copies.append(copy)
    squares = sums[...]
    squares = jnp.concatenate([squares, jnp.zeros((128 - squares.shape[0], 128), F32)], axis=0).T
    squares = jnp.where(tp == 0, squares[:rows], squares[rows:])
    factor = lax.rsqrt(squares * (1.0 / group_width) + 1e-05)
    for g in range(GROUPS):
        for k in range(g * group_width // PIECE, (g + 1) * group_width // PIECE):
            scaled = raw[k].astype(F32) * factor[:, 8 * g : 8 * g + 1]
            mixed_s[:, k * PIECE : (k + 1) * PIECE] = scaled.astype(BF16)
        cols = slice(g * group_width, (g + 1) * group_width)
        copy = pltpu.make_async_copy(mixed_s.at[:, cols], mixed_out.at[:, cols], sem.at[g])
        copy.start()
        copies.append(copy)
    for copy in copies:
        copy.wait()


def local_pair(
    doc_lengths,
    ssm_x,
    ssm_gate,
    ssm_b,
    ssm_c,
    step_size,
    decay_rate,
    norm_weight,
    queries,
    keys,
    values,
):
    tok, width = ssm_x.shape
    rows, half = 2 * tok, width // 2
    groups = step_size.shape[1] * GROUPS // HEADS // 2
    state = ssm_b.shape[1] // (2 * groups)
    kv_half = keys.shape[1] // 2
    q_half = queries.shape[1] // 2
    pieces = half // PIECE
    any_spec = pl.BlockSpec(memory_space=pl.ANY)
    vmem_spec = pl.BlockSpec(memory_space=pltpu.VMEM)
    part = rows // 4
    group_pieces = pieces // groups
    items = 4 * (kv_half // ATT_DIM - 1)
    step_width = HEADS_AT_ONCE * ATT_DIM
    state_piece = pltpu.VMEM((group_pieces, state, PIECE), BF16)
    scratch = [
        pltpu.VMEM((rows, half), BF16),
        pltpu.VMEM((rows, half), BF16),
        pltpu.VMEM((rows, groups * state), BF16),
        pltpu.VMEM((rows, groups * state), BF16),
        pltpu.VMEM((step_size.shape[1] // 2, rows), F32),
        pltpu.VMEM((rows, q_half), BF16),
        pltpu.VMEM((2, 3 * rows, kv_half), BF16),
        pltpu.VMEM((pieces, state, PIECE), BF16),
        state_piece,
        state_piece,
        state_piece,
        state_piece,
        state_piece,
        pltpu.VMEM((8, 128), F32),
        pltpu.VMEM((8, 128), F32),
        pltpu.VMEM((8, half // groups), F32),
        pltpu.VMEM((items, tok, ATT_DIM), BF16),
        pltpu.SMEM(doc_lengths.shape, jnp.int32),
        pltpu.VMEM((1, decay_rate.shape[0]), F32),
        pltpu.VMEM((1, norm_weight.shape[0]), F32),
        pltpu.VMEM((rows, half), F32),
        pltpu.VMEM((4, pieces, part, PIECE), BF16),
        pltpu.VMEM((8 * groups, rows), F32),
        pltpu.VMEM((q_half // step_width, 4, part, step_width), BF16),
        pltpu.VMEM((rows, 3 * rows), F32),
        pltpu.VMEM((rows, 128), F32),
        pltpu.VMEM((128, rows), F32),
        pltpu.VMEM((128, rows), F32),
        pltpu.VMEM((rows, 128), F32),
        pltpu.VMEM((rows, 128), F32),
        pltpu.SemaphoreType.DMA((10 + items,)),
        pltpu.SemaphoreType.DMA((11 + kv_half // ATT_DIM * 2 + items + 3 * group_pieces // 2,)),
        pltpu.SemaphoreType.DMA((7,)),
    ]
    raw, sums, attended = pl.pallas_call(
        functools.partial(pair_kernel, lax.axis_size("ctx")),
        out_shape=(
            pltpu.VMEM((4 * pieces, part, PIECE), BF16),
            pltpu.VMEM((8 * GROUPS, tok), F32),
            pltpu.VMEM((part, 4 * q_half), BF16),
        ),
        in_specs=[any_spec] * 11,
        out_specs=(vmem_spec, vmem_spec, vmem_spec),
        scratch_shapes=scratch,
        compiler_params=pltpu.CompilerParams(collective_id=0, has_side_effects=True),
    )(
        doc_lengths,
        ssm_x,
        ssm_gate,
        ssm_b,
        ssm_c,
        step_size.T,
        queries,
        keys,
        values,
        decay_rate[None, :],
        norm_weight[None, :],
    )
    return pl.pallas_call(
        scale_kernel,
        out_shape=(
            jax.ShapeDtypeStruct((part, 4 * half), BF16),
            jax.ShapeDtypeStruct(attended.shape, BF16),
        ),
        in_specs=[vmem_spec] * 3,
        out_specs=(any_spec, any_spec),
        scratch_shapes=[pltpu.VMEM((part, 4 * half), BF16), pltpu.SemaphoreType.DMA((GROUPS + part // 16,))],
    )(*[pltpu.with_memory_space_constraint(a, pltpu.VMEM) for a in (raw, sums, attended)])


def solution(mesh):
    tp = mesh.shape["tp"]
    paired = tp == 2 and mesh.shape["ctx"] % 4 == 0 and mesh.shape["ctx"] > 4 and GROUPS // tp % 2 == 0
    return jax.shard_map(
        local_pair if paired else local_any,
        mesh=mesh,
        in_specs=(
            P(),
            P("ctx", "tp"),
            P("ctx", "tp"),
            P("ctx", "tp"),
            P("ctx", "tp"),
            P("ctx", "tp"),
            P("tp"),
            P("tp"),
            P("ctx", "tp"),
            P("ctx", "tp"),
            P("ctx", "tp"),
        ),
        out_specs=(P(("ctx", "tp"), None), P(("ctx", "tp"), None)),
        check_vma=False,
    )
```
